32 devices in a mesh: row: 4 (over y, x), col: 2 (over core), dp: 4 (over z).
Axes of the slice: x: 2, y: 2, z: 4, core: 2. Of those that a mesh axis runs over, the one named last changes fastest.
Arguments:
- hidden_in: bfloat16 [16384, 768], P(('row', 'col', 'dp')), may hold values from -6 to 6
- cotangent: bfloat16 [16384, 768], P(('row', 'col', 'dp')), may hold values from -6 to 6
- seq_lengths: int32 [32, 4], replicated, may hold values from 0 to 512, as said below
- w_query: bfloat16 [768, 768], P('row', 'col'), may hold values from -0.21875 to 0.21875
- w_key: bfloat16 [768, 768], P('row', 'col'), may hold values from -0.21875 to 0.21875
- w_value: bfloat16 [768, 768], P('row', 'col'), may hold values from -0.21875 to 0.21875
- w_out: bfloat16 [768, 768], P('row', 'col'), may hold values from -1.75 to 1.75
- w_gate: bfloat16 [768, 2048], P('row', 'col'), may hold values from -0.21875 to 0.21875
- w_up: bfloat16 [768, 2048], P('row', 'col'), may hold values from -0.21875 to 0.21875
- w_down: bfloat16 [2048, 768], P('row', 'col'), may hold values from -0.125 to 0.125
- attn_gain: float32 [768], replicated, may hold values from 0.1 to 1.9
- ffn_gain: float32 [768], replicated, may hold values from 0.1 to 1.9
Outputs:
- layer_out: bfloat16 [16384, 768], P(('row', 'col', 'dp'))
- input_grad: float32 [16384, 768], P(('row', 'col', 'dp'))
- query_grad: float32 [768, 768], P('row', 'col')
- key_grad: float32 [768, 768], P('row', 'col')
- value_grad: float32 [768, 768], P('row', 'col')
- output_grad: float32 [768, 768], P('row', 'col')
- gate_grad: float32 [768, 2048], P('row', 'col')
- up_grad: float32 [768, 2048], P('row', 'col')
- down_grad: float32 [2048, 768], P('row', 'col')
- attn_gain_grad: float32 [768], replicated
- ffn_gain_grad: float32 [768], replicated
The draws below stay inside these ranges and needn't reach their ends.
Inputs may be any that keep to these rules, and one draw needn't show every extreme that they name: `seq_lengths`: each row holds 4 entries, each 0, 128, 256 or 512; a row sums to 512, and its zeros stand after its other entries.
All inputs are finite; a program needn't handle non-finite values.
Results may differ from the reference program's by a relative error of at most 0.019.
Values may be sent and summed in bfloat16 or wider, within the bound.
A program may use at most 128 MiB of HBM per device.

```python
import jax
import jax.numpy as jnp
from jax import lax

D = 768
HEADS = 12
FF = 2048
HEAD_DIM = 64
TOK_DEV = 512
PACKS = 32
TOKENS = 16384


def draw_seq_lengths(key, part):
    patterns = jnp.array([[4, 0, 0, 0], [2, 2, 0, 0], [2, 1, 1, 0], [1, 2, 1, 0], [1, 1, 2, 0], [1, 1, 1, 1]], jnp.int32)
    picks = jax.random.randint(key, (PACKS,), 0, 6)
    forced = jax.random.randint(jax.random.fold_in(key, 7), (), 0, PACKS)
    picks = jnp.where(jnp.arange(PACKS, dtype=jnp.int32) == forced, 0, picks)
    return (patterns[picks] * (TOK_DEV // 4)).astype(jnp.int32)


def block_levels(key, dims, split, smallest, top_value):
    def one(position, parts):
        draws = jax.random.uniform(jax.random.fold_in(jax.random.fold_in(key, 6), position), (parts,), jnp.float32, smallest / len(split), top_value / len(split))
        return jnp.repeat(jnp.exp(draws), dims[position] // parts).reshape((-1,) + (1,) * (len(dims) - position - 1))

    loudness = one(*split[0])
    for cut in split[1:]:
        loudness = loudness * one(*cut)
    return loudness


def normal_values(own_key, shape, deviation, bound, shards=(), kind=jnp.bfloat16):
    result = jax.random.normal(own_key, shape, jnp.float32) * deviation
    if len(shards) > 0:
        result = block_levels(own_key, shape, shards, -0.22, 0.18) * result
    return jnp.clip(result, min=-bound, max=bound).astype(kind)


def setup_inputs(seed: int = 0) -> dict:
    seeds = jax.random.split(jax.random.key(seed), 13)
    return {
        "hidden_in": normal_values(seeds[0], (TOKENS, D), 1.0, 6.0, ((0, 32),)),
        "cotangent": normal_values(seeds[1], (TOKENS, D), 1.0, 6.0, ((0, 32),)),
        "seq_lengths": draw_seq_lengths(jax.random.fold_in(seeds[12], 71), 0),
        "w_query": normal_values(seeds[3], (D, D), D ** -0.5, 0.21875, ((0, 4), (1, 2))),
        "w_key": normal_values(seeds[4], (D, D), D ** -0.5, 0.21875, ((0, 4), (1, 2))),
        "w_value": normal_values(seeds[5], (D, D), D ** -0.5, 0.21875, ((0, 4), (1, 2))),
        "w_out": normal_values(seeds[6], (D, D), (D // 64) ** -0.5, 1.75, ((0, 4), (1, 2))),
        "w_gate": normal_values(seeds[7], (D, FF), D ** -0.5, 0.21875, ((0, 4), (1, 2))),
        "w_up": normal_values(seeds[8], (D, FF), D ** -0.5, 0.21875, ((0, 4), (1, 2))),
        "w_down": normal_values(seeds[9], (FF, D), FF ** -0.5, 0.125, ((0, 4), (1, 2))),
        "attn_gain": jnp.clip(1.0 + 0.18 * jax.random.normal(seeds[10], (D,), jnp.float32), 0.1, 1.9),
        "ffn_gain": jnp.clip(1.0 + 0.18 * jax.random.normal(seeds[11], (D,), jnp.float32), 0.1, 1.9),
    }


norm_eps = 1e-06
masked_score = -1e+30
exact_mode = lax.Precision.HIGHEST

@jax.custom_vjp
def low(v):
    return lax.optimization_barrier(v.astype(jnp.bfloat16)).astype(jnp.float32)

@jax.custom_vjp
def low_back(v):
    return v

def low_keep(v):
    return (low(v), None)

def low_pass(kept, grad):
    return (grad,)

def back_keep(v):
    return (v, None)

def back_low(kept, grad):
    return (low(grad),)
low.defvjp(low_keep, low_pass)
low_back.defvjp(back_keep, back_low)

def product(left_side, right_side):
    return jnp.dot(left_side, right_side, precision=exact_mode)

def pack_info(lengths_row, places_count):
    places = jnp.arange(places_count, dtype=jnp.int32)
    seq_ends = jnp.cumsum(lengths_row).astype(jnp.int32)
    passed = (places[:, None] >= seq_ends[None, :]).astype(jnp.int32)
    segment = lax.optimization_barrier(jnp.sum(passed, axis=1)).astype(jnp.int32)
    seq_start = lax.optimization_barrier(jnp.sum(passed * lengths_row[None, :], axis=1)).astype(jnp.int32)
    return (segment, (places - seq_start).astype(jnp.float32))

def allowed(segment):
    places = jnp.arange(segment.shape[0], dtype=jnp.int32)
    return (segment[:, None] == segment[None, :]) & (places[:, None] >= places[None, :])

def angles(positions, head_width):
    half_width = head_width // 2
    frequency = 10000.0 ** (-jnp.arange(half_width, dtype=jnp.float32) * (2.0 / head_width))
    turned = positions[..., None] * frequency
    return (jnp.cos(turned), jnp.sin(turned))

def rotate(values, cosine, sine_part):
    half_width = values.shape[-1] // 2
    front_half = values[..., :half_width]
    back_half = values[..., half_width:]
    return jnp.concatenate([front_half * cosine - back_half * sine_part, back_half * cosine + front_half * sine_part], axis=-1)

def norm_rows(resid):
    return resid * lax.rsqrt(lax.optimization_barrier(jnp.mean(resid * resid, axis=-1, keepdims=True)) + norm_eps)

def attend(operands):
    query_raw, key_raw, value_low, lengths_row = operands
    segment, positions = pack_info(lengths_row, query_raw.shape[0])
    cosine, sine_part = angles(positions, query_raw.shape[-1])
    query_rot = low(rotate(query_raw, cosine[:, None, :], sine_part[:, None, :]))
    key_rot = low(rotate(key_raw, cosine[:, None, :], sine_part[:, None, :]))
    scores = low_back(jnp.einsum('thd,shd->hts', query_rot, key_rot, precision=exact_mode))
    scores = scores * query_raw.shape[-1] ** (-0.5)
    scores = jnp.where(allowed(segment)[None, :, :], scores, masked_score)
    row_max = lax.optimization_barrier(jnp.max(scores, axis=-1, keepdims=True))
    exponent = jnp.exp(scores - row_max)
    weights_soft = exponent / lax.optimization_barrier(jnp.sum(exponent, axis=-1, keepdims=True))
    mixed_out = jnp.einsum('hts,shd->thd', low(weights_soft), value_low, precision=exact_mode)
    return low(low_back(mixed_out))

def layer_forward(hidden_f32, w_query, w_key, w_value, w_out, w_gate, w_up, w_down, attn_gain, ffn_gain, seq_lengths):
    rows_all = hidden_f32.shape[0]
    blocks = rows_all // TOK_DEV
    shape_heads = (blocks, TOK_DEV, HEADS, HEAD_DIM)
    query_raw = low_back(product(hidden_f32, w_query)).reshape(shape_heads)
    key_raw = low_back(product(hidden_f32, w_key)).reshape(shape_heads)
    value_low = low(low_back(product(hidden_f32, w_value))).reshape(shape_heads)
    attended = lax.map(jax.checkpoint(attend), (query_raw, key_raw, value_low, seq_lengths))
    attn_rows = attended.reshape(rows_all, D)
    branch = low_back(product(attn_rows, w_out))
    middle = norm_rows(hidden_f32 + branch) * attn_gain
    middle_low = low(middle)
    gate_pre = low_back(product(middle_low, w_gate))
    up_pre = low_back(product(middle_low, w_up))
    hidden_low = low(gate_pre * jax.nn.sigmoid(gate_pre) * up_pre)
    ffn_part = low_back(product(hidden_low, w_down))
    return norm_rows(middle + ffn_part) * ffn_gain

def reference(hidden_in, cotangent, seq_lengths, w_query, w_key, w_value, w_out, w_gate, w_up, w_down, attn_gain, ffn_gain):
    inputs = (hidden_in.astype(jnp.float32), w_query.astype(jnp.float32), w_key.astype(jnp.float32), w_value.astype(jnp.float32), w_out.astype(jnp.float32), w_gate.astype(jnp.float32), w_up.astype(jnp.float32), w_down.astype(jnp.float32), attn_gain.astype(jnp.float32), ffn_gain.astype(jnp.float32))

    def forward(hidden_f32, query_mat, key_mat, value_mat, out_mat, gate_mat, up_mat, down_mat, gain_one, gain_two):
        return layer_forward(hidden_f32, query_mat, key_mat, value_mat, out_mat, gate_mat, up_mat, down_mat, gain_one, gain_two, seq_lengths)
    layer_out, pullback = jax.vjp(forward, inputs[0], inputs[1], inputs[2], inputs[3], inputs[4], inputs[5], inputs[6], inputs[7], inputs[8], inputs[9])
    gradients = pullback(cotangent.astype(jnp.float32))
    return (layer_out.astype(jnp.bfloat16), gradients[0], gradients[1], gradients[2], gradients[3], gradients[4], gradients[5], gradients[6], gradients[7], gradients[8], gradients[9])
```

```python
import jax
import jax.numpy as jnp
from jax import lax
from jax.sharding import PartitionSpec as P

HEAD_DIM = 64
HALF = HEAD_DIM // 2
EPS = 1e-06
MASKED = -1e30
BF16 = jnp.bfloat16
F32 = jnp.float32


def pack_info(lengths_row, places_count):
    places = jnp.arange(places_count, dtype=jnp.int32)
    segment = jnp.zeros((places_count,), jnp.int32)
    start = jnp.zeros((places_count,), jnp.int32)
    end = jnp.int32(0)
    for i in range(lengths_row.shape[0]):
        end = end + lengths_row[i]
        passed = (places >= end).astype(jnp.int32)
        segment = segment + passed
        start = start + passed * lengths_row[i]
    return segment, (places - start).astype(F32)


def angles(positions):
    frequency = 10000.0 ** (-jnp.arange(HALF, dtype=F32) * (2.0 / HEAD_DIM))
    turned = positions[..., None] * frequency
    return jnp.cos(turned), jnp.sin(turned)


def rotate(values, cosine, sine):
    a, b = values[..., :HALF], values[..., HALF:]
    return jnp.concatenate([a * cosine - b * sine, b * cosine + a * sine], axis=-1)


def dot(a, b):
    return jnp.dot(a, b, preferred_element_type=F32)


def dot_nt(a, b):
    return lax.dot_general(a, b, (((1,), (1,)), ((), ())), preferred_element_type=F32)


def dot_tn(a, b):
    return lax.dot_general(a, b, (((0,), (0,)), ((), ())), preferred_element_type=F32)


def norm_forward(resid):
    inverse = lax.rsqrt(jnp.mean(resid * resid, axis=-1, keepdims=True) + EPS)
    return resid * inverse, inverse


def norm_backward(grad, normed, inverse):
    return inverse * (grad - normed * jnp.mean(grad * normed, axis=-1, keepdims=True))


def heads_first(matrix):
    t, w = matrix.shape
    return matrix.reshape(t, w // HEAD_DIM, HEAD_DIM).transpose(1, 0, 2)


def heads_last(stacked):
    h, t, w = stacked.shape
    return stacked.transpose(1, 0, 2).reshape(t, h * w)


def block_local(x, c, lengths, wq, wk, wv, wo, wg, wu, wd, gain1, gain2):
    t = x.shape[0]
    segment, positions = pack_info(lengths, t)
    cosine, sine = angles(positions)
    places = jnp.arange(t, dtype=jnp.int32)
    mask = (segment[:, None] == segment[None, :]) & (places[:, None] >= places[None, :])
    scale = HEAD_DIM ** (-0.5)
    q = rotate(heads_first(dot(x, wq)), cosine, sine).astype(BF16)
    k = rotate(heads_first(dot(x, wk)), cosine, sine).astype(BF16)
    v = heads_first(dot(x, wv).astype(BF16))
    bmm = lambda e, a, b: jnp.einsum(e, a, b, preferred_element_type=F32)
    s = jnp.where(mask, bmm("htd,hsd->hts", q, k) * scale, MASKED)
    e = jnp.exp(s - jnp.max(s, axis=-1, keepdims=True))
    probs = e / jnp.sum(e, axis=-1, keepdims=True)
    low = probs.astype(BF16)
    attn = heads_last(bmm("hts,hsd->htd", low, v).astype(BF16))
    n1, r1 = norm_forward(x.astype(F32) + dot(attn, wo))
    y1 = n1 * gain1
    y1_low = y1.astype(BF16)
    gate, up = dot(y1_low, wg), dot(y1_low, wu)
    sig = jax.nn.sigmoid(gate)
    hidden = (gate * sig * up).astype(BF16)
    n2, r2 = norm_forward(y1 + dot(hidden, wd))
    layer_out = (n2 * gain2).astype(BF16)
    cf = c.astype(F32)
    gain2_grad = jnp.sum(cf * n2, axis=0)
    dh2 = norm_backward(cf * gain2, n2, r2)
    dffn = dh2.astype(BF16)
    d_down = dot_tn(hidden, dffn)
    dhidden = dot_nt(dffn, wd)
    dgate = (dhidden * up * sig * (1.0 + gate * (1.0 - sig))).astype(BF16)
    dup = (dhidden * gate * sig).astype(BF16)
    d_gate, d_up = dot_tn(y1_low, dgate), dot_tn(y1_low, dup)
    dy1 = dh2 + dot_nt(dgate, wg) + dot_nt(dup, wu)
    gain1_grad = jnp.sum(dy1 * n1, axis=0)
    dh1 = norm_backward(dy1 * gain1, n1, r1)
    dbranch = dh1.astype(BF16)
    d_out = dot_tn(attn, dbranch)
    dattn = heads_first(dot_nt(dbranch, wo).astype(BF16))
    dprobs = bmm("htd,hsd->hts", dattn, v)
    dscores = (probs * (dprobs - jnp.sum(probs * dprobs, axis=-1, keepdims=True)) * scale).astype(BF16)
    dq = heads_last(rotate(bmm("hts,hsd->htd", dscores, k), cosine, -sine)).astype(BF16)
    dk = heads_last(rotate(bmm("hts,htd->hsd", dscores, q), cosine, -sine)).astype(BF16)
    dv = heads_last(bmm("hts,htd->hsd", low, dattn)).astype(BF16)
    d_q, d_k, d_v = dot_tn(x, dq), dot_tn(x, dk), dot_tn(x, dv)
    dx = dh1 + dot_nt(dq, wq) + dot_nt(dk, wk) + dot_nt(dv, wv)
    return layer_out, dx, (d_q, d_k, d_v, d_out, d_gate, d_up, d_down), gain1_grad, gain2_grad


def body(x, c, seq_lengths, wq, wk, wv, wo, wg, wu, wd, gain1, gain2):
    block = (lax.axis_index("row") * lax.axis_size("col") + lax.axis_index("col")) * lax.axis_size("dp") + lax.axis_index("dp")
    lengths = lax.dynamic_index_in_dim(seq_lengths, block, keepdims=False)
    full = [
        lax.all_gather(lax.all_gather(w, "col", axis=1, tiled=True), "row", axis=0, tiled=True)
        for w in (wq, wk, wv, wo, wg, wu, wd)
    ]
    layer_out, dx, grads, g1, g2 = block_local(x, c, lengths, *full, gain1, gain2)
    summed = []
    for g in grads:
        g = lax.psum_scatter(g.astype(BF16), "col", scatter_dimension=1, tiled=True)
        g = lax.psum_scatter(g, "row", scatter_dimension=0, tiled=True)
        summed.append(lax.psum(g, "dp").astype(F32))
    g1, g2 = lax.psum((g1, g2), ("row", "col", "dp"))
    return (layer_out, dx, *summed, g1, g2)


def solution(mesh):
    tok = P(("row", "col", "dp"), None)
    mat = P("row", "col")
    return jax.shard_map(
        body, mesh=mesh, in_specs=(tok, tok, P(), *[mat] * 7, P(), P()),
        out_specs=(tok, tok, *[mat] * 7, P(), P()), check_vma=False,
    )
```

```python
import functools

import jax
import jax.numpy as jnp
import numpy as np
from jax import lax
from jax.experimental import pallas as pl
from jax.experimental.pallas import tpu as pltpu
from jax.sharding import PartitionSpec as P

MESH = pl.DeviceIdType.MESH

HEAD_DIM = 64
HALF = HEAD_DIM // 2
EPS = 1e-06
MASKED = -1e30
BF16 = jnp.bfloat16
F32 = jnp.float32

T, D, FF, HEADS = 512, 768, 2048, 12
PAIRS = HEADS // 2
NAMES = ("q", "k", "v", "o", "g", "u", "d")
SHARD = {"q": (192, 384), "k": (192, 384), "v": (192, 384), "o": (192, 384), "g": (192, 1024), "u": (192, 1024), "d": (512, 384)}
PIECES = (
    ("q", 0, 192, 0, 384), ("k", 0, 192, 0, 384), ("v", 0, 192, 0, 384), ("o", 0, 192, 0, 384),
    ("g", 0, 192, 0, 512), ("u", 0, 192, 0, 512), ("g", 0, 192, 512, 512), ("u", 0, 192, 512, 512),
    ("d", 0, 128, 0, 384), ("d", 128, 128, 0, 384), ("d", 256, 128, 0, 384), ("d", 384, 128, 0, 384),
)
AHEAD = 3
CHUNKS = ("D0", "D1", "G0", "U0", "G1", "U1", "O", "A0", "A1", "A2")
SHAPE = {n: {"D": (256, 384), "G": (192, 512), "U": (192, 512), "O": (192, 384), "A": (192, 384)}[n[0]] for n in CHUNKS}
SLOTS = 2


def dot(a, b):
    return jnp.dot(a, b, preferred_element_type=F32)


def dot_nt(a, b):
    return lax.dot_general(a, b, (((1,), (1,)), ((), ())), preferred_element_type=F32)


def dot_tn(a, b):
    return lax.dot_general(a, b, (((0,), (0,)), ((), ())), preferred_element_type=F32)


def ds(start, size, multiple=None):
    if isinstance(start, int):
        return pl.ds(start, size)
    return pl.ds(pl.multiple_of(start, multiple or size), size)


def loop(n, f, start=0):
    def step(i, carry):
        f(i)
        return carry
    lax.fori_loop(start, n, step, 0)


SCRATCH = dict(
    wq=((D, D), BF16), wk=((D, D), BF16), wv=((D, D), BF16), wo=((D, D), BF16),
    wg=((D, FF), BF16), wu=((D, FF), BF16), wd=((FF, D), BF16),
    x=((T, D), BF16), xt=((D, T), BF16), c=((T, D), BF16),
    q=((T, D), BF16), k=((T, D), BF16), v=((T, D), BF16),
    p0=((HEADS, 256, 256), BF16), p1=((HEADS, 256, 512), BF16),
    attn=((T, D), BF16), attnt=((D, T), BF16),
    n1=((T, D), F32), y1=((T, D), BF16), y1t=((D, T), BF16),
    a=((T, FF), BF16), b=((T, FF), BF16), hid=((T, FF), BF16), hidt=((FF, T), BF16),
    h2=((T, D), F32), dffn=((T, D), BF16), bias=((T, T), F32),
    cos=((T, 128), F32), sin=((T, 128), F32), r1=((T, 1), F32),
    gains=((8, D), F32), gains_in=((5, 8, D), F32),
    gd=((2, 1024, 384), BF16), ggu=((4, 768, 512), BF16), ga=((4, 768, 384), BF16),
    send0=((SLOTS, 1024, 512), BF16),
)
REMOTE = dict(
    recv0=((SLOTS, 1024, 512), BF16),
    d1=((2, 2, 256, 384), BF16), gu1=((4, 2, 192, 512), BF16), qa1=((4, 2, 192, 384), BF16),
    d2=((2, 256, 384), BF16), gu2=((4, 192, 512), BF16), qa2=((4, 192, 384), BF16),
    da=((2, 256, 384), BF16), gua=((4, 192, 512), BF16), qaa=((4, 192, 384), BF16),
    db=((2, 256, 384), BF16), gub=((4, 192, 512), BF16), qab=((4, 192, 384), BF16),
)
SEMS = dict(
    lsem=(4,), gsend=(len(PIECES), 7), grecv=(len(PIECES), 7), glocal=(len(PIECES),),
    s0=(2, len(CHUNKS)), s1=(2, len(CHUNKS), 2), s2=(2, len(CHUNKS)), sz=(3, 2, len(CHUNKS)), so=(len(CHUNKS), 3), sg=(2, 5),
)


class Step:
    def __init__(self, refs, comm):
        self.__dict__.update(refs)
        self.comm = comm
        self.sent = []
        if comm:
            self.r, self.cc, self.z = lax.axis_index("row"), lax.axis_index("col"), lax.axis_index("dp")
        else:
            self.r = self.cc = self.z = jnp.int32(0)
        self.oc = 1 - self.cc
        r, z = self.r, self.z
        rx = r + 1 - 2 * (r % 2)
        ry = r + 2 - 4 * (r // 2)
        odd = z % 2
        self.rx, self.ry = rx, ry
        self.ga_row = rx + odd * (ry - rx)
        self.gb_row = ry + odd * (rx - ry)
        self.diag = 3 - r
        self.zn = z + 1 - 2 * odd
        self.zm = 3 - z

    def load(self):
        self.copies = []
        for i, (src, dst) in enumerate(((self.x_in, self.x), (self.c_in, self.c))):
            cp = pltpu.make_async_copy(src, dst, self.lsem.at[i])
            cp.start()
            self.copies.append(cp)

    def tables(self):
        block = (self.r * 2 + self.cc) * 4 + self.z
        lens = [self.lens[block, i] for i in range(4)]
        ends = [lens[0], lens[0] + lens[1], lens[0] + lens[1] + lens[2]]

        def angle_rows(i):
            rows = ds(i * 128, 128)
            place = lax.broadcasted_iota(jnp.int32, (128, 128), 0) + i * 128
            start = jnp.zeros((128, 128), jnp.int32)
            for l, e in zip(lens, ends):
                start = start + jnp.where(place >= e, l, 0)
            angle = (place - start).astype(F32) * self.freq[0:1, :]
            self.cos[rows, :] = jnp.cos(angle)
            self.sin[rows, :] = jnp.sin(angle) * self.freq[1:2, :]
        loop(4, angle_rows)

        def bias_rows(i):
            rows = ds(i * 128, 128)
            place = lax.broadcasted_iota(jnp.int32, (128, T), 0) + i * 128
            key = lax.broadcasted_iota(jnp.int32, (128, T), 1)
            seg_q = jnp.zeros((128, T), jnp.int32)
            seg_k = jnp.zeros((128, T), jnp.int32)
            for e in ends:
                seg_q = seg_q + jnp.where(place >= e, 1, 0)
                seg_k = seg_k + jnp.where(key >= e, 1, 0)
            ok = (seg_q == seg_k) & (place >= key)
            self.bias[rows, :] = jnp.where(ok, 0.0, MASKED)
        loop(4, bias_rows)

    def transpose_x(self):
        def step(i):
            cols = ds(i * 128, 128)
            self.xt[cols, :] = self.x[:, cols].T
        loop(6, step)

    def turn(self, t, sign):
        lane = lax.broadcasted_iota(jnp.int32, t.shape, 1)
        front = lane % HEAD_DIM < HALF
        partner = jnp.where(front, pltpu.roll(t, 128 - HALF, 1), pltpu.roll(t, HALF, 1))
        return t * self.cos[...] + partner * (self.sin[...] * sign)

    def project(self, name):
        w, out = getattr(self, "w" + name), getattr(self, name)

        def step(i):
            t = dot(self.x[...], w[:, ds(i * 256, 256)])
            for j in range(2):
                s = t[:, j * 128:(j + 1) * 128]
                if name != "v":
                    s = self.turn(s, 1.0)
                if name == "q":
                    s = s * HEAD_DIM ** -0.5
                out[:, ds(i * 256 + j * 128, 128, 128)] = s.astype(BF16)
        loop(3, step)

    def attend(self, first, last):
        def pair(hp):
            lanes = ds(hp * 128, 128)
            q2, k2, v2 = self.q[:, lanes], self.k[:, lanes], self.v[:, lanes]
            lane = lax.broadcasted_iota(jnp.int32, (T, 128), 1)
            outs = []
            for j in range(2):
                qm = jnp.where((lane >= HEAD_DIM) == bool(j), q2, jnp.zeros_like(q2))
                parts = []
                for qb in range(2):
                    keys = (qb + 1) * 256
                    rows = slice(qb * 256, qb * 256 + 256)
                    s = dot_nt(qm[rows], k2[:keys]) + self.bias[rows, :keys]
                    e = jnp.exp(s - jnp.max(s, axis=-1, keepdims=True))
                    p = (e * (1.0 / jnp.sum(e, axis=-1, keepdims=True))).astype(BF16)
                    (self.p1 if qb else self.p0)[2 * hp + j] = p
                    parts.append(dot(p, v2[:keys]))
                outs.append(parts)
            for qb in range(2):
                o = jnp.where(lane[:256] < HEAD_DIM, outs[0][qb], outs[1][qb]).astype(BF16)
                self.attn[qb * 256:(qb + 1) * 256, lanes] = o
                self.attnt[lanes, qb * 256:(qb + 1) * 256] = o.T
        loop(last, pair, first)

    def norm_one(self):
        def step(i):
            rows = ds(i * 256, 256)
            h = self.x[rows, :].astype(F32) + dot(self.attn[rows, :], self.wo[...])
            r = lax.rsqrt(jnp.mean(h * h, axis=-1, keepdims=True) + EPS)
            n = h * r
            self.n1[rows, :] = n
            self.r1[rows, :] = r
            y = (n * self.gain1[...]).astype(BF16)
            self.y1[rows, :] = y
            self.y1t[:, rows] = y.T
        loop(2, step)

    def ffn(self, half):
        def step(i):
            cols = ds((i // 2) * 1024 + half * 512 + (i % 2) * 256, 256)
            g = dot(self.y1[...], self.wg[:, cols])
            u = dot(self.y1[...], self.wu[:, cols])
            s = jax.nn.sigmoid(g)
            gs = g * s
            h = (gs * u).astype(BF16)
            self.hid[:, cols] = h
            self.hidt[cols, :] = h.T
            self.b[:, cols] = gs.astype(BF16)
            self.a[:, cols] = (u * s * (1.0 + g * (1.0 - s))).astype(BF16)
        loop(4, step)

    def down(self, part):
        last = part == 3

        def step(i):
            rows = ds(i * 256, 256)
            left = jnp.concatenate([self.hid[rows, s * 512 + part * 128:s * 512 + part * 128 + 128] for s in range(4)], axis=1)
            right = jnp.concatenate([self.wd[s * 512 + part * 128:s * 512 + part * 128 + 128, :] for s in range(4)], axis=0)
            t = dot(left, right)
            if part == 0:
                self.h2[rows, :] = self.n1[rows, :] * self.gain1[...] + t
                return
            h = self.h2[rows, :] + t
            if not last:
                self.h2[rows, :] = h
                return
            r = lax.rsqrt(jnp.mean(h * h, axis=-1, keepdims=True) + EPS)
            n = h * r
            c = self.c[rows, :].astype(F32)
            self.c[rows, :] = (n * self.gain2[...]).astype(BF16)
            self.gains[1:2, :] += jnp.sum(c * n, axis=0, keepdims=True)
            g = c * self.gain2[...]
            dh = r * (g - n * jnp.mean(g * n, axis=-1, keepdims=True))
            self.h2[rows, :] = dh
            self.dffn[rows, :] = dh.astype(BF16)
        if part == 0:
            self.gains[...] = jnp.zeros_like(self.gains)
        loop(2, step)
        if last:
            cp = pltpu.make_async_copy(self.c, self.layer_out, self.lsem.at[2])
            cp.start()
            self.copies.append(cp)

    def dhidden(self):
        def step(i):
            cols = ds(i * 256, 256)
            t = dot_nt(self.dffn[...], self.wd[cols, :])
            self.a[:, cols] = (t * self.a[:, cols].astype(F32)).astype(BF16)
            self.b[:, cols] = (t * self.b[:, cols].astype(F32)).astype(BF16)
        loop(8, step)

    def back_one(self):
        def step(i):
            rows = ds(i * 256, 256)
            dy = self.h2[rows, :] + dot_nt(self.a[rows, :], self.wg[...]) + dot_nt(self.b[rows, :], self.wu[...])
            n = self.n1[rows, :]
            self.gains[0:1, :] += jnp.sum(dy * n, axis=0, keepdims=True)
            g = dy * self.gain1[...]
            dh = self.r1[rows, :] * (g - n * jnp.mean(g * n, axis=-1, keepdims=True))
            self.h2[rows, :] = dh
            self.dffn[rows, :] = dh.astype(BF16)
        loop(2, step)

    def dattn(self):
        def step(i):
            cols = ds(i * 256, 256)
            self.x[:, cols] = dot_nt(self.dffn[...], self.wo[cols, :]).astype(BF16)
        loop(3, step)

    def attend_back(self, hp):
        lanes = ds(hp * 128, 128)
        q2, k2, v2, do2 = self.q[:, lanes], self.k[:, lanes], self.v[:, lanes], self.x[:, lanes]
        lane = lax.broadcasted_iota(jnp.int32, (T, 128), 1)
        dqs, dks, dvs = [], [], []
        for j in range(2):
            dom = jnp.where((lane >= HEAD_DIM) == bool(j), do2, jnp.zeros_like(do2))
            dq, dk, dv = [], [], []
            for qb in range(2):
                keys = (qb + 1) * 256
                rows = slice(qb * 256, qb * 256 + 256)
                low = (self.p1 if qb else self.p0)[2 * hp + j]
                p = low.astype(F32)
                dp = dot_nt(dom[rows], v2[:keys])
                s = (p * (dp - jnp.sum(p * dp, axis=-1, keepdims=True))).astype(BF16)
                dq.append(dot(s, k2[:keys]))
                dk.append(dot_tn(s, q2[rows]))
                dv.append(dot_tn(low, do2[rows]))
            dqs.append(dq)
            dks.append(dk)
            dvs.append(dv)
        front = lane[:256] < HEAD_DIM
        dq = jnp.concatenate([jnp.where(front, dqs[0][b], dqs[1][b]) for b in range(2)], axis=0)

        def whole(parts):
            return jnp.concatenate([parts[0] + parts[1][:256], parts[1][256:]], axis=0)
        dk = jnp.where(lane < HEAD_DIM, whole(dks[0]), whole(dks[1]))
        dv = jnp.where(lane < HEAD_DIM, whole(dvs[0]), whole(dvs[1]))
        self.q[:, lanes] = self.turn(dq * HEAD_DIM ** -0.5, -1.0).astype(BF16)
        self.k[:, lanes] = self.turn(dk, -1.0).astype(BF16)
        self.v[:, lanes] = dv.astype(BF16)

    def attend_back_two(self, i):
        loop(2, lambda h: self.attend_back(h * 3 + i))

    def input_grad(self):
        def step(i):
            rows = ds(i * 256, 256)
            self.h2[rows, :] += (dot_nt(self.q[rows, :], self.wq[...]) + dot_nt(self.k[rows, :], self.wk[...])
                                 + dot_nt(self.v[rows, :], self.wv[...]))
        loop(2, step)
        cp = pltpu.make_async_copy(self.h2, self.dx, self.lsem.at[3])
        cp.start()
        self.copies.append(cp)

    def own(self, n):
        return {"D": lambda: self.gd.at[int(n[1:])], "G": lambda: self.ggu.at[2 * int(n[1])], "U": lambda: self.ggu.at[2 * int(n[1]) + 1],
                "O": lambda: self.ga.at[3], "A": lambda: self.ga.at[int(n[1:])]}[n[0]]()

    def out0(self, n):
        rows, cols = SHAPE[n]
        return self.send0.at[CHUNKS.index(n) % SLOTS, 0:4 * rows, 0:cols]

    def grad(self, n):
        own, other = self.own(n), self.out0(n)
        c0 = self.cc == 0

        def both(rows, t):
            lo, hi = t[:, :384], t[:, 384:]
            own[rows, :] = jnp.where(c0, lo, hi).astype(BF16)
            other[rows, :] = jnp.where(c0, hi, lo).astype(BF16)
        if n[0] == "D":
            j = int(n[1])

            def step(i):
                both(ds(i * 256, 256), dot(self.hidt[ds(i * 512 + j * 256, 256), :], self.dffn[...]))
            loop(4, step)
        elif n[0] == "O":
            def step(i):
                rows = ds(i * 256, 256)
                both(rows, dot(self.attnt[rows, :], self.dffn[...]))
            loop(3, step)
        elif n[0] in "GU":
            j = int(n[1])
            src = self.a if n[0] == "G" else self.b
            for half, dst in ((self.oc, other), (self.cc, own)):
                def step(i, half=half, dst=dst):
                    t = dot(self.y1t[...], src[:, ds(half * 1024 + j * 512 + i * 256, 256)])
                    dst[:, ds(i * 256, 256)] = t.astype(BF16)
                loop(2, step)
        else:
            j = int(n[1])
            for half, dst in ((self.oc, other), (self.cc, own)):
                lanes = ds((half * 3 + j) * 128, 128)
                right = jnp.concatenate([self.q[:, lanes], self.k[:, lanes], self.v[:, lanes]], axis=1)
                for i in range(3):
                    dst[i * 256:(i + 1) * 256, :] = dot(self.xt[i * 256:(i + 1) * 256, :], right).astype(BF16)

    def remote(self, src, dst, send, recv, **where):
        cp = pltpu.make_async_remote_copy(src_ref=src, dst_ref=dst, send_sem=send, recv_sem=recv, device_id=where, device_id_type=MESH)
        return cp

    def enter(self):
        barrier = pltpu.get_barrier_semaphore()
        for where in ({"col": self.oc}, {"row": self.rx}, {"row": self.ry}, {"dp": self.zn}, {"dp": self.zm}):
            pl.semaphore_signal(barrier, inc=1, device_id=where, device_id_type=MESH)
        pl.semaphore_wait(barrier, 5)

    def region(self, i, row, core):
        n, r0, nr, c0, nc = PIECES[i]
        rows, cols = SHARD[n]
        return getattr(self, "w" + n).at[ds(row * rows + r0, nr, 64), ds(core * cols + c0, nc, 128)]

    def shard(self, i):
        n, r0, nr, c0, nc = PIECES[i]
        return getattr(self, "h" + n).at[r0:r0 + nr, c0:c0 + nc]

    def gather(self, i, what):
        row = (self.r, self.ga_row, self.ga_row, self.r, self.ga_row, self.diag, self.gb_row)[what]
        where = ({"row": self.ga_row}, {"row": self.gb_row}, {"dp": self.zn}, *[{"col": self.oc}] * 4)[what]
        src = self.shard(i) if what in (0, 3) else self.region(i, row, self.cc)
        return self.remote(src, self.region(i, row, self.cc), self.gsend.at[i, what], self.grecv.at[i, what], **where)

    def go(self, i, *whats):
        for what in whats:
            cp = self.gather(i, what)
            cp.start()
            self.sent.append(cp)

    def gather_start(self):
        for i in range(AHEAD):
            self.go(i, 0)
        for i in range(len(PIECES)):
            self.go(i, 3)
            pltpu.make_async_copy(self.shard(i), self.region(i, self.r, self.cc), self.glocal.at[i]).start()

    def relay(self, i):
        self.gather(i, 0).wait_recv()
        self.go(i, 1, 2, 4)
        if i + AHEAD < len(PIECES):
            self.go(i + AHEAD, 0)

    def relay_two(self, i):
        self.gather(i, 1).wait_recv()
        self.go(i, 5)
        self.gather(i, 2).wait_recv()
        self.go(i, 6)

    def ready(self, i):
        pltpu.make_async_copy(self.shard(i), self.region(i, self.r, self.cc), self.glocal.at[i]).wait()
        for what in (3, 4, 5, 6):
            self.gather(i, what).wait_recv()

    def part(self, kind, n):
        i = {"D": lambda: int(n[1:]), "G": lambda: 2 * int(n[1]), "U": lambda: 2 * int(n[1]) + 1, "O": lambda: 3, "A": lambda: int(n[1:])}[n[0]]()
        return getattr(self, {"D": "d", "G": "gu", "U": "gu", "O": "qa", "A": "qa"}[n[0]] + kind).at[i]

    def chunk(self, n):
        k = CHUNKS.index(n)
        rows, cols = SHAPE[n]
        ra, rb = (self.rx, self.ry) if k % 2 == 0 else (self.ry, self.rx)
        block = lambda row: ds(row * rows, rows)
        return k, rows, cols, ra, rb, block

    def copy0(self, n):
        k, rows, cols, *_ = self.chunk(n)
        at = (k % SLOTS, slice(0, 4 * rows), slice(0, cols))
        return self.remote(self.send0.at[at], self.recv0.at[at], self.s0.at[0, k], self.s0.at[1, k], col=self.oc)

    def copy1(self, n, which):
        k, rows, cols, ra, rb, block = self.chunk(n)
        row = (ra, self.diag)[which]
        return self.remote(self.own(n).at[block(row), :], self.part("1", n).at[which], self.s1.at[0, k, which], self.s1.at[1, k, which], row=ra)

    def copy2(self, n):
        k, rows, cols, ra, rb, block = self.chunk(n)
        return self.remote(self.own(n).at[block(rb), :], self.part("2", n), self.s2.at[0, k], self.s2.at[1, k], row=rb)

    def copy_z(self, n, leg):
        k, rows, cols, ra, rb, block = self.chunk(n)
        src = self.part("2", n) if leg == 2 else self.own(n).at[block(self.r), :]
        dst = self.part("b" if leg == 1 else "a", n)
        return self.remote(src, dst, self.sz.at[leg, 0, k], self.sz.at[leg, 1, k], dp=self.zm if leg == 1 else self.zn)

    def inner(self):
        return ((self.z + 1) // 2) % 2 == 1

    def outer(self):
        return ((self.z + 1) // 2) % 2 == 0

    def add(self, ref, other):
        ref[...] = (ref[...].astype(F32) + other[...].astype(F32)).astype(BF16)

    def make(self, n):
        k = CHUNKS.index(n)
        if k >= SLOTS:
            self.copy0(CHUNKS[k - SLOTS]).wait_send()
        self.grad(n)
        if k >= SLOTS:
            pl.semaphore_wait(self.credit, 1)
        self.copy0(n).start()

    def sum0(self, n):
        k, rows, cols, ra, rb, block = self.chunk(n)
        self.copy0(n).wait_recv()
        own = self.own(n)
        got = self.recv0.at[k % SLOTS, 0:4 * rows, 0:cols]
        for row, which in ((self.diag, 1), (ra, 0), (rb, None), (self.r, None)):
            self.add(own.at[block(row), :], got.at[block(row), :])
            if which is not None:
                self.copy1(n, which).start()
        if k + SLOTS < len(CHUNKS):
            pl.semaphore_signal(self.credit, inc=1, device_id={"col": self.oc}, device_id_type=MESH)

    def sum1(self, n):
        k, rows, cols, ra, rb, block = self.chunk(n)
        own, got = self.own(n), self.part("1", n)
        self.copy1(n, 1).wait_recv()
        self.add(own.at[block(rb), :], got.at[1])
        self.copy2(n).start()
        self.copy1(n, 0).wait_recv()
        self.add(own.at[block(self.r), :], got.at[0])

    def sum2(self, n):
        k, rows, cols, ra, rb, block = self.chunk(n)
        own = self.own(n).at[block(self.r), :]
        self.copy2(n).wait_recv()
        self.add(own, self.part("2", n))

        @pl.when(self.outer())
        def _():
            self.copy_z(n, 0).start()

    def sum_z1(self, n):
        k, rows, cols, ra, rb, block = self.chunk(n)

        @pl.when(self.inner())
        def _():
            self.copy_z(n, 0).wait_recv()
            self.add(self.own(n).at[block(self.r), :], self.part("a", n))
            self.copy_z(n, 1).start()

    def sum_z2(self, n):
        k, rows, cols, ra, rb, block = self.chunk(n)

        @pl.when(self.inner())
        def _():
            self.copy_z(n, 1).wait_recv()
            total = self.part("2", n)
            own = self.own(n).at[block(self.r), :]
            total[...] = (own[...].astype(F32) + self.part("b", n)[...].astype(F32)).astype(BF16)
            self.copy_z(n, 2).start()
            for cp in self.results(n, total):
                cp.start()

    def sum_z3(self, n):
        @pl.when(self.outer())
        def _():
            self.copy_z(n, 2).wait_recv()
            for cp in self.results(n, self.part("a", n)):
                cp.start()

    def results(self, n, src):
        k = CHUNKS.index(n)
        j = int(n[1:] or 0)
        if n[0] == "A":
            return [pltpu.make_async_copy(src.at[:, i * 128:(i + 1) * 128], getattr(self, "out_" + m).at[:, j * 128:(j + 1) * 128], self.so.at[k, i])
                    for i, m in enumerate("qkv")]
        out = getattr(self, "out_" + n[0].lower())
        dst = {"D": lambda: out.at[j * 256:(j + 1) * 256, :], "G": lambda: out.at[:, j * 512:(j + 1) * 512],
               "U": lambda: out.at[:, j * 512:(j + 1) * 512], "O": lambda: out}[n[0]]()
        return [pltpu.make_async_copy(src, dst, self.so.at[k, 0])]

    def gains_copy(self, t):
        where = ({"col": self.oc}, {"row": self.rx}, {"row": self.ry}, {"dp": self.zn}, {"dp": self.zm})[t]
        return self.remote(self.gains, self.gains_in.at[t], self.sg.at[0, t], self.sg.at[1, t], **where)

    def gains_send(self, t):
        self.gains_copy(t).start()

    def gains_add(self, t):
        self.gains_copy(t).wait()
        self.gains[...] += self.gains_in[t]

    def finish(self):
        for cp in self.sent:
            cp.wait_send()
        for k, n in enumerate(CHUNKS):
            if k >= len(CHUNKS) - SLOTS:
                self.copy0(n).wait_send()
            self.copy1(n, 0).wait_send()
            self.copy1(n, 1).wait_send()
            self.copy2(n).wait_send()

        @pl.when(self.outer())
        def _():
            for n in CHUNKS:
                self.copy_z(n, 0).wait_send()
                for cp in self.results(n, self.part("a", n)):
                    cp.wait()

        @pl.when(self.inner())
        def _():
            for n in CHUNKS:
                self.copy_z(n, 1).wait_send()
                self.copy_z(n, 2).wait_send()
                for cp in self.results(n, self.part("2", n)):
                    cp.wait()
        for cp in self.copies:
            cp.wait()


PLAN = (
    "start", "tables", "transpose_x", "R0", "R1", "r0", "R2", "r1", "ready0", "project:q", "R3", "r2", "ready1", "project:k", "ready2", "project:v",
    "attend:0,1", "R4", "r3", "attend:1,2", "R5", "r4", "attend:2,4", "R6", "r5", "attend:4,6", "ready3", "norm_one", "R7", "r6", "ready4", "ready5", "ffn:0", "R8", "r7", "R9", "r8", "ready6", "ready7", "ffn:1",
    "R10", "r9", "ready8", "down:0", "R11", "r10", "ready9", "down:1", "r11", "ready10", "down:2", "ready11", "down:3",
    "make:D0", "make:D1", "sum0:D0", "dhidden", "sum0:D1", "make:G0", "make:U0", "sum0:G0", "sum1:D0", "make:G1", "sum0:U0", "sum1:D1", "sum2:D0", "make:U1", "sum0:G1", "sum1:G0", "sum2:D1", "z1:D0",
    "back_one", "gs0", "sum0:U1", "make:O", "z2:D0", "z1:D1", "sum1:U0", "sum2:G0", "dattn", "sum0:O", "ge0", "gs1", "z3:D0", "z2:D1", "z1:G0", "sum1:G1", "sum2:U0",
    "back:0", "ge1", "gs2", "make:A0", "sum0:A0", "z3:D1", "z2:G0", "z1:U0", "sum1:U1", "sum2:G1", "sum1:O", "z3:G0", "z2:U0", "z1:G1", "sum2:U1", "sum2:O", "ge2", "gs3",
    "back:1", "make:A1", "sum0:A1", "sum1:A0", "z3:U0", "z2:G1", "z1:U1", "z1:O", "sum2:A0", "z3:G1", "z2:U1", "z2:O", "ge3", "gs4",
    "back:2", "make:A2", "sum0:A2", "sum1:A1", "z3:U1", "z3:O", "z1:A0", "sum2:A1", "z2:A0", "ge4", "input_grad", "sum1:A2", "z3:A0", "z1:A1", "sum2:A2", "z2:A1", "z1:A2", "z3:A1", "z2:A2", "z3:A2",
)

OUTS = ("layer_out", "dx", "out_q", "out_k", "out_v", "out_o", "out_g", "out_u", "out_d", "gain1_out", "gain2_out")
INS = ("x_in", "c_in", "lens", "hq", "hk", "hv", "ho", "hg", "hu", "hd", "gain1", "gain2", "freq")


def step_kernel(*refs):
    names = INS + OUTS + tuple(SCRATCH) + tuple(REMOTE) + tuple(SEMS) + ("credit",)
    s = Step(dict(zip(names, refs, strict=True)), True)
    s.enter()
    for word in PLAN:
        op, _, arg = word.partition(":")
        if op == "start":
            s.gather_start()
            s.load()
        elif op[0] == "R":
            s.relay(int(op[1:]))
        elif op[0] == "r" and op[1:].isdigit():
            s.relay_two(int(op[1:]))
        elif op.startswith("ready"):
            s.ready(int(op[5:]))
        elif op == "attend":
            s.attend(*map(int, arg.split(",")))
        elif op in ("ffn", "down", "back"):
            {"ffn": s.ffn, "down": s.down, "back": s.attend_back_two}[op](int(arg))
        elif op in ("make", "sum0", "sum1", "sum2", "project"):
            getattr(s, op)(arg)
        elif op in ("z1", "z2", "z3"):
            getattr(s, "sum_" + op)(arg)
        elif op[:2] == "gs":
            s.gains_send(int(op[2:]))
        elif op[:2] == "ge":
            s.gains_add(int(op[2:]))
        else:
            if op == "transpose_x":
                s.copies[0].wait()
                s.copies[1].wait()
                s.copies = []
            getattr(s, op)()
    s.gain1_out[...] = s.gains[0:1, :]
    s.gain2_out[...] = s.gains[1:2, :]
    s.finish()


def fused_body(x, c, lens, wq, wk, wv, wo, wg, wu, wd, gain1, gain2):
    lane = np.arange(128)
    freq = np.zeros((8, 128), np.float32)
    freq[0] = 10000.0 ** (-(lane % HALF) * (2.0 / HEAD_DIM))
    freq[1] = np.where(lane % HEAD_DIM < HALF, -1.0, 1.0)
    hbm, vmem, smem = (pl.BlockSpec(memory_space=m) for m in (pl.ANY, pltpu.VMEM, pltpu.SMEM))
    struct = jax.ShapeDtypeStruct
    shards = [SHARD[n] for n in NAMES]
    out = pl.pallas_call(
        step_kernel,
        out_shape=[struct((T, D), BF16), struct((T, D), F32), *[struct(s, BF16) for s in shards], struct((1, D), F32), struct((1, D), F32)],
        in_specs=[hbm, hbm, smem, *[hbm] * 7, vmem, vmem, vmem],
        out_specs=[*[hbm] * 9, vmem, vmem],
        scratch_shapes=[*[pltpu.VMEM(*v) for v in (SCRATCH | REMOTE).values()], *[pltpu.SemaphoreType.DMA(v) for v in SEMS.values()],
                        pltpu.SemaphoreType.REGULAR],
        compiler_params=pltpu.CompilerParams(collective_id=0, has_side_effects=True, vmem_limit_bytes=63 << 20),
        name="step",
    )(x, c, lens, wq, wk, wv, wo, wg, wu, wd, gain1[None], gain2[None], jnp.asarray(freq))
    return (out[0], out[1], *[g.astype(F32) for g in out[2:9]], out[9][0], out[10][0])


def pack_info(lengths_row, places_count):
    places = jnp.arange(places_count, dtype=jnp.int32)
    segment = jnp.zeros((places_count,), jnp.int32)
    start = jnp.zeros((places_count,), jnp.int32)
    end = jnp.int32(0)
    for i in range(lengths_row.shape[0]):
        end = end + lengths_row[i]
        passed = (places >= end).astype(jnp.int32)
        segment = segment + passed
        start = start + passed * lengths_row[i]
    return segment, (places - start).astype(F32)


def angles(positions):
    frequency = 10000.0 ** (-jnp.arange(HALF, dtype=F32) * (2.0 / HEAD_DIM))
    turned = positions[..., None] * frequency
    return jnp.cos(turned), jnp.sin(turned)


def rotate(values, cosine, sine):
    a, b = values[..., :HALF], values[..., HALF:]
    return jnp.concatenate([a * cosine - b * sine, b * cosine + a * sine], axis=-1)


def norm_forward(resid):
    inverse = lax.rsqrt(jnp.mean(resid * resid, axis=-1, keepdims=True) + EPS)
    return resid * inverse, inverse


def norm_backward(grad, normed, inverse):
    return inverse * (grad - normed * jnp.mean(grad * normed, axis=-1, keepdims=True))


def heads_first(matrix):
    t, w = matrix.shape
    return matrix.reshape(t, w // HEAD_DIM, HEAD_DIM).transpose(1, 0, 2)


def heads_last(stacked):
    h, t, w = stacked.shape
    return stacked.transpose(1, 0, 2).reshape(t, h * w)


def block_local(x, c, lengths, wq, wk, wv, wo, wg, wu, wd, gain1, gain2):
    t = x.shape[0]
    segment, positions = pack_info(lengths, t)
    cosine, sine = angles(positions)
    places = jnp.arange(t, dtype=jnp.int32)
    mask = (segment[:, None] == segment[None, :]) & (places[:, None] >= places[None, :])
    scale = HEAD_DIM ** (-0.5)
    q = rotate(heads_first(dot(x, wq)), cosine, sine).astype(BF16)
    k = rotate(heads_first(dot(x, wk)), cosine, sine).astype(BF16)
    v = heads_first(dot(x, wv).astype(BF16))
    bmm = lambda e, a, b: jnp.einsum(e, a, b, preferred_element_type=F32)
    s = jnp.where(mask, bmm("htd,hsd->hts", q, k) * scale, MASKED)
    e = jnp.exp(s - jnp.max(s, axis=-1, keepdims=True))
    probs = e / jnp.sum(e, axis=-1, keepdims=True)
    low = probs.astype(BF16)
    attn = heads_last(bmm("hts,hsd->htd", low, v).astype(BF16))
    n1, r1 = norm_forward(x.astype(F32) + dot(attn, wo))
    y1 = n1 * gain1
    y1_low = y1.astype(BF16)
    gate, up = dot(y1_low, wg), dot(y1_low, wu)
    sig = jax.nn.sigmoid(gate)
    hidden = (gate * sig * up).astype(BF16)
    n2, r2 = norm_forward(y1 + dot(hidden, wd))
    layer_out = (n2 * gain2).astype(BF16)
    cf = c.astype(F32)
    gain2_grad = jnp.sum(cf * n2, axis=0)
    dh2 = norm_backward(cf * gain2, n2, r2)
    dffn = dh2.astype(BF16)
    d_down = dot_tn(hidden, dffn)
    dhidden = dot_nt(dffn, wd)
    dgate = (dhidden * up * sig * (1.0 + gate * (1.0 - sig))).astype(BF16)
    dup = (dhidden * gate * sig).astype(BF16)
    d_gate, d_up = dot_tn(y1_low, dgate), dot_tn(y1_low, dup)
    dy1 = dh2 + dot_nt(dgate, wg) + dot_nt(dup, wu)
    gain1_grad = jnp.sum(dy1 * n1, axis=0)
    dh1 = norm_backward(dy1 * gain1, n1, r1)
    dbranch = dh1.astype(BF16)
    d_out = dot_tn(attn, dbranch)
    dattn = heads_first(dot_nt(dbranch, wo).astype(BF16))
    dprobs = bmm("htd,hsd->hts", dattn, v)
    dscores = (probs * (dprobs - jnp.sum(probs * dprobs, axis=-1, keepdims=True)) * scale).astype(BF16)
    dq = heads_last(rotate(bmm("hts,hsd->htd", dscores, k), cosine, -sine)).astype(BF16)
    dk = heads_last(rotate(bmm("hts,htd->hsd", dscores, q), cosine, -sine)).astype(BF16)
    dv = heads_last(bmm("hts,htd->hsd", low, dattn)).astype(BF16)
    d_q, d_k, d_v = dot_tn(x, dq), dot_tn(x, dk), dot_tn(x, dv)
    dx = dh1 + dot_nt(dq, wq) + dot_nt(dk, wk) + dot_nt(dv, wv)
    return layer_out, dx, (d_q, d_k, d_v, d_out, d_gate, d_up, d_down), gain1_grad, gain2_grad


def body(x, c, seq_lengths, wq, wk, wv, wo, wg, wu, wd, gain1, gain2):
    block = (lax.axis_index("row") * lax.axis_size("col") + lax.axis_index("col")) * lax.axis_size("dp") + lax.axis_index("dp")
    lengths = lax.dynamic_index_in_dim(seq_lengths, block, keepdims=False)
    full = [
        lax.all_gather(lax.all_gather(w, "col", axis=1, tiled=True), "row", axis=0, tiled=True)
        for w in (wq, wk, wv, wo, wg, wu, wd)
    ]
    layer_out, dx, grads, g1, g2 = block_local(x, c, lengths, *full, gain1, gain2)
    summed = []
    for g in grads:
        g = lax.psum_scatter(g.astype(BF16), "col", scatter_dimension=1, tiled=True)
        g = lax.psum_scatter(g, "row", scatter_dimension=0, tiled=True)
        summed.append(lax.psum(g, "dp").astype(F32))
    g1, g2 = lax.psum((g1, g2), ("row", "col", "dp"))
    return (layer_out, dx, *summed, g1, g2)


def solution(mesh):
    tok = P(("row", "col", "dp"), None)
    mat = P("row", "col")
    fits = tuple(mesh.shape[a] for a in ("row", "col", "dp")) == (4, 2, 4)
    return jax.shard_map(
        fused_body if fits else body, mesh=mesh, in_specs=(tok, tok, P(), *[mat] * 7, P(), P()),
        out_specs=(tok, tok, *[mat] * 7, P(), P()), check_vma=False,
    )
```

```python
import math

import jax
import jax.numpy as jnp
from jax import lax
from jax.experimental import pallas as pl
from jax.experimental.pallas import tpu as pltpu
from jax.sharding import PartitionSpec as P

MESH = pl.DeviceIdType.MESH

HEAD_DIM = 64
HALF = HEAD_DIM // 2
EPS = 1e-06
MASKED = -1e30
BF16 = jnp.bfloat16
F32 = jnp.float32

T, D, FF, HEADS = 512, 768, 2048, 12
PAIRS = HEADS // 2
NAMES = ("q", "k", "v", "o", "g", "u", "d")
SHARD = {"q": (192, 384), "k": (192, 384), "v": (192, 384), "o": (192, 384), "g": (192, 1024), "u": (192, 1024), "d": (512, 384)}
PIECES = (
    ("q", 0, 192, 0, 384), ("k", 0, 192, 0, 384), ("v", 0, 192, 0, 384), ("o", 0, 192, 0, 384),
    ("g", 0, 192, 0, 512), ("u", 0, 192, 0, 512), ("g", 0, 192, 512, 512), ("u", 0, 192, 512, 512),
    ("d", 0, 128, 0, 384), ("d", 128, 128, 0, 384), ("d", 256, 128, 0, 384), ("d", 384, 128, 0, 384),
)
AHEAD = 3
CHUNKS = ("D0", "D1", "G0", "U0", "G1", "U1", "O", "A0", "A1", "B0", "B1")
SHAPE = {n: {"D": (256, 384), "G": (192, 512), "U": (192, 512), "O": (192, 384), "A": (192, 384), "B": (96, 384)}[n[0]] for n in CHUNKS}
SLOTS = 2


def dot(a, b):
    return jnp.dot(a, b, preferred_element_type=F32)


def dot_nt(a, b):
    return lax.dot_general(a, b, (((1,), (1,)), ((), ())), preferred_element_type=F32)


def dot_tn(a, b):
    return lax.dot_general(a, b, (((0,), (0,)), ((), ())), preferred_element_type=F32)


def ds(start, size, multiple=None):
    if isinstance(start, int):
        return pl.ds(start, size)
    return pl.ds(pl.multiple_of(start, multiple or size), size)


def loop(n, f, start=0):
    def step(i, carry):
        f(i)
        return carry
    lax.fori_loop(start, n, step, 0)


SCRATCH = dict(
    wq=((D, D), BF16), wk=((D, D), BF16), wv=((D, D), BF16), wo=((D, D), BF16),
    wg=((D, FF), BF16), wu=((D, FF), BF16), wd=((FF, D), BF16),
    x=((T, D), BF16), xt=((D, T), BF16), c=((T, D), BF16),
    q=((T, D), BF16), k=((T, D), BF16), v=((T, D), BF16),
    p0=((HEADS, 256, 256), BF16), p1=((HEADS, 256, 512), BF16),
    attn=((T, D), BF16), attnt=((D, T), BF16),
    n1=((T, D), F32), y1=((T, D), BF16), y1t=((D, T), BF16),
    a=((T, FF), BF16), b=((T, FF), BF16), hid=((T, FF), BF16), hidt=((FF, T), BF16),
    h2=((T, D), F32), dffn=((T, D), BF16), bias=((T, T), F32),
    cos=((T, 128), F32), sin=((T, 128), F32), r1=((T, 1), F32),
    gain1=((1, D), F32), gain2=((1, D), F32), gains=((8, D), F32), gains_in=((5, 8, D), F32),
    gd=((2, 1024, 384), BF16), ggu=((4, 768, 512), BF16), ga=((4, 768, 384), BF16),
    send0=((SLOTS, 1024, 512), BF16),
)
REMOTE = dict(
    recv0=((SLOTS, 1024, 512), BF16),
    d1=((2, 2, 256, 384), BF16), gu1=((4, 2, 192, 512), BF16), qa1=((4, 2, 192, 384), BF16),
    d2=((2, 256, 384), BF16), gu2=((4, 192, 512), BF16), qa2=((4, 192, 384), BF16),
    da=((2, 256, 384), BF16), gua=((4, 192, 512), BF16), qaa=((4, 192, 384), BF16),
    db=((2, 256, 384), BF16), gub=((4, 192, 512), BF16), qab=((4, 192, 384), BF16),
)
SEMS = dict(
    lsem=(4,), gsend=(len(PIECES), 7), grecv=(len(PIECES), 7), glocal=(len(PIECES),),
    s0=(2, len(CHUNKS)), s1=(2, len(CHUNKS), 2), s2=(2, len(CHUNKS)), sz=(3, 2, len(CHUNKS)), so=(len(CHUNKS), 3), sg=(2, 5),
)


class Step:
    def __init__(self, refs, comm):
        self.__dict__.update(refs)
        self.comm = comm
        self.copies, self.sent, self.sent0, self.ended = [], [], {}, []
        if comm:
            self.r, self.cc, self.z = lax.axis_index("row"), lax.axis_index("col"), lax.axis_index("dp")
        else:
            self.r = self.cc = self.z = jnp.int32(0)
        self.oc = 1 - self.cc
        r, z = self.r, self.z
        rx = r + 1 - 2 * (r % 2)
        ry = r + 2 - 4 * (r // 2)
        odd = z % 2
        self.rx, self.ry = rx, ry
        self.ga_row = rx + odd * (ry - rx)
        self.gb_row = ry + odd * (rx - ry)
        self.diag = 3 - r
        self.zn = z + 1 - 2 * odd
        self.zm = 3 - z

    def load(self):
        self.copies = []
        for i, (src, dst) in enumerate(((self.x_in, self.x), (self.c_in, self.c))):
            cp = pltpu.make_async_copy(src, dst, self.lsem.at[i])
            cp.start()
            self.copies.append(cp)

    def loaded(self):
        for cp in self.copies:
            cp.wait()
        self.copies = []

    def tables(self):
        block = (self.r * 2 + self.cc) * 4 + self.z
        mine = lax.broadcasted_iota(jnp.int32, (1, self.lens.shape[1]), 1) == block
        lens = [jnp.sum(jnp.where(mine, self.lens[i:i + 1, :], 0), axis=1, keepdims=True) for i in range(3)]
        ends = [lens[0], lens[0] + lens[1], lens[0] + lens[1] + lens[2]]

        def angle_rows(i):
            rows = ds(i * 128, 128)
            place = lax.broadcasted_iota(jnp.int32, (128, 128), 0) + i * 128
            lane = lax.broadcasted_iota(jnp.int32, (1, 128), 1)
            frequency = jnp.exp((lane % HALF).astype(F32) * (-2.0 / HEAD_DIM * math.log(10000.0)))
            start = jnp.zeros((128, 128), jnp.int32)
            for l, e in zip(lens, ends):
                start = start + jnp.where(place >= e, l, 0)
            angle = (place - start).astype(F32) * frequency
            self.cos[rows, :] = jnp.cos(angle)
            self.sin[rows, :] = jnp.sin(angle) * jnp.where(lane % HEAD_DIM < HALF, -1.0, 1.0)
        loop(4, angle_rows)
        self.gain1[...] = self.gain1_in[...].reshape(1, D)
        self.gain2[...] = self.gain2_in[...].reshape(1, D)

        def bias_rows(i):
            rows = ds(i * 128, 128)
            place = lax.broadcasted_iota(jnp.int32, (128, T), 0) + i * 128
            key = lax.broadcasted_iota(jnp.int32, (128, T), 1)
            seg_q = jnp.zeros((128, T), jnp.int32)
            seg_k = jnp.zeros((128, T), jnp.int32)
            for e in ends:
                seg_q = seg_q + jnp.where(place >= e, 1, 0)
                seg_k = seg_k + jnp.where(key >= e, 1, 0)
            ok = (seg_q == seg_k) & (place >= key)
            self.bias[rows, :] = jnp.where(ok, 0.0, MASKED)
        loop(4, bias_rows)

    def transpose_x(self):
        def step(i):
            cols = ds(i * 128, 128)
            self.xt[cols, :] = self.x[:, cols].T
        loop(6, step)

    def turn(self, t, sign):
        lane = lax.broadcasted_iota(jnp.int32, t.shape, 1)
        front = lane % HEAD_DIM < HALF
        partner = jnp.where(front, pltpu.roll(t, 128 - HALF, 1), pltpu.roll(t, HALF, 1))
        return t * self.cos[...] + partner * (self.sin[...] * sign)

    def project(self, name):
        w, out = getattr(self, "w" + name), getattr(self, name)

        def step(i):
            t = dot(self.x[...], w[:, ds(i * 256, 256)])
            for j in range(2):
                s = t[:, j * 128:(j + 1) * 128]
                if name != "v":
                    s = self.turn(s, 1.0)
                if name == "q":
                    s = s * HEAD_DIM ** -0.5
                out[:, ds(i * 256 + j * 128, 128, 128)] = s.astype(BF16)
        loop(3, step)

    def attend(self, first, last):
        def pair(hp):
            lanes = ds(hp * 128, 128)
            q2, k2, v2 = self.q[:, lanes], self.k[:, lanes], self.v[:, lanes]
            lane = lax.broadcasted_iota(jnp.int32, (T, 128), 1)
            outs = []
            for j in range(2):
                qm = jnp.where((lane >= HEAD_DIM) == bool(j), q2, jnp.zeros_like(q2))
                parts = []
                for qb in range(2):
                    keys = (qb + 1) * 256
                    rows = slice(qb * 256, qb * 256 + 256)
                    s = dot_nt(qm[rows], k2[:keys]) + self.bias[rows, :keys]
                    e = jnp.exp(s - jnp.max(s, axis=-1, keepdims=True))
                    p = (e * (1.0 / jnp.sum(e, axis=-1, keepdims=True))).astype(BF16)
                    (self.p1 if qb else self.p0)[2 * hp + j] = p
                    parts.append(dot(p, v2[:keys]))
                outs.append(parts)
            for qb in range(2):
                o = jnp.where(lane[:256] < HEAD_DIM, outs[0][qb], outs[1][qb]).astype(BF16)
                self.attn[qb * 256:(qb + 1) * 256, lanes] = o
                self.attnt[lanes, qb * 256:(qb + 1) * 256] = o.T
        loop(last, pair, first)

    def norm_one(self):
        def step(i):
            rows = ds(i * 256, 256)
            h = self.x[rows, :].astype(F32) + dot(self.attn[rows, :], self.wo[...])
            r = lax.rsqrt(jnp.mean(h * h, axis=-1, keepdims=True) + EPS)
            n = h * r
            self.n1[rows, :] = n
            self.r1[rows, :] = r
            y = (n * self.gain1[...]).astype(BF16)
            self.y1[rows, :] = y
            self.y1t[:, rows] = y.T
        loop(2, step)

    def ffn(self, half):
        def step(i):
            cols = ds((i // 2) * 1024 + half * 512 + (i % 2) * 256, 256)
            g = dot(self.y1[...], self.wg[:, cols])
            u = dot(self.y1[...], self.wu[:, cols])
            s = jax.nn.sigmoid(g)
            gs = g * s
            h = (gs * u).astype(BF16)
            self.hid[:, cols] = h
            self.hidt[cols, :] = h.T
            self.b[:, cols] = gs.astype(BF16)
            self.a[:, cols] = (u * s * (1.0 + g * (1.0 - s))).astype(BF16)
        loop(4, step)

    def down(self, part):
        last = part == 3

        def step(i):
            rows = ds(i * 256, 256)
            left = jnp.concatenate([self.hid[rows, s * 512 + part * 128:s * 512 + part * 128 + 128] for s in range(4)], axis=1)
            right = jnp.concatenate([self.wd[s * 512 + part * 128:s * 512 + part * 128 + 128, :] for s in range(4)], axis=0)
            t = dot(left, right)
            if part == 0:
                self.h2[rows, :] = self.n1[rows, :] * self.gain1[...] + t
                return
            h = self.h2[rows, :] + t
            if not last:
                self.h2[rows, :] = h
                return
            r = lax.rsqrt(jnp.mean(h * h, axis=-1, keepdims=True) + EPS)
            n = h * r
            c = self.c[rows, :].astype(F32)
            self.c[rows, :] = (n * self.gain2[...]).astype(BF16)
            self.gains[1:2, :] += jnp.sum(c * n, axis=0, keepdims=True)
            g = c * self.gain2[...]
            dh = r * (g - n * jnp.mean(g * n, axis=-1, keepdims=True))
            self.h2[rows, :] = dh
            self.dffn[rows, :] = dh.astype(BF16)
        if part == 0:
            self.gains[...] = jnp.zeros_like(self.gains)
        loop(2, step)
        if last:
            cp = pltpu.make_async_copy(self.c, self.layer_out, self.lsem.at[2])
            cp.start()
            self.copies.append(cp)

    def dhidden(self):
        def step(i):
            cols = ds(i * 256, 256)
            t = dot_nt(self.dffn[...], self.wd[cols, :])
            self.a[:, cols] = (t * self.a[:, cols].astype(F32)).astype(BF16)
            self.b[:, cols] = (t * self.b[:, cols].astype(F32)).astype(BF16)
        loop(8, step)

    def back_one(self):
        def step(i):
            rows = ds(i * 256, 256)
            dy = self.h2[rows, :] + dot_nt(self.a[rows, :], self.wg[...]) + dot_nt(self.b[rows, :], self.wu[...])
            n = self.n1[rows, :]
            self.gains[0:1, :] += jnp.sum(dy * n, axis=0, keepdims=True)
            g = dy * self.gain1[...]
            dh = self.r1[rows, :] * (g - n * jnp.mean(g * n, axis=-1, keepdims=True))
            self.h2[rows, :] = dh
            self.dffn[rows, :] = dh.astype(BF16)
        loop(2, step)

    def dattn(self):
        def step(i):
            cols = ds(i * 256, 256)
            self.x[:, cols] = dot_nt(self.dffn[...], self.wo[cols, :]).astype(BF16)
        loop(3, step)

    def attend_back(self, hp):
        lanes = ds(hp * 128, 128)
        q2, k2, v2, do2 = self.q[:, lanes], self.k[:, lanes], self.v[:, lanes], self.x[:, lanes]
        lane = lax.broadcasted_iota(jnp.int32, (T, 128), 1)
        dqs, dks, dvs = [], [], []
        for j in range(2):
            dom = jnp.where((lane >= HEAD_DIM) == bool(j), do2, jnp.zeros_like(do2))
            dq, dk, dv = [], [], []
            for qb in range(2):
                keys = (qb + 1) * 256
                rows = slice(qb * 256, qb * 256 + 256)
                low = (self.p1 if qb else self.p0)[2 * hp + j]
                p = low.astype(F32)
                dp = dot_nt(dom[rows], v2[:keys])
                s = (p * (dp - jnp.sum(p * dp, axis=-1, keepdims=True))).astype(BF16)
                dq.append(dot(s, k2[:keys]))
                dk.append(dot_tn(s, q2[rows]))
                dv.append(dot_tn(low, do2[rows]))
            dqs.append(dq)
            dks.append(dk)
            dvs.append(dv)
        front = lane[:256] < HEAD_DIM
        dq = jnp.concatenate([jnp.where(front, dqs[0][b], dqs[1][b]) for b in range(2)], axis=0)

        def whole(parts):
            return jnp.concatenate([parts[0] + parts[1][:256], parts[1][256:]], axis=0)
        dk = jnp.where(lane < HEAD_DIM, whole(dks[0]), whole(dks[1]))
        dv = jnp.where(lane < HEAD_DIM, whole(dvs[0]), whole(dvs[1]))
        self.q[:, lanes] = self.turn(dq * HEAD_DIM ** -0.5, -1.0).astype(BF16)
        self.k[:, lanes] = self.turn(dk, -1.0).astype(BF16)
        self.v[:, lanes] = dv.astype(BF16)

    def attend_back_two(self, i):
        loop(2, lambda h: self.attend_back(h * 3 + i))

    def input_grad(self):
        def step(i):
            rows = ds(i * 256, 256)
            self.h2[rows, :] += (dot_nt(self.q[rows, :], self.wq[...]) + dot_nt(self.k[rows, :], self.wk[...])
                                 + dot_nt(self.v[rows, :], self.wv[...]))
        loop(2, step)
        cp = pltpu.make_async_copy(self.h2, self.dx, self.lsem.at[3])
        cp.start()
        self.copies.append(cp)

    def pick(self, n, d, gu, qa):
        j = int(n[1:] or 0)
        if n[0] == "D":
            return d.at[j]
        if n[0] in "GU":
            return gu.at[2 * j + (n[0] == "U")]
        if n[0] == "B":
            rows = qa.shape[-2] // 2
            return qa.at[(2, *[slice(None)] * (len(qa.shape) - 3), slice(j * rows, (j + 1) * rows))]
        return qa.at[3 if n[0] == "O" else j]

    def own(self, n):
        return self.pick(n, self.gd, self.ggu, self.ga)

    def out0(self, n):
        rows, cols = SHAPE[n]
        return self.send0.at[CHUNKS.index(n) % SLOTS, 0:4 * rows, 0:cols]

    def grad(self, n):
        own, other = self.own(n), self.out0(n)
        c0 = self.cc == 0

        def both(rows, t):
            lo, hi = t[:, :384], t[:, 384:]
            own[rows, :] = jnp.where(c0, lo, hi).astype(BF16)
            other[rows, :] = jnp.where(c0, hi, lo).astype(BF16)
        if n[0] == "D":
            j = int(n[1])

            def step(i):
                both(ds(i * 256, 256), dot(self.hidt[ds(i * 512 + j * 256, 256), :], self.dffn[...]))
            loop(4, step)
        elif n[0] == "O":
            def step(i):
                rows = ds(i * 256, 256)
                both(rows, dot(self.attnt[rows, :], self.dffn[...]))
            loop(3, step)
        elif n[0] in "GU":
            j = int(n[1])
            src = self.a if n[0] == "G" else self.b
            for half, dst in ((self.oc, other), (self.cc, own)):
                def step(i, half=half, dst=dst):
                    t = dot(self.y1t[...], src[:, ds(half * 1024 + j * 512 + i * 256, 256)])
                    dst[:, ds(i * 256, 256)] = t.astype(BF16)
                loop(2, step)
        else:
            j = 2 if n[0] == "B" else int(n[1])
            for half, dst in ((self.oc, other), (self.cc, own)):
                lanes = ds((half * 3 + j) * 128, 128)
                right = jnp.concatenate([self.q[:, lanes], self.k[:, lanes], self.v[:, lanes]], axis=1)
                if n[0] == "B":
                    at = int(n[1]) * 96
                    left = jnp.concatenate([self.xt[s * 192 + at:s * 192 + at + 96, :] for s in range(4)], axis=0)
                    dst[...] = dot(left, right).astype(BF16)
                    continue
                for i in range(3):
                    dst[i * 256:(i + 1) * 256, :] = dot(self.xt[i * 256:(i + 1) * 256, :], right).astype(BF16)

    def remote(self, src, dst, send, recv, **where):
        cp = pltpu.make_async_remote_copy(src_ref=src, dst_ref=dst, send_sem=send, recv_sem=recv, device_id=where, device_id_type=MESH)
        return cp

    def begin(self, cp, sent):
        cp.start()
        sent.append(cp)

    def enter(self):
        barrier = pltpu.get_barrier_semaphore()
        for where in ({"col": self.oc}, {"row": self.rx}, {"row": self.ry}, {"dp": self.zn}, {"dp": self.zm}):
            pl.semaphore_signal(barrier, inc=1, device_id=where, device_id_type=MESH)
        pl.semaphore_wait(barrier, 5)

    def region(self, i, row, core):
        n, r0, nr, c0, nc = PIECES[i]
        rows, cols = SHARD[n]
        return getattr(self, "w" + n).at[ds(row * rows + r0, nr, 64), ds(core * cols + c0, nc, 128)]

    def shard(self, i):
        n, r0, nr, c0, nc = PIECES[i]
        return getattr(self, "h" + n).at[r0:r0 + nr, c0:c0 + nc]

    def gather(self, i, what):
        row = (self.r, self.ga_row, self.ga_row, self.r, self.ga_row, self.diag, self.gb_row)[what]
        where = ({"row": self.ga_row}, {"row": self.gb_row}, {"dp": self.zn}, *[{"col": self.oc}] * 4)[what]
        src = self.shard(i) if what in (0, 3) else self.region(i, row, self.cc)
        return self.remote(src, self.region(i, row, self.cc), self.gsend.at[i, what], self.grecv.at[i, what], **where)

    def go(self, i, *whats):
        for what in whats:
            self.begin(self.gather(i, what), self.sent)

    def start(self):
        for i in range(AHEAD):
            self.go(i, 0)
        for i in range(len(PIECES)):
            self.go(i, 3)
            pltpu.make_async_copy(self.shard(i), self.region(i, self.r, self.cc), self.glocal.at[i]).start()

    def relay(self, i):
        self.gather(i, 0).wait_recv()
        self.go(i, 1, 2, 4)
        if i + AHEAD < len(PIECES):
            self.go(i + AHEAD, 0)

    def relay_two(self, i):
        self.gather(i, 1).wait_recv()
        self.go(i, 5)
        self.gather(i, 2).wait_recv()
        self.go(i, 6)

    def ready(self, i):
        pltpu.make_async_copy(self.shard(i), self.region(i, self.r, self.cc), self.glocal.at[i]).wait()
        for what in (3, 4, 5, 6):
            self.gather(i, what).wait_recv()

    def part(self, kind, n):
        d, gu, qa = {"1": (self.d1, self.gu1, self.qa1), "2": (self.d2, self.gu2, self.qa2), "a": (self.da, self.gua, self.qaa),
                     "b": (self.db, self.gub, self.qab)}[kind]
        return self.pick(n, d, gu, qa)

    def chunk(self, n):
        k = CHUNKS.index(n)
        rows, cols = SHAPE[n]
        ra, rb = (self.rx, self.ry) if k % 2 == 0 else (self.ry, self.rx)
        block = lambda row: ds(row * rows, rows)
        return k, rows, cols, ra, rb, block

    def copy0(self, n):
        k, rows, cols, *_ = self.chunk(n)
        at = (k % SLOTS, slice(0, 4 * rows), slice(0, cols))
        return self.remote(self.send0.at[at], self.recv0.at[at], self.s0.at[0, k], self.s0.at[1, k], col=self.oc)

    def copy1(self, n, which):
        k, rows, cols, ra, rb, block = self.chunk(n)
        row = (ra, self.diag)[which]
        return self.remote(self.own(n).at[block(row), :], self.part("1", n).at[which], self.s1.at[0, k, which], self.s1.at[1, k, which], row=ra)

    def copy2(self, n):
        k, rows, cols, ra, rb, block = self.chunk(n)
        return self.remote(self.own(n).at[block(rb), :], self.part("2", n), self.s2.at[0, k], self.s2.at[1, k], row=rb)

    def copy_z(self, n, leg):
        k, rows, cols, ra, rb, block = self.chunk(n)
        src = self.part("2", n) if leg == 2 else self.own(n).at[block(self.r), :]
        dst = self.part("b" if leg == 1 else "a", n)
        return self.remote(src, dst, self.sz.at[leg, 0, k], self.sz.at[leg, 1, k], dp=self.zm if leg == 1 else self.zn)

    def inner(self):
        return ((self.z + 1) // 2) % 2 == 1

    def outer(self):
        return ((self.z + 1) // 2) % 2 == 0

    def add(self, ref, other):
        ref[...] = (ref[...].astype(F32) + other[...].astype(F32)).astype(BF16)

    def make(self, n):
        k = CHUNKS.index(n)
        if k >= SLOTS:
            self.sent0[k - SLOTS].wait_send()
            self.sent = [cp for cp in self.sent if cp is not self.sent0[k - SLOTS]]
        self.grad(n)
        if k >= SLOTS:
            pl.semaphore_wait(self.credit, 1)
        self.begin(self.copy0(n), self.sent)
        self.sent0[k] = self.sent[-1]

    def sum0(self, n):
        k, rows, cols, ra, rb, block = self.chunk(n)
        self.copy0(n).wait_recv()
        own = self.own(n)
        got = self.recv0.at[k % SLOTS, 0:4 * rows, 0:cols]
        for row, which in ((self.diag, 1), (ra, 0), (rb, None), (self.r, None)):
            self.add(own.at[block(row), :], got.at[block(row), :])
            if which is not None:
                self.begin(self.copy1(n, which), self.sent)
        if k + SLOTS < len(CHUNKS):
            pl.semaphore_signal(self.credit, inc=1, device_id={"col": self.oc}, device_id_type=MESH)

    def sum1(self, n):
        k, rows, cols, ra, rb, block = self.chunk(n)
        self.copy1(n, 1).wait_recv()
        self.add(self.own(n).at[block(rb), :], self.part("1", n).at[1])
        self.begin(self.copy2(n), self.sent)

    def sum2(self, n):
        k, rows, cols, ra, rb, block = self.chunk(n)
        own = self.own(n).at[block(self.r), :]
        self.copy1(n, 0).wait_recv()
        self.copy2(n).wait_recv()
        own[...] = (own[...].astype(F32) + self.part("1", n)[0].astype(F32) + self.part("2", n)[...].astype(F32)).astype(BF16)

        @pl.when(self.outer())
        def _():
            self.copy_z(n, 0).start()

    def sum_z1(self, n):
        k, rows, cols, ra, rb, block = self.chunk(n)

        @pl.when(self.inner())
        def _():
            self.copy_z(n, 0).wait_recv()
            self.add(self.own(n).at[block(self.r), :], self.part("a", n))
            self.copy_z(n, 1).start()

    def sum_z2(self, n):
        k, rows, cols, ra, rb, block = self.chunk(n)

        @pl.when(self.inner())
        def _():
            self.copy_z(n, 1).wait_recv()
            total = self.part("2", n)
            own = self.own(n).at[block(self.r), :]
            total[...] = (own[...].astype(F32) + self.part("b", n)[...].astype(F32)).astype(BF16)
            self.copy_z(n, 2).start()
            for cp in self.results(n, total):
                cp.start()

    def sum_z3(self, n):
        self.ended.append(n)

        @pl.when(self.outer())
        def _():
            self.copy_z(n, 2).wait_recv()
            for cp in self.results(n, self.part("a", n)):
                cp.start()

    def results(self, n, src):
        k = CHUNKS.index(n)
        j = int(n[1:] or 0)
        if n[0] in "AB":
            rows, j = (slice(j * 96, j * 96 + 96), 2) if n[0] == "B" else (slice(0, 192), j)
            return [pltpu.make_async_copy(src.at[:, i * 128:(i + 1) * 128], getattr(self, "out_" + m).at[rows, j * 128:(j + 1) * 128], self.so.at[k, i])
                    for i, m in enumerate("qkv")]
        out = getattr(self, "out_" + n[0].lower())
        dst = {"D": lambda: out.at[j * 256:(j + 1) * 256, :], "G": lambda: out.at[:, j * 512:(j + 1) * 512],
               "U": lambda: out.at[:, j * 512:(j + 1) * 512], "O": lambda: out}[n[0]]()
        return [pltpu.make_async_copy(src, dst, self.so.at[k, 0])]

    def gains_copy(self, t):
        where = ({"col": self.oc}, {"row": self.rx}, {"row": self.ry}, {"dp": self.zn}, {"dp": self.zm})[t]
        return self.remote(self.gains, self.gains_in.at[t], self.sg.at[0, t], self.sg.at[1, t], **where)

    def gains_send(self, t):
        self.gains_copy(t).start()

    def gains_add(self, t):
        self.gains_copy(t).wait()
        self.gains[...] += self.gains_in[t]

    def settle(self):
        slots = [cp for cp in self.sent if any(cp is s for s in self.sent0.values())]
        for cp in self.sent:
            if not any(cp is s for s in slots):
                cp.wait_send()
        self.sent = slots

    def finish(self):
        for cp in self.sent:
            cp.wait_send()
        for inner, legs, kind in ((self.outer(), (0,), "a"), (self.inner(), (1, 2), "2")):
            @pl.when(inner)
            def _():
                for n in self.ended:
                    for leg in legs:
                        self.copy_z(n, leg).wait_send()
                    for cp in self.results(n, self.part(kind, n)):
                        cp.wait()
        for cp in self.copies:
            cp.wait()


D0, D1, G0, U0, G1, U1, O, A0, A1, B0, B1 = CHUNKS


def order(s):
    s.start(); s.load(); s.tables(); s.loaded(); s.transpose_x(); s.relay(0); s.relay(1); s.relay_two(0); s.relay(2); s.relay_two(1); s.ready(0); s.project('q'); s.relay(3); s.relay_two(2)
    s.ready(1); s.project('k'); s.ready(2); s.project('v'); s.attend(0, 1); s.relay(4); s.relay_two(3); s.attend(1, 2); s.relay(5); s.relay_two(4); s.attend(2, 4); s.relay(6); s.relay_two(5); s.attend(4, 6)
    s.ready(3); s.norm_one(); s.relay(7); s.relay_two(6); s.ready(4); s.ready(5); s.ffn(0); s.relay(8); s.relay_two(7); s.relay(9); s.relay_two(8); s.ready(6); s.ready(7); s.ffn(1)
    s.relay(10); s.relay_two(9); s.ready(8); s.down(0); s.relay(11); s.relay_two(10); s.ready(9); s.down(1); s.relay_two(11); s.ready(10); s.down(2); s.ready(11); s.down(3); s.make(D0)
    s.make(D1); s.sum0(D0); s.sum0(D1); s.dhidden(); s.make(G0); s.sum1(D1); s.sum1(D0); s.make(U0); s.sum0(G0); s.make(G1); s.sum0(U0); s.make(U1); s.sum2(D1); s.back_one()
    s.gains_send(0); s.dattn(); s.sum1(G0); s.sum1(U0); s.sum0(G1); s.sum2(D0); s.sum_z1(D1); s.sum0(U1); s.make(O); s.attend_back_two(0); s.sum_z1(D0); s.sum2(G0); s.gains_add(0); s.gains_send(1)
    s.sum2(U0); s.attend_back_two(1); s.sum1(U1); s.sum_z2(D1); s.make(A0); s.sum_z1(G0); s.sum1(G1); s.sum0(O); s.sum0(A0); s.sum_z2(D0); s.make(A1); s.gains_add(1); s.gains_send(2); s.sum2(U1)
    s.sum_z1(U0); s.sum0(A1); s.sum_z2(G0); s.sum2(G1); s.attend_back_two(2); s.sum1(O); s.sum_z1(U1); s.sum_z2(U0); s.make(B0); s.sum1(A0); s.gains_add(2); s.gains_send(3); s.make(B1); s.sum1(A1)
    s.sum_z1(G1); s.sum0(B0); s.sum2(O); s.sum_z2(U1); s.sum2(A1); s.sum0(B1); s.sum_z1(O); s.sum_z2(G1); s.settle(); s.sum2(A0); s.gains_add(3); s.gains_send(4); s.sum_z3(D0); s.sum1(B0)
    s.sum_z1(A1); s.sum1(B1); s.sum_z3(G0); s.sum_z3(U1); s.sum_z2(O); s.sum2(B0); s.sum_z1(A0); s.sum2(B1); s.sum_z2(A1); s.gains_add(4); s.sum_z1(B0); s.sum_z3(U0); s.sum_z2(A0); s.sum_z3(G1)
    s.sum_z1(B1); s.sum_z2(B0); s.input_grad(); s.sum_z3(O); s.sum_z2(B1); s.sum_z3(B0); s.sum_z3(D1); s.sum_z3(A1); s.sum_z3(A0); s.sum_z3(B1)


OUTS = ("layer_out", "dx", "out_q", "out_k", "out_v", "out_o", "out_g", "out_u", "out_d", "gains_out")
INS = ("x_in", "c_in", "lens", "hq", "hk", "hv", "ho", "hg", "hu", "hd", "gain1_in", "gain2_in")


def step_kernel(*refs):
    names = INS + OUTS + tuple(SCRATCH) + tuple(REMOTE) + tuple(SEMS) + ("credit",)
    s = Step(dict(zip(names, refs, strict=True)), True)
    s.enter()
    order(s)
    s.gains_out[...] = s.gains[...]
    s.finish()


def widen_kernel(*refs):
    ins, outs, low, wide, sems = refs[:10], refs[10:21], refs[21:30], refs[30:37], refs[37]
    wide = [*low[:2], *wide]
    loads = [pltpu.make_async_copy(ins[i], low[i], sems.at[0, i]) for i in range(9)]
    stores = [pltpu.make_async_copy(wide[i], outs[i], sems.at[1, i]) for i in range(9)]
    for cp in loads:
        cp.start()
    outs[9][...] = ins[9][0, :]
    outs[10][...] = ins[9][1, :]
    for i in range(9):
        loads[i].wait()
        if i > 1:
            wide[i][...] = low[i][...].astype(F32)
        stores[i].start()
    for cp in stores:
        cp.wait()


def fused_body(x, c, lens, wq, wk, wv, wo, wg, wu, wd, gain1, gain2):
    hbm, vmem = pl.BlockSpec(memory_space=pl.ANY), pl.BlockSpec(memory_space=pltpu.VMEM)
    struct = jax.ShapeDtypeStruct
    shards = [SHARD[n] for n in NAMES]
    out = pl.pallas_call(
        step_kernel,
        out_shape=[struct((T, D), BF16), struct((T, D), F32), *[struct(s, BF16) for s in shards], struct((8, D), F32)],
        in_specs=[hbm, hbm, vmem, *[hbm] * 7, vmem, vmem],
        out_specs=[*[hbm] * 9, vmem],
        scratch_shapes=[*[pltpu.VMEM(*v) for v in (SCRATCH | REMOTE).values()], *[pltpu.SemaphoreType.DMA(v) for v in SEMS.values()],
                        pltpu.SemaphoreType.REGULAR],
        compiler_params=pltpu.CompilerParams(collective_id=0, has_side_effects=True, vmem_limit_bytes=63 << 20),
        name="step",
    )(x, c, lens.T, wq, wk, wv, wo, wg, wu, wd, gain1, gain2)
    return pl.pallas_call(
        widen_kernel,
        out_shape=[struct((T, D), BF16), struct((T, D), F32), *[struct(s, F32) for s in shards], struct((D,), F32), struct((D,), F32)],
        in_specs=[*[hbm] * 9, vmem],
        out_specs=[*[hbm] * 9, vmem, vmem],
        scratch_shapes=[pltpu.VMEM((T, D), BF16), pltpu.VMEM((T, D), F32), *[pltpu.VMEM(s, BF16) for s in shards],
                        *[pltpu.VMEM(s, F32) for s in shards], pltpu.SemaphoreType.DMA((2, 9))],
        compiler_params=pltpu.CompilerParams(vmem_limit_bytes=63 << 20),
        name="widen",
    )(*out)


def pack_info(lengths_row, places_count):
    places = jnp.arange(places_count, dtype=jnp.int32)
    segment = jnp.zeros((places_count,), jnp.int32)
    start = jnp.zeros((places_count,), jnp.int32)
    end = jnp.int32(0)
    for i in range(lengths_row.shape[0]):
        end = end + lengths_row[i]
        passed = (places >= end).astype(jnp.int32)
        segment = segment + passed
        start = start + passed * lengths_row[i]
    return segment, (places - start).astype(F32)


def angles(positions):
    frequency = 10000.0 ** (-jnp.arange(HALF, dtype=F32) * (2.0 / HEAD_DIM))
    turned = positions[..., None] * frequency
    return jnp.cos(turned), jnp.sin(turned)


def rotate(values, cosine, sine):
    a, b = values[..., :HALF], values[..., HALF:]
    return jnp.concatenate([a * cosine - b * sine, b * cosine + a * sine], axis=-1)


def norm_forward(resid):
    inverse = lax.rsqrt(jnp.mean(resid * resid, axis=-1, keepdims=True) + EPS)
    return resid * inverse, inverse


def norm_backward(grad, normed, inverse):
    return inverse * (grad - normed * jnp.mean(grad * normed, axis=-1, keepdims=True))


def heads_first(matrix):
    t, w = matrix.shape
    return matrix.reshape(t, w // HEAD_DIM, HEAD_DIM).transpose(1, 0, 2)


def heads_last(stacked):
    h, t, w = stacked.shape
    return stacked.transpose(1, 0, 2).reshape(t, h * w)


def block_local(x, c, lengths, wq, wk, wv, wo, wg, wu, wd, gain1, gain2):
    t = x.shape[0]
    segment, positions = pack_info(lengths, t)
    cosine, sine = angles(positions)
    places = jnp.arange(t, dtype=jnp.int32)
    mask = (segment[:, None] == segment[None, :]) & (places[:, None] >= places[None, :])
    scale = HEAD_DIM ** (-0.5)
    q = rotate(heads_first(dot(x, wq)), cosine, sine).astype(BF16)
    k = rotate(heads_first(dot(x, wk)), cosine, sine).astype(BF16)
    v = heads_first(dot(x, wv).astype(BF16))
    bmm = lambda e, a, b: jnp.einsum(e, a, b, preferred_element_type=F32)
    s = jnp.where(mask, bmm("htd,hsd->hts", q, k) * scale, MASKED)
    e = jnp.exp(s - jnp.max(s, axis=-1, keepdims=True))
    probs = e / jnp.sum(e, axis=-1, keepdims=True)
    low = probs.astype(BF16)
    attn = heads_last(bmm("hts,hsd->htd", low, v).astype(BF16))
    n1, r1 = norm_forward(x.astype(F32) + dot(attn, wo))
    y1 = n1 * gain1
    y1_low = y1.astype(BF16)
    gate, up = dot(y1_low, wg), dot(y1_low, wu)
    sig = jax.nn.sigmoid(gate)
    hidden = (gate * sig * up).astype(BF16)
    n2, r2 = norm_forward(y1 + dot(hidden, wd))
    layer_out = (n2 * gain2).astype(BF16)
    cf = c.astype(F32)
    gain2_grad = jnp.sum(cf * n2, axis=0)
    dh2 = norm_backward(cf * gain2, n2, r2)
    dffn = dh2.astype(BF16)
    d_down = dot_tn(hidden, dffn)
    dhidden = dot_nt(dffn, wd)
    dgate = (dhidden * up * sig * (1.0 + gate * (1.0 - sig))).astype(BF16)
    dup = (dhidden * gate * sig).astype(BF16)
    d_gate, d_up = dot_tn(y1_low, dgate), dot_tn(y1_low, dup)
    dy1 = dh2 + dot_nt(dgate, wg) + dot_nt(dup, wu)
    gain1_grad = jnp.sum(dy1 * n1, axis=0)
    dh1 = norm_backward(dy1 * gain1, n1, r1)
    dbranch = dh1.astype(BF16)
    d_out = dot_tn(attn, dbranch)
    dattn = heads_first(dot_nt(dbranch, wo).astype(BF16))
    dprobs = bmm("htd,hsd->hts", dattn, v)
    dscores = (probs * (dprobs - jnp.sum(probs * dprobs, axis=-1, keepdims=True)) * scale).astype(BF16)
    dq = heads_last(rotate(bmm("hts,hsd->htd", dscores, k), cosine, -sine)).astype(BF16)
    dk = heads_last(rotate(bmm("hts,htd->hsd", dscores, q), cosine, -sine)).astype(BF16)
    dv = heads_last(bmm("hts,htd->hsd", low, dattn)).astype(BF16)
    d_q, d_k, d_v = dot_tn(x, dq), dot_tn(x, dk), dot_tn(x, dv)
    dx = dh1 + dot_nt(dq, wq) + dot_nt(dk, wk) + dot_nt(dv, wv)
    return layer_out, dx, (d_q, d_k, d_v, d_out, d_gate, d_up, d_down), gain1_grad, gain2_grad


def body(x, c, seq_lengths, wq, wk, wv, wo, wg, wu, wd, gain1, gain2):
    block = (lax.axis_index("row") * lax.axis_size("col") + lax.axis_index("col")) * lax.axis_size("dp") + lax.axis_index("dp")
    lengths = lax.dynamic_index_in_dim(seq_lengths, block, keepdims=False)
    full = [
        lax.all_gather(lax.all_gather(w, "col", axis=1, tiled=True), "row", axis=0, tiled=True)
        for w in (wq, wk, wv, wo, wg, wu, wd)
    ]
    layer_out, dx, grads, g1, g2 = block_local(x, c, lengths, *full, gain1, gain2)
    summed = []
    for g in grads:
        g = lax.psum_scatter(g.astype(BF16), "col", scatter_dimension=1, tiled=True)
        g = lax.psum_scatter(g, "row", scatter_dimension=0, tiled=True)
        summed.append(lax.psum(g, "dp").astype(F32))
    g1, g2 = lax.psum((g1, g2), ("row", "col", "dp"))
    return (layer_out, dx, *summed, g1, g2)


def solution(mesh):
    tok = P(("row", "col", "dp"), None)
    mat = P("row", "col")
    fits = tuple(mesh.shape[a] for a in ("row", "col", "dp")) == (4, 2, 4)
    return jax.shard_map(
        fused_body if fits else body, mesh=mesh, in_specs=(tok, tok, P(), *[mat] * 7, P(), P()),
        out_specs=(tok, tok, *[mat] * 7, P(), P()), check_vma=False,
    )
```

```python
import math

import jax
import jax.numpy as jnp
from jax import lax
from jax.experimental import pallas as pl
from jax.experimental.pallas import tpu as pltpu
from jax.sharding import PartitionSpec as P

MESH = pl.DeviceIdType.MESH

HEAD_DIM = 64
HALF = HEAD_DIM // 2
EPS = 1e-06
MASKED = -1e30
BF16 = jnp.bfloat16
F32 = jnp.float32

T, D, FF, HEADS = 512, 768, 2048, 12
PAIRS = HEADS // 2
NAMES = ("q", "k", "v", "o", "g", "u", "d")
SHARD = {"q": (192, 384), "k": (192, 384), "v": (192, 384), "o": (192, 384), "g": (192, 1024), "u": (192, 1024), "d": (512, 384)}
PIECES = (
    ("q", 0, 64, 0, 384), ("q", 64, 64, 0, 384), ("q", 128, 64, 0, 384), ("k", 0, 192, 0, 384), ("v", 0, 192, 0, 384), ("o", 0, 192, 0, 384),
    ("g", 0, 192, 0, 512), ("u", 0, 192, 0, 512), ("g", 0, 192, 512, 512), ("u", 0, 192, 512, 512),
    ("d", 0, 128, 0, 384), ("d", 128, 128, 0, 384), ("d", 256, 128, 0, 384), ("d", 384, 128, 0, 384),
)
CHUNKS = ("D0", "D1", "D2", "D3", "G0", "U0", "G1", "U1", "O", "A0", "A1", "B0", "B1")
SHAPE = {n: {"D": (128, 384), "G": (192, 512), "U": (192, 512), "O": (192, 384), "A": (192, 384), "B": (96, 384)}[n[0]] for n in CHUNKS}
SPREAD = ("D0", "D1", "D2", "D3", "G0", "U0")
SLOTS = 3


def dot(a, b):
    return jnp.dot(a, b, preferred_element_type=F32)


def dot_nt(a, b):
    return lax.dot_general(a, b, (((1,), (1,)), ((), ())), preferred_element_type=F32)


def dot_tn(a, b):
    return lax.dot_general(a, b, (((0,), (0,)), ((), ())), preferred_element_type=F32)


def ds(start, size, multiple=None):
    if isinstance(start, int):
        return pl.ds(start, size)
    return pl.ds(pl.multiple_of(start, multiple or size), size)


def loop(n, f, start=0):
    def step(i, carry):
        f(i)
        return carry
    lax.fori_loop(start, n, step, 0)


SCRATCH = dict(
    wq=((D, D), BF16), wk=((D, D), BF16), wv=((D, D), BF16), wo=((D, D), BF16),
    wg=((D, FF), BF16), wu=((D, FF), BF16), wd=((FF, D), BF16),
    x=((T, D), BF16), xt=((D, T), BF16), c=((T, D), BF16),
    q=((T, D), BF16), k=((T, D), BF16), v=((T, D), BF16),
    p0=((HEADS, 256, 256), BF16), p1=((HEADS, 256, 512), BF16),
    attn=((T, D), BF16), attnt=((D, T), BF16),
    n1=((T, D), F32), y1=((T, D), BF16), y1t=((D, T), BF16),
    a=((T, FF), BF16), b=((T, FF), BF16), hid=((T, FF), BF16), hidt=((FF, T), BF16),
    h2=((T, D), F32), dffn=((T, D), BF16), bias=((T, T), F32),
    cos=((T, 128), F32), sin=((T, 128), F32), r1=((T, 1), F32),
    gain1=((1, D), F32), gain2=((1, D), F32), gains=((8, D), F32), gains_in=((5, 8, D), F32),
    gd=((4, 512, 384), BF16), ggu=((4, 768, 512), BF16), ga=((4, 768, 384), BF16),
    send0=((SLOTS, 768, 512), BF16),
)
REMOTE = dict(
    recv0=((SLOTS, 768, 512), BF16),
    d1=((4, 2, 128, 384), BF16), gu1=((4, 2, 192, 512), BF16), qa1=((4, 2, 192, 384), BF16),
    d2=((4, 128, 384), BF16), gu2=((4, 192, 512), BF16), qa2=((4, 192, 384), BF16),
    da=((4, 128, 384), BF16), gua=((4, 192, 512), BF16), qaa=((4, 192, 384), BF16),
    db=((4, 128, 384), BF16), gub=((4, 192, 512), BF16), qab=((4, 192, 384), BF16),
)
SEMS = dict(
    lsem=(4,), gsend=(len(PIECES), 7), grecv=(len(PIECES), 7), glocal=(len(PIECES),),
    s0=(2, len(CHUNKS)), s1=(2, len(CHUNKS), 2), s2=(2, len(CHUNKS)), sz=(3, 2, len(CHUNKS)), so=(len(CHUNKS), 3), sg=(2, 5),
)


class Step:
    def __init__(self, refs, comm):
        self.__dict__.update(refs)
        self.comm = comm
        self.copies, self.sent, self.sent0, self.ended = [], [], {}, []
        if comm:
            self.r, self.cc, self.z = lax.axis_index("row"), lax.axis_index("col"), lax.axis_index("dp")
        else:
            self.r = self.cc = self.z = jnp.int32(0)
        self.oc = 1 - self.cc
        r, z = self.r, self.z
        rx = r + 1 - 2 * (r % 2)
        ry = r + 2 - 4 * (r // 2)
        odd = z % 2
        self.rx, self.ry = rx, ry
        first, second = rx + odd * (ry - rx), ry + odd * (rx - ry)
        self.axes = ((first, second), (second, first))
        self.diag = 3 - r
        self.zn = z + 1 - 2 * odd
        self.zm = 3 - z

    def load(self):
        self.copies = []
        for i, (src, dst) in enumerate(((self.x_in, self.x), (self.c_in, self.c))):
            cp = pltpu.make_async_copy(src, dst, self.lsem.at[i])
            cp.start()
            self.copies.append(cp)

    def loaded(self):
        for cp in self.copies:
            cp.wait()
        self.copies = []

    def tables(self):
        block = (self.r * 2 + self.cc) * 4 + self.z
        mine = lax.broadcasted_iota(jnp.int32, (1, self.lens.shape[1]), 1) == block
        lens = [jnp.sum(jnp.where(mine, self.lens[i:i + 1, :], 0), axis=1, keepdims=True) for i in range(3)]
        ends = [lens[0], lens[0] + lens[1], lens[0] + lens[1] + lens[2]]

        def angle_rows(i):
            rows = ds(i * 128, 128)
            place = lax.broadcasted_iota(jnp.int32, (128, 128), 0) + i * 128
            lane = lax.broadcasted_iota(jnp.int32, (1, 128), 1)
            frequency = jnp.exp((lane % HALF).astype(F32) * (-2.0 / HEAD_DIM * math.log(10000.0)))
            start = jnp.zeros((128, 128), jnp.int32)
            for l, e in zip(lens, ends):
                start = start + jnp.where(place >= e, l, 0)
            angle = (place - start).astype(F32) * frequency
            self.cos[rows, :] = jnp.cos(angle)
            self.sin[rows, :] = jnp.sin(angle) * jnp.where(lane % HEAD_DIM < HALF, -1.0, 1.0)
        loop(4, angle_rows)
        self.gain1[...] = self.gain1_in[...].reshape(1, D)
        self.gain2[...] = self.gain2_in[...].reshape(1, D)

        def bias_rows(i):
            rows = ds(i * 128, 128)
            place = lax.broadcasted_iota(jnp.int32, (128, T), 0) + i * 128
            key = lax.broadcasted_iota(jnp.int32, (128, T), 1)
            seg_q = jnp.zeros((128, T), jnp.int32)
            seg_k = jnp.zeros((128, T), jnp.int32)
            for e in ends:
                seg_q = seg_q + jnp.where(place >= e, 1, 0)
                seg_k = seg_k + jnp.where(key >= e, 1, 0)
            ok = (seg_q == seg_k) & (place >= key)
            self.bias[rows, :] = jnp.where(ok, 0.0, MASKED)
        loop(4, bias_rows)

    def transpose_x(self):
        def step(i):
            cols = ds(i * 128, 128)
            self.xt[cols, :] = self.x[:, cols].T
        loop(6, step)

    def turn(self, t, sign):
        lane = lax.broadcasted_iota(jnp.int32, t.shape, 1)
        front = lane % HEAD_DIM < HALF
        partner = jnp.where(front, pltpu.roll(t, 128 - HALF, 1), pltpu.roll(t, HALF, 1))
        return t * self.cos[...] + partner * (self.sin[...] * sign)

    def project(self, name):
        out = getattr(self, name)
        t = dot(self.x[...], getattr(self, "w" + name)[...])
        for i in range(PAIRS):
            s = t[:, i * 128:(i + 1) * 128]
            if name != "v":
                s = self.turn(s, 1.0)
            if name == "q":
                s = s * HEAD_DIM ** -0.5
            out[:, i * 128:(i + 1) * 128] = s.astype(BF16)

    def halves(self, two):
        first = lax.broadcasted_iota(jnp.int32, two.shape, 1) < HEAD_DIM
        none = jnp.zeros_like(two)
        return jnp.where(first, two, none), jnp.where(first, none, two)

    def attend(self, hp):
        lanes = ds(hp * 128, 128)
        q, k2, v = self.halves(self.q[:, lanes]), self.k[:, lanes], self.halves(self.v[:, lanes])
        for qb in range(2):
            keys = (qb + 1) * 256
            rows = slice(qb * 256, qb * 256 + 256)
            both = []
            for j in range(2):
                s = dot_nt(q[j][rows], k2[:keys]) + self.bias[rows, :keys]
                e = jnp.exp(s - jnp.max(s, axis=-1, keepdims=True))
                p = (e * (1.0 / jnp.sum(e, axis=-1, keepdims=True))).astype(BF16)
                (self.p1 if qb else self.p0)[2 * hp + j] = p
                both.append(p)
            o = dot(jnp.concatenate(both, axis=1), jnp.concatenate([v[0][:keys], v[1][:keys]], axis=0)).astype(BF16)
            self.attn[rows, lanes] = o
            self.attnt[lanes, rows] = o.T

    def norm_one(self):
        def step(i):
            rows = ds(i * 256, 256)
            h = self.x[rows, :].astype(F32) + dot(self.attn[rows, :], self.wo[...])
            r = lax.rsqrt(jnp.mean(h * h, axis=-1, keepdims=True) + EPS)
            n = h * r
            self.n1[rows, :] = n
            self.r1[rows, :] = r
            y = (n * self.gain1[...]).astype(BF16)
            self.y1[rows, :] = y
            self.y1t[:, rows] = y.T
        loop(2, step)

    def ffn(self, quarter):
        at = (quarter % 2) * 1024 + (quarter // 2) * 512
        cols = slice(at, at + 512)
        for i in range(2):
            rows = slice(i * 256, (i + 1) * 256)
            g = dot(self.y1[rows, :], self.wg[:, cols])
            u = dot(self.y1[rows, :], self.wu[:, cols])
            s = jax.nn.sigmoid(g)
            gs = g * s
            h = (gs * u).astype(BF16)
            self.hid[rows, cols] = h
            self.hidt[cols, rows] = h.T
            self.b[rows, cols] = gs.astype(BF16)
            self.a[rows, cols] = (u * s * (1.0 + g * (1.0 - s))).astype(BF16)

    def down(self, part):
        last = part == 3

        def step(i):
            rows = slice(i * 256, (i + 1) * 256)
            left = jnp.concatenate([self.hid[rows, s * 512 + part * 128:s * 512 + part * 128 + 128] for s in range(4)], axis=1)
            right = jnp.concatenate([self.wd[s * 512 + part * 128:s * 512 + part * 128 + 128, :] for s in range(4)], axis=0)
            t = dot(left, right)
            if part == 0:
                self.h2[rows, :] = self.n1[rows, :] * self.gain1[...] + t
                return
            h = self.h2[rows, :] + t
            if not last:
                self.h2[rows, :] = h
                return
            r = lax.rsqrt(jnp.mean(h * h, axis=-1, keepdims=True) + EPS)
            n = h * r
            c = self.c[rows, :].astype(F32)
            self.c[rows, :] = (n * self.gain2[...]).astype(BF16)
            self.gains[1:2, :] += jnp.sum(c * n, axis=0, keepdims=True)
            g = c * self.gain2[...]
            dh = r * (g - n * jnp.mean(g * n, axis=-1, keepdims=True))
            self.h2[rows, :] = dh
            self.dffn[rows, :] = dh.astype(BF16)
        if part == 0:
            self.gains[...] = jnp.zeros_like(self.gains)
        step(0)
        step(1)
        if last:
            cp = pltpu.make_async_copy(self.c, self.layer_out, self.lsem.at[2])
            cp.start()
            self.copies.append(cp)

    def dhidden(self, half):
        for i in (2 * half, 2 * half + 1):
            cols = slice(i * 512, (i + 1) * 512)
            t = dot_nt(self.dffn[...], self.wd[cols, :])
            self.a[:, cols] = (t * self.a[:, cols].astype(F32)).astype(BF16)
            self.b[:, cols] = (t * self.b[:, cols].astype(F32)).astype(BF16)

    def back_one(self, half):
        rows = ds(half * 256, 256)
        dy = self.h2[rows, :] + dot_nt(self.a[rows, :], self.wg[...]) + dot_nt(self.b[rows, :], self.wu[...])
        n = self.n1[rows, :]
        self.gains[0:1, :] += jnp.sum(dy * n, axis=0, keepdims=True)
        g = dy * self.gain1[...]
        dh = self.r1[rows, :] * (g - n * jnp.mean(g * n, axis=-1, keepdims=True))
        self.h2[rows, :] = dh
        self.dffn[rows, :] = dh.astype(BF16)

    def dattn(self):
        self.x[...] = dot_nt(self.dffn[...], self.wo[...]).astype(BF16)

    def attend_back(self, hp):
        lanes = ds(hp * 128, 128)
        v2 = self.v[:, lanes]
        q, k, do = self.halves(self.q[:, lanes]), self.halves(self.k[:, lanes]), self.halves(self.x[:, lanes])
        dq, s, p = [], [], []
        for qb in range(2):
            keys = (qb + 1) * 256
            rows = slice(qb * 256, qb * 256 + 256)
            low = [(self.p1 if qb else self.p0)[2 * hp + j] for j in range(2)]
            ds_low = []
            for j in range(2):
                wide = low[j].astype(F32)
                dp = dot_nt(do[j][rows], v2[:keys])
                ds_low.append((wide * (dp - jnp.sum(wide * dp, axis=-1, keepdims=True))).astype(BF16))
            dq.append(dot(jnp.concatenate(ds_low, axis=1), jnp.concatenate([k[0][:keys], k[1][:keys]], axis=0)))
            s.append(ds_low)
            p.append(low)

        def over_queries(of, rows):
            first = dot_tn(jnp.concatenate([*of[0], of[1][0][:, :256], of[1][1][:, :256]], axis=0),
                           jnp.concatenate([rows[0][:256], rows[1][:256], rows[0][256:], rows[1][256:]], axis=0))
            second = dot_tn(jnp.concatenate([of[1][0][:, 256:], of[1][1][:, 256:]], axis=0),
                            jnp.concatenate([rows[0][256:], rows[1][256:]], axis=0))
            return jnp.concatenate([first, second], axis=0)
        dk, dv = over_queries(s, q), over_queries(p, do)
        self.q[:, lanes] = self.turn(jnp.concatenate(dq, axis=0) * HEAD_DIM ** -0.5, -1.0).astype(BF16)
        self.k[:, lanes] = self.turn(dk, -1.0).astype(BF16)
        self.v[:, lanes] = dv.astype(BF16)

    def input_grad(self):
        self.h2[...] += dot_nt(self.q[...], self.wq[...]) + dot_nt(self.k[...], self.wk[...]) + dot_nt(self.v[...], self.wv[...])
        cp = pltpu.make_async_copy(self.h2, self.dx, self.lsem.at[3])
        cp.start()
        self.copies.append(cp)

    def pick(self, n, d, gu, qa):
        j = int(n[1:] or 0)
        if n[0] == "D":
            return d.at[j]
        if n[0] in "GU":
            return gu.at[2 * j + (n[0] == "U")]
        if n[0] == "B":
            rows = qa.shape[-2] // 2
            return qa.at[(2, *[slice(None)] * (len(qa.shape) - 3), slice(j * rows, (j + 1) * rows))]
        return qa.at[3 if n[0] == "O" else j]

    def own(self, n):
        return self.pick(n, self.gd, self.ggu, self.ga)

    def out0(self, n):
        rows, cols = SHAPE[n]
        return self.send0.at[CHUNKS.index(n) % SLOTS, 0:4 * rows, 0:cols]

    def grad(self, n):
        own, other = self.own(n), self.out0(n)
        c0 = self.cc == 0

        def both(t):
            lo, hi = t[:, :384], t[:, 384:]
            own[...] = jnp.where(c0, lo, hi).astype(BF16)
            other[...] = jnp.where(c0, hi, lo).astype(BF16)
        j = int(n[1:] or 0)
        if n[0] == "D":
            both(dot(jnp.concatenate([self.hidt[s * 512 + j * 128:s * 512 + j * 128 + 128, :] for s in range(4)], axis=0), self.dffn[...]))
        elif n[0] == "O":
            both(dot(self.attnt[...], self.dffn[...]))
        elif n[0] in "GU":
            src = self.a if n[0] == "G" else self.b
            for half, dst in ((self.oc, other), (self.cc, own)):
                dst[...] = dot(self.y1t[...], src[:, ds(half * 1024 + j * 512, 512)]).astype(BF16)
        else:
            right = []
            for half in (self.oc, self.cc):
                lanes = ds((half * 3 + (2 if n[0] == "B" else j)) * 128, 128)
                right += [self.q[:, lanes], self.k[:, lanes], self.v[:, lanes]]
            left = self.xt[...]
            if n[0] == "B":
                left = jnp.concatenate([self.xt[s * 192 + j * 96:s * 192 + j * 96 + 96, :] for s in range(4)], axis=0)
            t = dot(left, jnp.concatenate(right, axis=1)).astype(BF16)
            other[...] = t[:, :384]
            own[...] = t[:, 384:]

    def remote(self, src, dst, send, recv, **where):
        cp = pltpu.make_async_remote_copy(src_ref=src, dst_ref=dst, send_sem=send, recv_sem=recv, device_id=where, device_id_type=MESH)
        return cp

    def begin(self, cp, sent):
        cp.start()
        sent.append(cp)

    def enter(self):
        barrier = pltpu.get_barrier_semaphore()
        for where in ({"col": self.oc}, {"row": self.rx}, {"row": self.ry}, {"dp": self.zn}, {"dp": self.zm}):
            pl.semaphore_signal(barrier, inc=1, device_id=where, device_id_type=MESH)
        pl.semaphore_wait(barrier, 5)

    def region(self, i, row, core):
        n, r0, nr, c0, nc = PIECES[i]
        rows, cols = SHARD[n]
        return getattr(self, "w" + n).at[ds(row * rows + r0, nr, 64), ds(core * cols + c0, nc, 128)]

    def shard(self, i):
        n, r0, nr, c0, nc = PIECES[i]
        return getattr(self, "h" + n).at[r0:r0 + nr, c0:c0 + nc]

    def gather(self, i, what):
        a, b = self.axes[i % 2]
        row = (self.r, a, a, self.r, a, self.diag, b)[what]
        where = ({"row": a}, {"row": b}, {"dp": self.zn}, *[{"col": self.oc}] * 4)[what]
        src = self.shard(i) if what in (0, 3) else self.region(i, row, self.cc)
        return self.remote(src, self.region(i, row, self.cc), self.gsend.at[i, what], self.grecv.at[i, what], **where)

    def go(self, i, *whats):
        for what in whats:
            self.begin(self.gather(i, what), self.sent)

    def push(self, i):
        self.go(i, 0)

    def share(self, i):
        self.go(i, 3)
        pltpu.make_async_copy(self.shard(i), self.region(i, self.r, self.cc), self.glocal.at[i]).start()

    def relay(self, i):
        self.gather(i, 0).wait_recv()
        self.go(i, 1, 2, 4)

    def relay_two(self, i):
        self.gather(i, 1).wait_recv()
        self.go(i, 5)
        self.gather(i, 2).wait_recv()
        self.go(i, 6)

    def ready(self, i):
        pltpu.make_async_copy(self.shard(i), self.region(i, self.r, self.cc), self.glocal.at[i]).wait()
        for what in (3, 4, 5, 6):
            self.gather(i, what).wait_recv()

    def part(self, kind, n):
        d, gu, qa = {"1": (self.d1, self.gu1, self.qa1), "2": (self.d2, self.gu2, self.qa2), "a": (self.da, self.gua, self.qaa),
                     "b": (self.db, self.gub, self.qab)}[kind]
        return self.pick(n, d, gu, qa)

    def chunk(self, n):
        k = CHUNKS.index(n)
        rows, cols = SHAPE[n]
        if n in SPREAD:
            ra, rb = self.axes[k % 2]
        else:
            ra, rb = (self.rx, self.ry) if k % 2 == 0 else (self.ry, self.rx)
        block = lambda row: ds(row * rows, rows)
        return k, rows, cols, ra, rb, block

    def copy0(self, n):
        k, rows, cols, *_ = self.chunk(n)
        at = (k % SLOTS, slice(0, 4 * rows), slice(0, cols))
        return self.remote(self.send0.at[at], self.recv0.at[at], self.s0.at[0, k], self.s0.at[1, k], col=self.oc)

    def copy1(self, n, which):
        k, rows, cols, ra, rb, block = self.chunk(n)
        if n in SPREAD:
            row, where = ((rb, {"dp": self.zn}), (self.diag, {"row": rb}))[which]
        else:
            row, where = (ra, self.diag)[which], {"row": ra}
        return self.remote(self.own(n).at[block(row), :], self.part("1", n).at[which], self.s1.at[0, k, which], self.s1.at[1, k, which], **where)

    def copy2(self, n):
        k, rows, cols, ra, rb, block = self.chunk(n)
        row = ra if n in SPREAD else rb
        return self.remote(self.own(n).at[block(row), :], self.part("2", n), self.s2.at[0, k], self.s2.at[1, k], row=row)

    def copy_z(self, n, leg):
        k, rows, cols, ra, rb, block = self.chunk(n)
        src = self.part("2", n) if leg == 2 else self.own(n).at[block(self.r), :]
        dst = self.part("b" if leg == 1 else "a", n)
        return self.remote(src, dst, self.sz.at[leg, 0, k], self.sz.at[leg, 1, k], dp=self.zm if leg == 1 else self.zn)

    def inner(self):
        return ((self.z + 1) // 2) % 2 == 1

    def outer(self):
        return ((self.z + 1) // 2) % 2 == 0

    def add(self, ref, other):
        ref[...] = (ref[...].astype(F32) + other[...].astype(F32)).astype(BF16)

    def make(self, n):
        k = CHUNKS.index(n)
        if k >= SLOTS:
            self.sent0[k - SLOTS].wait_send()
            self.sent = [cp for cp in self.sent if cp is not self.sent0[k - SLOTS]]
        self.grad(n)
        if k >= SLOTS:
            pl.semaphore_wait(self.credit.at[k % SLOTS], 1)
        self.begin(self.copy0(n), self.sent)
        self.sent0[k] = self.sent[-1]

    def sum0(self, n):
        k, rows, cols, ra, rb, block = self.chunk(n)
        self.copy0(n).wait_recv()
        own = self.own(n)
        got = self.recv0.at[k % SLOTS, 0:4 * rows, 0:cols]
        for row, which in ((self.diag, 1), (rb, 0), (ra, None), (self.r, None)) if n in SPREAD else ((self.diag, 1), (ra, 0), (rb, None), (self.r, None)):
            self.add(own.at[block(row), :], got.at[block(row), :])
            if which is not None:
                self.begin(self.copy1(n, which), self.sent)
        if k + SLOTS < len(CHUNKS):
            pl.semaphore_signal(self.credit.at[k % SLOTS], inc=1, device_id={"col": self.oc}, device_id_type=MESH)

    def sum1(self, n):
        k, rows, cols, ra, rb, block = self.chunk(n)
        self.copy1(n, 1).wait_recv()
        self.add(self.own(n).at[block(ra if n in SPREAD else rb), :], self.part("1", n).at[1])
        if n in SPREAD:
            self.copy1(n, 0).wait_recv()
            self.add(self.own(n).at[block(ra), :], self.part("1", n).at[0])
        self.begin(self.copy2(n), self.sent)

    def sum2(self, n):
        k, rows, cols, ra, rb, block = self.chunk(n)
        own = self.own(n).at[block(self.r), :]
        if n not in SPREAD:
            self.copy1(n, 0).wait_recv()
            self.add(own, self.part("1", n).at[0])
        self.copy2(n).wait_recv()
        self.add(own, self.part("2", n))

        @pl.when(self.outer())
        def _():
            self.copy_z(n, 0).start()

    def sum_z1(self, n):
        k, rows, cols, ra, rb, block = self.chunk(n)

        @pl.when(self.inner())
        def _():
            self.copy_z(n, 0).wait_recv()
            self.add(self.own(n).at[block(self.r), :], self.part("a", n))
            self.copy_z(n, 1).start()

    def sum_z2(self, n):
        k, rows, cols, ra, rb, block = self.chunk(n)

        @pl.when(self.inner())
        def _():
            self.copy_z(n, 1).wait_recv()
            total = self.part("2", n)
            own = self.own(n).at[block(self.r), :]
            total[...] = (own[...].astype(F32) + self.part("b", n)[...].astype(F32)).astype(BF16)
            self.copy_z(n, 2).start()
            for cp in self.results(n, total):
                cp.start()

    def sum_z3(self, n):
        self.ended.append(n)

        @pl.when(self.outer())
        def _():
            self.copy_z(n, 2).wait_recv()
            for cp in self.results(n, self.part("a", n)):
                cp.start()

    def results(self, n, src):
        k = CHUNKS.index(n)
        j = int(n[1:] or 0)
        if n[0] in "AB":
            rows, j = (slice(j * 96, j * 96 + 96), 2) if n[0] == "B" else (slice(0, 192), j)
            return [pltpu.make_async_copy(src.at[:, i * 128:(i + 1) * 128], getattr(self, "out_" + m).at[rows, j * 128:(j + 1) * 128], self.so.at[k, i])
                    for i, m in enumerate("qkv")]
        out = getattr(self, "out_" + n[0].lower())
        dst = {"D": lambda: out.at[j * 128:(j + 1) * 128, :], "G": lambda: out.at[:, j * 512:(j + 1) * 512],
               "U": lambda: out.at[:, j * 512:(j + 1) * 512], "O": lambda: out}[n[0]]()
        return [pltpu.make_async_copy(src, dst, self.so.at[k, 0])]

    def gains_copy(self, t):
        where = ({"col": self.oc}, {"row": self.rx}, {"row": self.ry}, {"dp": self.zn}, {"dp": self.zm})[t]
        return self.remote(self.gains, self.gains_in.at[t], self.sg.at[0, t], self.sg.at[1, t], **where)

    def gains_send(self, t):
        self.gains_copy(t).start()

    def gains_add(self, t):
        self.gains_copy(t).wait()
        self.gains[...] += self.gains_in[t]

    def settle(self):
        slots = [cp for cp in self.sent if any(cp is s for s in self.sent0.values())]
        for cp in self.sent:
            if not any(cp is s for s in slots):
                cp.wait_send()
        self.sent = slots

    def finish(self):
        for cp in self.sent:
            cp.wait_send()
        for inner, legs, kind in ((self.outer(), (0,), "a"), (self.inner(), (1, 2), "2")):
            @pl.when(inner)
            def _():
                for n in self.ended:
                    for leg in legs:
                        self.copy_z(n, leg).wait_send()
                    for cp in self.results(n, self.part(kind, n)):
                        cp.wait()
        for cp in self.copies:
            cp.wait()


D0, D1, D2, D3, G0, U0, G1, U1, O, A0, A1, B0, B1 = CHUNKS


def order(s):
    s.load(); s.push(0); s.push(1); s.share(12); s.share(5); s.share(6); s.push(2); s.push(3); s.push(4); s.relay(0); s.share(0); s.relay(1); s.relay(2); s.relay(3)
    s.push(5); s.push(6); s.share(2); s.share(3); s.share(4); s.relay_two(0); s.relay(4); s.share(8); s.relay_two(1); s.push(7); s.share(1); s.push(8); s.relay_two(2); s.tables()
    s.share(9); s.ready(1); s.loaded(); s.transpose_x(); s.ready(0); s.push(9); s.relay(5); s.share(10); s.share(11); s.relay_two(3); s.relay_two(4); s.relay(6); s.ready(3); s.project('k')
    s.ready(2); s.push(10); s.project('q'); s.ready(4); s.relay(7); s.share(13); s.project('v'); s.attend(0); s.share(7); s.attend(1); s.relay(8); s.push(11); s.attend(2); s.attend(3)
    s.relay(9); s.relay_two(5); s.relay_two(6); s.push(12); s.relay(10); s.attend(4); s.push(13); s.relay_two(7); s.ready(6); s.attend(5); s.ready(5); s.norm_one(); s.ready(7); s.relay_two(8)
    s.ffn(0); s.relay(11); s.relay_two(9); s.ready(8); s.ffn(1); s.relay(12); s.relay_two(10); s.ready(9); s.ffn(2); s.relay(13); s.relay_two(11); s.ffn(3); s.relay_two(12); s.ready(11)
    s.ready(10); s.down(0); s.down(1); s.relay_two(13); s.ready(12); s.down(2); s.ready(13); s.down(3); s.make(D0); s.make(D1); s.make(D2); s.sum0(D0); s.make(D3); s.sum0(D1)
    s.dhidden(0); s.dhidden(1); s.sum0(D2); s.sum0(D3); s.make(G0); s.make(U0); s.sum1(D0); s.sum1(D1); s.make(G1); s.sum0(G0); s.sum1(D2); s.sum0(U0); s.make(U1); s.back_one(0)
    s.sum1(D3); s.back_one(1); s.sum1(G0); s.sum0(U1); s.sum0(G1); s.sum2(D1); s.dattn(); s.gains_send(0); s.sum2(D2); s.attend_back(4); s.attend_back(3); s.sum2(D0); s.sum_z1(D1); s.sum2(D3)
    s.sum2(G0); s.attend_back(1); s.sum_z1(D2); s.sum1(U0); s.make(O); s.gains_add(0); s.attend_back(0); s.sum1(G1); s.sum_z1(D0); s.make(A0); s.sum1(U1); s.sum_z1(D3); s.sum_z2(D2); s.make(A1)
    s.sum2(U0); s.gains_send(1); s.sum0(A0); s.sum_z2(D0); s.sum_z1(G0); s.sum0(A1); s.sum_z2(D3); s.sum_z2(D1); s.sum2(U1); s.attend_back(2); s.sum_z1(U0); s.sum2(G1); s.gains_add(1); s.sum_z2(G0)
    s.gains_send(2); s.sum1(A0); s.sum_z3(D3); s.sum1(A1); s.attend_back(5); s.sum_z1(U1); s.gains_add(2); s.gains_send(3); s.sum0(O); s.make(B0); s.sum_z2(U0); s.sum0(B0); s.sum2(A1); s.sum_z1(G1)
    s.sum_z3(D1); s.sum_z3(D0); s.make(B1); s.settle(); s.sum2(A0); s.gains_add(3); s.sum_z2(U1); s.sum1(B0); s.sum1(O); s.sum_z1(A1); s.sum0(B1); s.sum_z3(D2); s.sum_z2(G1); s.sum2(B0)
    s.sum2(O); s.sum_z1(A0); s.sum_z2(A1); s.sum_z1(B0); s.sum1(B1); s.sum_z3(U0); s.sum_z2(A0); s.sum_z1(O); s.sum2(B1); s.sum_z2(B0); s.input_grad(); s.gains_send(4); s.sum_z1(B1); s.sum_z2(O)
    s.sum_z2(B1); s.sum_z3(U1); s.sum_z3(O); s.sum_z3(A0); s.gains_add(4); s.sum_z3(G0); s.sum_z3(G1); s.sum_z3(A1); s.sum_z3(B0); s.sum_z3(B1)


OUTS = ("layer_out", "dx", "out_q", "out_k", "out_v", "out_o", "out_g", "out_u", "out_d", "gains_out")
INS = ("x_in", "c_in", "lens", "hq", "hk", "hv", "ho", "hg", "hu", "hd", "gain1_in", "gain2_in")


def step_kernel(*refs):
    names = INS + OUTS + tuple(SCRATCH) + tuple(REMOTE) + tuple(SEMS) + ("credit",)
    s = Step(dict(zip(names, refs, strict=True)), True)
    s.enter()
    order(s)
    s.gains_out[...] = s.gains[...]
    s.finish()


def widen_kernel(*refs):
    ins, outs, low, wide, sems = refs[:10], refs[10:21], refs[21:30], refs[30:37], refs[37]
    wide = [*low[:2], *wide]
    loads = [pltpu.make_async_copy(ins[i], low[i], sems.at[0, i]) for i in range(9)]
    stores = [pltpu.make_async_copy(wide[i], outs[i], sems.at[1, i]) for i in range(9)]
    for cp in loads:
        cp.start()
    outs[9][...] = ins[9][0, :]
    outs[10][...] = ins[9][1, :]
    for i in range(9):
        loads[i].wait()
        if i > 1:
            wide[i][...] = low[i][...].astype(F32)
        stores[i].start()
    for cp in stores:
        cp.wait()


def fused_body(x, c, lens, wq, wk, wv, wo, wg, wu, wd, gain1, gain2):
    hbm, vmem = pl.BlockSpec(memory_space=pl.ANY), pl.BlockSpec(memory_space=pltpu.VMEM)
    struct = jax.ShapeDtypeStruct
    shards = [SHARD[n] for n in NAMES]
    out = pl.pallas_call(
        step_kernel,
        out_shape=[struct((T, D), BF16), struct((T, D), F32), *[struct(s, BF16) for s in shards], struct((8, D), F32)],
        in_specs=[hbm, hbm, vmem, *[hbm] * 7, vmem, vmem],
        out_specs=[*[hbm] * 9, vmem],
        scratch_shapes=[*[pltpu.VMEM(*v) for v in (SCRATCH | REMOTE).values()], *[pltpu.SemaphoreType.DMA(v) for v in SEMS.values()],
                        pltpu.SemaphoreType.REGULAR((SLOTS,))],
        compiler_params=pltpu.CompilerParams(collective_id=0, has_side_effects=True, vmem_limit_bytes=63 << 20),
        name="step",
    )(x, c, lens.T, wq, wk, wv, wo, wg, wu, wd, gain1, gain2)
    return pl.pallas_call(
        widen_kernel,
        out_shape=[struct((T, D), BF16), struct((T, D), F32), *[struct(s, F32) for s in shards], struct((D,), F32), struct((D,), F32)],
        in_specs=[*[hbm] * 9, vmem],
        out_specs=[*[hbm] * 9, vmem, vmem],
        scratch_shapes=[pltpu.VMEM((T, D), BF16), pltpu.VMEM((T, D), F32), *[pltpu.VMEM(s, BF16) for s in shards],
                        *[pltpu.VMEM(s, F32) for s in shards], pltpu.SemaphoreType.DMA((2, 9))],
        compiler_params=pltpu.CompilerParams(vmem_limit_bytes=63 << 20),
        name="widen",
    )(*out)


def pack_info(lengths_row, places_count):
    places = jnp.arange(places_count, dtype=jnp.int32)
    segment = jnp.zeros((places_count,), jnp.int32)
    start = jnp.zeros((places_count,), jnp.int32)
    end = jnp.int32(0)
    for i in range(lengths_row.shape[0]):
        end = end + lengths_row[i]
        passed = (places >= end).astype(jnp.int32)
        segment = segment + passed
        start = start + passed * lengths_row[i]
    return segment, (places - start).astype(F32)


def angles(positions):
    frequency = 10000.0 ** (-jnp.arange(HALF, dtype=F32) * (2.0 / HEAD_DIM))
    turned = positions[..., None] * frequency
    return jnp.cos(turned), jnp.sin(turned)


def rotate(values, cosine, sine):
    a, b = values[..., :HALF], values[..., HALF:]
    return jnp.concatenate([a * cosine - b * sine, b * cosine + a * sine], axis=-1)


def norm_forward(resid):
    inverse = lax.rsqrt(jnp.mean(resid * resid, axis=-1, keepdims=True) + EPS)
    return resid * inverse, inverse


def norm_backward(grad, normed, inverse):
    return inverse * (grad - normed * jnp.mean(grad * normed, axis=-1, keepdims=True))


def heads_first(matrix):
    t, w = matrix.shape
    return matrix.reshape(t, w // HEAD_DIM, HEAD_DIM).transpose(1, 0, 2)


def heads_last(stacked):
    h, t, w = stacked.shape
    return stacked.transpose(1, 0, 2).reshape(t, h * w)


def block_local(x, c, lengths, wq, wk, wv, wo, wg, wu, wd, gain1, gain2):
    t = x.shape[0]
    segment, positions = pack_info(lengths, t)
    cosine, sine = angles(positions)
    places = jnp.arange(t, dtype=jnp.int32)
    mask = (segment[:, None] == segment[None, :]) & (places[:, None] >= places[None, :])
    scale = HEAD_DIM ** (-0.5)
    q = rotate(heads_first(dot(x, wq)), cosine, sine).astype(BF16)
    k = rotate(heads_first(dot(x, wk)), cosine, sine).astype(BF16)
    v = heads_first(dot(x, wv).astype(BF16))
    bmm = lambda e, a, b: jnp.einsum(e, a, b, preferred_element_type=F32)
    s = jnp.where(mask, bmm("htd,hsd->hts", q, k) * scale, MASKED)
    e = jnp.exp(s - jnp.max(s, axis=-1, keepdims=True))
    probs = e / jnp.sum(e, axis=-1, keepdims=True)
    low = probs.astype(BF16)
    attn = heads_last(bmm("hts,hsd->htd", low, v).astype(BF16))
    n1, r1 = norm_forward(x.astype(F32) + dot(attn, wo))
    y1 = n1 * gain1
    y1_low = y1.astype(BF16)
    gate, up = dot(y1_low, wg), dot(y1_low, wu)
    sig = jax.nn.sigmoid(gate)
    hidden = (gate * sig * up).astype(BF16)
    n2, r2 = norm_forward(y1 + dot(hidden, wd))
    layer_out = (n2 * gain2).astype(BF16)
    cf = c.astype(F32)
    gain2_grad = jnp.sum(cf * n2, axis=0)
    dh2 = norm_backward(cf * gain2, n2, r2)
    dffn = dh2.astype(BF16)
    d_down = dot_tn(hidden, dffn)
    dhidden = dot_nt(dffn, wd)
    dgate = (dhidden * up * sig * (1.0 + gate * (1.0 - sig))).astype(BF16)
    dup = (dhidden * gate * sig).astype(BF16)
    d_gate, d_up = dot_tn(y1_low, dgate), dot_tn(y1_low, dup)
    dy1 = dh2 + dot_nt(dgate, wg) + dot_nt(dup, wu)
    gain1_grad = jnp.sum(dy1 * n1, axis=0)
    dh1 = norm_backward(dy1 * gain1, n1, r1)
    dbranch = dh1.astype(BF16)
    d_out = dot_tn(attn, dbranch)
    dattn = heads_first(dot_nt(dbranch, wo).astype(BF16))
    dprobs = bmm("htd,hsd->hts", dattn, v)
    dscores = (probs * (dprobs - jnp.sum(probs * dprobs, axis=-1, keepdims=True)) * scale).astype(BF16)
    dq = heads_last(rotate(bmm("hts,hsd->htd", dscores, k), cosine, -sine)).astype(BF16)
    dk = heads_last(rotate(bmm("hts,htd->hsd", dscores, q), cosine, -sine)).astype(BF16)
    dv = heads_last(bmm("hts,htd->hsd", low, dattn)).astype(BF16)
    d_q, d_k, d_v = dot_tn(x, dq), dot_tn(x, dk), dot_tn(x, dv)
    dx = dh1 + dot_nt(dq, wq) + dot_nt(dk, wk) + dot_nt(dv, wv)
    return layer_out, dx, (d_q, d_k, d_v, d_out, d_gate, d_up, d_down), gain1_grad, gain2_grad


def body(x, c, seq_lengths, wq, wk, wv, wo, wg, wu, wd, gain1, gain2):
    block = (lax.axis_index("row") * lax.axis_size("col") + lax.axis_index("col")) * lax.axis_size("dp") + lax.axis_index("dp")
    lengths = lax.dynamic_index_in_dim(seq_lengths, block, keepdims=False)
    full = [
        lax.all_gather(lax.all_gather(w, "col", axis=1, tiled=True), "row", axis=0, tiled=True)
        for w in (wq, wk, wv, wo, wg, wu, wd)
    ]
    layer_out, dx, grads, g1, g2 = block_local(x, c, lengths, *full, gain1, gain2)
    summed = []
    for g in grads:
        g = lax.psum_scatter(g.astype(BF16), "col", scatter_dimension=1, tiled=True)
        g = lax.psum_scatter(g, "row", scatter_dimension=0, tiled=True)
        summed.append(lax.psum(g, "dp").astype(F32))
    g1, g2 = lax.psum((g1, g2), ("row", "col", "dp"))
    return (layer_out, dx, *summed, g1, g2)


def solution(mesh):
    tok = P(("row", "col", "dp"), None)
    mat = P("row", "col")
    fits = tuple(mesh.shape[a] for a in ("row", "col", "dp")) == (4, 2, 4)
    return jax.shard_map(
        fused_body if fits else body, mesh=mesh, in_specs=(tok, tok, P(), *[mat] * 7, P(), P()),
        out_specs=(tok, tok, *[mat] * 7, P(), P()), check_vma=False,
    )
```

```python
import math

import jax
import jax.numpy as jnp
from jax import lax
from jax.experimental import pallas as pl
from jax.experimental.pallas import tpu as pltpu
from jax.sharding import PartitionSpec as P

MESH = pl.DeviceIdType.MESH

HEAD_DIM = 64
HALF = HEAD_DIM // 2
EPS = 1e-06
MASKED = -1e30
BF16 = jnp.bfloat16
F32 = jnp.float32

T, D, FF, HEADS = 512, 768, 2048, 12
PAIRS = HEADS // 2
NAMES = ("q", "k", "v", "o", "g", "u", "d")
SHARD = {"q": (192, 384), "k": (192, 384), "v": (192, 384), "o": (192, 384), "g": (192, 1024), "u": (192, 1024), "d": (512, 384)}
PIECES = (
    ("q", 0, 64, 0, 384), ("q", 64, 64, 0, 384), ("q", 128, 64, 0, 384), ("k", 0, 192, 0, 384), ("v", 0, 192, 0, 384), ("o", 0, 192, 0, 384),
    ("g", 0, 192, 0, 512), ("u", 0, 192, 0, 512), ("g", 0, 192, 512, 512), ("u", 0, 192, 512, 512),
    ("d", 0, 128, 0, 384), ("d", 128, 128, 0, 384), ("d", 256, 128, 0, 384), ("d", 384, 128, 0, 384),
)
CHUNKS = ("D0", "D1", "D2", "D3", "G0", "U0", "G1", "U1", "O", "A0", "A1", "B0", "B1")
SHAPE = {n: {"D": (128, 384), "G": (192, 512), "U": (192, 512), "O": (192, 384), "A": (192, 384), "B": (96, 384)}[n[0]] for n in CHUNKS}
SPREAD = ("D0", "D1", "D2", "D3", "G0", "U0")
SLOTS = 2


def dot(a, b):
    return jnp.dot(a, b, preferred_element_type=F32)


def dot_nt(a, b):
    return lax.dot_general(a, b, (((1,), (1,)), ((), ())), preferred_element_type=F32)


def dot_tn(a, b):
    return lax.dot_general(a, b, (((0,), (0,)), ((), ())), preferred_element_type=F32)


def ds(start, size, multiple=None):
    if isinstance(start, int):
        return pl.ds(start, size)
    return pl.ds(pl.multiple_of(start, multiple or size), size)


def loop(n, f, start=0):
    def step(i, carry):
        f(i)
        return carry
    lax.fori_loop(start, n, step, 0)


SCRATCH = dict(
    wq=((D, D), BF16), wk=((D, D), BF16), wv=((D, D), BF16), wo=((D, D), BF16),
    wg=((D, FF), BF16), wu=((D, FF), BF16), wd=((FF, D), BF16),
    x=((T, D), BF16), xt=((D, T), BF16), c=((T, D), BF16),
    q=((T, D), BF16), k=((T, D), BF16), v=((T, D), BF16),
    p0=((HEADS, 256, 256), BF16), p1=((HEADS, 256, 512), BF16),
    attn=((T, D), BF16), attnt=((D, T), BF16),
    n1=((T, D), F32), y1=((T, D), BF16), y1t=((D, T), BF16),
    a=((T, FF), BF16), b=((T, FF), BF16), hid=((T, FF), BF16), hidt=((FF, T), BF16),
    h2=((T, D), F32), dffn=((T, D), BF16), bias=((T, T), F32),
    cos=((T, 128), F32), sin=((T, 128), F32), r1=((T, 1), F32),
    gain1=((1, D), F32), gain2=((1, D), F32), gains=((8, D), F32), gains_in=((5, 8, D), F32),
    gd=((4, 512, 384), BF16), ggu=((4, 768, 512), BF16), ga=((4, 768, 384), BF16),
    send0=((SLOTS, 768, 512), BF16),
)
REMOTE = dict(
    recv0=((SLOTS, 768, 512), BF16),
    d1=((4, 2, 128, 384), BF16), gu1=((4, 2, 192, 512), BF16), qa1=((4, 2, 192, 384), BF16),
    d2=((4, 128, 384), BF16), gu2=((4, 192, 512), BF16), qa2=((4, 192, 384), BF16),
    da=((4, 128, 384), BF16), gua=((4, 192, 512), BF16), qaa=((4, 192, 384), BF16),
    db=((4, 128, 384), BF16), gub=((4, 192, 512), BF16), qab=((4, 192, 384), BF16),
)
SEMS = dict(
    lsem=(4,), gsend=(len(PIECES), 7), grecv=(len(PIECES), 7), glocal=(len(PIECES),),
    s0=(2, len(CHUNKS)), s1=(2, len(CHUNKS), 2), s2=(2, len(CHUNKS)), sz=(3, 2, len(CHUNKS)), so=(len(CHUNKS), 3), sg=(2, 5),
)


class Step:
    def __init__(self, refs, comm):
        self.__dict__.update(refs)
        self.comm = comm
        self.copies, self.sent, self.sent0, self.ended = [], [], {}, []
        if comm:
            self.r, self.cc, self.z = lax.axis_index("row"), lax.axis_index("col"), lax.axis_index("dp")
        else:
            self.r = self.cc = self.z = jnp.int32(0)
        self.oc = 1 - self.cc
        r, z = self.r, self.z
        rx = r + 1 - 2 * (r % 2)
        ry = r + 2 - 4 * (r // 2)
        odd = z % 2
        self.rx, self.ry = rx, ry
        first, second = rx + odd * (ry - rx), ry + odd * (rx - ry)
        self.axes = ((first, second), (second, first))
        self.diag = 3 - r
        self.zn = z + 1 - 2 * odd
        self.zm = 3 - z

    def load(self):
        self.copies = []
        for i, (src, dst) in enumerate(((self.x_in, self.x), (self.c_in, self.c))):
            cp = pltpu.make_async_copy(src, dst, self.lsem.at[i])
            cp.start()
            self.copies.append(cp)

    def loaded(self):
        for cp in self.copies:
            cp.wait()
        self.copies = []

    def tables(self):
        block = (self.r * 2 + self.cc) * 4 + self.z
        mine = lax.broadcasted_iota(jnp.int32, (1, self.lens.shape[1]), 1) == block
        lens = [jnp.sum(jnp.where(mine, self.lens[i:i + 1, :], 0), axis=1, keepdims=True) for i in range(3)]
        ends = [lens[0], lens[0] + lens[1], lens[0] + lens[1] + lens[2]]

        def angle_rows(i):
            rows = ds(i * 128, 128)
            place = lax.broadcasted_iota(jnp.int32, (128, 128), 0) + i * 128
            lane = lax.broadcasted_iota(jnp.int32, (1, 128), 1)
            frequency = jnp.exp((lane % HALF).astype(F32) * (-2.0 / HEAD_DIM * math.log(10000.0)))
            start = jnp.zeros((128, 128), jnp.int32)
            for l, e in zip(lens, ends):
                start = start + jnp.where(place >= e, l, 0)
            angle = (place - start).astype(F32) * frequency
            self.cos[rows, :] = jnp.cos(angle)
            self.sin[rows, :] = jnp.sin(angle) * jnp.where(lane % HEAD_DIM < HALF, -1.0, 1.0)
        loop(4, angle_rows)
        self.gain1[...] = self.gain1_in[...].reshape(1, D)
        self.gain2[...] = self.gain2_in[...].reshape(1, D)

        def bias_rows(i):
            rows = ds(i * 128, 128)
            place = lax.broadcasted_iota(jnp.int32, (128, T), 0) + i * 128
            key = lax.broadcasted_iota(jnp.int32, (128, T), 1)
            seg_q = jnp.zeros((128, T), jnp.int32)
            seg_k = jnp.zeros((128, T), jnp.int32)
            for e in ends:
                seg_q = seg_q + jnp.where(place >= e, 1, 0)
                seg_k = seg_k + jnp.where(key >= e, 1, 0)
            ok = (seg_q == seg_k) & (place >= key)
            self.bias[rows, :] = jnp.where(ok, 0.0, MASKED)
        loop(4, bias_rows)

    def transpose_x(self):
        def step(i):
            cols = ds(i * 128, 128)
            self.xt[cols, :] = self.x[:, cols].T
        loop(6, step)

    def turn(self, t, sign):
        lane = lax.broadcasted_iota(jnp.int32, t.shape, 1)
        front = lane % HEAD_DIM < HALF
        partner = jnp.where(front, pltpu.roll(t, 128 - HALF, 1), pltpu.roll(t, HALF, 1))
        return t * self.cos[...] + partner * (self.sin[...] * sign)

    def project(self, name):
        out = getattr(self, name)
        t = dot(self.x[...], getattr(self, "w" + name)[...])
        for i in range(PAIRS):
            s = t[:, i * 128:(i + 1) * 128]
            if name != "v":
                s = self.turn(s, 1.0)
            if name == "q":
                s = s * HEAD_DIM ** -0.5
            out[:, i * 128:(i + 1) * 128] = s.astype(BF16)

    def halves(self, two):
        first = lax.broadcasted_iota(jnp.int32, two.shape, 1) < HEAD_DIM
        none = jnp.zeros_like(two)
        return jnp.where(first, two, none), jnp.where(first, none, two)

    def attend(self, first):
        loop(first + 2, self.attend_pair, first)

    def attend_pair(self, hp):
        lanes = ds(hp * 128, 128)
        q, k2, v = self.halves(self.q[:, lanes]), self.k[:, lanes], self.halves(self.v[:, lanes])
        for qb in range(2):
            keys = (qb + 1) * 256
            rows = slice(qb * 256, qb * 256 + 256)
            both = []
            for j in range(2):
                s = dot_nt(q[j][rows], k2[:keys]) + self.bias[rows, :keys]
                e = jnp.exp(s - jnp.max(s, axis=-1, keepdims=True))
                p = (e * (1.0 / jnp.sum(e, axis=-1, keepdims=True))).astype(BF16)
                (self.p1 if qb else self.p0)[2 * hp + j] = p
                both.append(p)
            o = dot(jnp.concatenate(both, axis=1), jnp.concatenate([v[0][:keys], v[1][:keys]], axis=0)).astype(BF16)
            self.attn[rows, lanes] = o
            self.attnt[lanes, rows] = o.T

    def norm_one(self):
        def step(i):
            rows = ds(i * 256, 256)
            h = self.x[rows, :].astype(F32) + dot(self.attn[rows, :], self.wo[...])
            r = lax.rsqrt(jnp.mean(h * h, axis=-1, keepdims=True) + EPS)
            n = h * r
            self.n1[rows, :] = n
            self.r1[rows, :] = r
            y = (n * self.gain1[...]).astype(BF16)
            self.y1[rows, :] = y
            self.y1t[:, rows] = y.T
        loop(2, step)

    def ffn(self, quarter):
        at = (quarter % 2) * 1024 + (quarter // 2) * 512
        cols = slice(at, at + 512)

        def step(i):
            rows = ds(i * 256, 256)
            g = dot(self.y1[rows, :], self.wg[:, cols])
            u = dot(self.y1[rows, :], self.wu[:, cols])
            s = jax.nn.sigmoid(g)
            gs = g * s
            h = (gs * u).astype(BF16)
            self.hid[rows, cols] = h
            self.hidt[cols, rows] = h.T
            self.b[rows, cols] = gs.astype(BF16)
            self.a[rows, cols] = (u * s * (1.0 + g * (1.0 - s))).astype(BF16)
        loop(2, step)

    def down(self, part):
        last = part == 3

        def step(i):
            rows = slice(i * 256, (i + 1) * 256)
            left = jnp.concatenate([self.hid[rows, s * 512 + part * 128:s * 512 + part * 128 + 128] for s in range(4)], axis=1)
            right = jnp.concatenate([self.wd[s * 512 + part * 128:s * 512 + part * 128 + 128, :] for s in range(4)], axis=0)
            t = dot(left, right)
            if part == 0:
                self.h2[rows, :] = self.n1[rows, :] * self.gain1[...] + t
                return
            h = self.h2[rows, :] + t
            if not last:
                self.h2[rows, :] = h
                return
            r = lax.rsqrt(jnp.mean(h * h, axis=-1, keepdims=True) + EPS)
            n = h * r
            c = self.c[rows, :].astype(F32)
            self.c[rows, :] = (n * self.gain2[...]).astype(BF16)
            self.gains[1:2, :] += jnp.sum(c * n, axis=0, keepdims=True)
            g = c * self.gain2[...]
            dh = r * (g - n * jnp.mean(g * n, axis=-1, keepdims=True))
            self.h2[rows, :] = dh
            self.dffn[rows, :] = dh.astype(BF16)
        if part == 0:
            self.gains[...] = jnp.zeros_like(self.gains)
        step(0)
        step(1)
        if last:
            cp = pltpu.make_async_copy(self.c, self.layer_out, self.lsem.at[2])
            cp.start()
            self.copies.append(cp)

    def dhidden(self, half):
        for i in (2 * half, 2 * half + 1):
            cols = slice(i * 512, (i + 1) * 512)
            t = dot_nt(self.dffn[...], self.wd[cols, :])
            self.a[:, cols] = (t * self.a[:, cols].astype(F32)).astype(BF16)
            self.b[:, cols] = (t * self.b[:, cols].astype(F32)).astype(BF16)

    def back_one(self):
        def step(i):
            rows = ds(i * 256, 256)
            dy = self.h2[rows, :] + dot_nt(self.a[rows, :], self.wg[...]) + dot_nt(self.b[rows, :], self.wu[...])
            n = self.n1[rows, :]
            self.gains[0:1, :] += jnp.sum(dy * n, axis=0, keepdims=True)
            g = dy * self.gain1[...]
            dh = self.r1[rows, :] * (g - n * jnp.mean(g * n, axis=-1, keepdims=True))
            self.h2[rows, :] = dh
            self.dffn[rows, :] = dh.astype(BF16)
        loop(2, step)

    def dattn(self):
        self.x[...] = dot_nt(self.dffn[...], self.wo[...]).astype(BF16)

    def attend_back(self, i):
        loop(2, lambda half: self.attend_back_pair(half * 3 + i))

    def attend_back_pair(self, hp):
        lanes = ds(hp * 128, 128)
        v2 = self.v[:, lanes]
        q, k, do = self.halves(self.q[:, lanes]), self.halves(self.k[:, lanes]), self.halves(self.x[:, lanes])
        dq, s, p = [], [], []
        for qb in range(2):
            keys = (qb + 1) * 256
            rows = slice(qb * 256, qb * 256 + 256)
            low = [(self.p1 if qb else self.p0)[2 * hp + j] for j in range(2)]
            ds_low = []
            for j in range(2):
                wide = low[j].astype(F32)
                dp = dot_nt(do[j][rows], v2[:keys])
                ds_low.append((wide * (dp - jnp.sum(wide * dp, axis=-1, keepdims=True))).astype(BF16))
            dq.append(dot(jnp.concatenate(ds_low, axis=1), jnp.concatenate([k[0][:keys], k[1][:keys]], axis=0)))
            s.append(ds_low)
            p.append(low)

        def over_queries(of, rows):
            first = dot_tn(jnp.concatenate([*of[0], of[1][0][:, :256], of[1][1][:, :256]], axis=0),
                           jnp.concatenate([rows[0][:256], rows[1][:256], rows[0][256:], rows[1][256:]], axis=0))
            second = dot_tn(jnp.concatenate([of[1][0][:, 256:], of[1][1][:, 256:]], axis=0),
                            jnp.concatenate([rows[0][256:], rows[1][256:]], axis=0))
            return jnp.concatenate([first, second], axis=0)
        dk, dv = over_queries(s, q), over_queries(p, do)
        self.q[:, lanes] = self.turn(jnp.concatenate(dq, axis=0) * HEAD_DIM ** -0.5, -1.0).astype(BF16)
        self.k[:, lanes] = self.turn(dk, -1.0).astype(BF16)
        self.v[:, lanes] = dv.astype(BF16)

    def input_grad(self):
        self.h2[...] += dot_nt(self.q[...], self.wq[...]) + dot_nt(self.k[...], self.wk[...]) + dot_nt(self.v[...], self.wv[...])
        cp = pltpu.make_async_copy(self.h2, self.dx, self.lsem.at[3])
        cp.start()
        self.copies.append(cp)

    def pick(self, n, d, gu, qa):
        j = int(n[1:] or 0)
        if n[0] == "D":
            return d.at[j]
        if n[0] in "GU":
            return gu.at[2 * j + (n[0] == "U")]
        if n[0] == "B":
            rows = qa.shape[-2] // 2
            return qa.at[(2, *[slice(None)] * (len(qa.shape) - 3), slice(j * rows, (j + 1) * rows))]
        return qa.at[3 if n[0] == "O" else j]

    def own(self, n):
        return self.pick(n, self.gd, self.ggu, self.ga)

    def out0(self, n):
        rows, cols = SHAPE[n]
        return self.send0.at[CHUNKS.index(n) % SLOTS, 0:4 * rows, 0:cols]

    def grad(self, n):
        own, other = self.own(n), self.out0(n)
        c0 = self.cc == 0

        def both(t):
            lo, hi = t[:, :384], t[:, 384:]
            own[...] = jnp.where(c0, lo, hi).astype(BF16)
            other[...] = jnp.where(c0, hi, lo).astype(BF16)
        j = int(n[1:] or 0)
        if n[0] == "D":
            both(dot(jnp.concatenate([self.hidt[s * 512 + j * 128:s * 512 + j * 128 + 128, :] for s in range(4)], axis=0), self.dffn[...]))
        elif n[0] == "O":
            both(dot(self.attnt[...], self.dffn[...]))
        elif n[0] in "GU":
            src = self.a if n[0] == "G" else self.b
            for half, dst in ((self.oc, other), (self.cc, own)):
                dst[...] = dot(self.y1t[...], src[:, ds(half * 1024 + j * 512, 512)]).astype(BF16)
        else:
            right = []
            for half in (self.oc, self.cc):
                lanes = ds((half * 3 + (2 if n[0] == "B" else j)) * 128, 128)
                right += [self.q[:, lanes], self.k[:, lanes], self.v[:, lanes]]
            left = self.xt[...]
            if n[0] == "B":
                left = jnp.concatenate([self.xt[s * 192 + j * 96:s * 192 + j * 96 + 96, :] for s in range(4)], axis=0)
            t = dot(left, jnp.concatenate(right, axis=1)).astype(BF16)
            other[...] = t[:, :384]
            own[...] = t[:, 384:]

    def remote(self, src, dst, send, recv, **where):
        cp = pltpu.make_async_remote_copy(src_ref=src, dst_ref=dst, send_sem=send, recv_sem=recv, device_id=where, device_id_type=MESH)
        return cp

    def begin(self, cp, sent):
        cp.start()
        sent.append(cp)

    def enter(self):
        barrier = pltpu.get_barrier_semaphore()
        for where in ({"col": self.oc}, {"row": self.rx}, {"row": self.ry}, {"dp": self.zn}, {"dp": self.zm}):
            pl.semaphore_signal(barrier, inc=1, device_id=where, device_id_type=MESH)
        pl.semaphore_wait(barrier, 5)

    def region(self, i, row, core):
        n, r0, nr, c0, nc = PIECES[i]
        rows, cols = SHARD[n]
        return getattr(self, "w" + n).at[ds(row * rows + r0, nr, 64), ds(core * cols + c0, nc, 128)]

    def shard(self, i):
        n, r0, nr, c0, nc = PIECES[i]
        return getattr(self, "h" + n).at[r0:r0 + nr, c0:c0 + nc]

    def gather(self, i, what):
        a, b = self.axes[i % 2]
        row = (self.r, a, a, self.r, a, self.diag, b)[what]
        where = ({"row": a}, {"row": b}, {"dp": self.zn}, *[{"col": self.oc}] * 4)[what]
        src = self.shard(i) if what in (0, 3) else self.region(i, row, self.cc)
        return self.remote(src, self.region(i, row, self.cc), self.gsend.at[i, what], self.grecv.at[i, what], **where)

    def go(self, i, *whats):
        for what in whats:
            self.begin(self.gather(i, what), self.sent)

    def push(self, i):
        self.go(i, 0)

    def share(self, i):
        self.go(i, 3)
        pltpu.make_async_copy(self.shard(i), self.region(i, self.r, self.cc), self.glocal.at[i]).start()

    def relay(self, i):
        self.gather(i, 0).wait_recv()
        self.go(i, 1, 2, 4)

    def relay_two(self, i):
        self.gather(i, 1).wait_recv()
        self.go(i, 5)
        self.gather(i, 2).wait_recv()
        self.go(i, 6)

    def ready(self, i):
        pltpu.make_async_copy(self.shard(i), self.region(i, self.r, self.cc), self.glocal.at[i]).wait()
        for what in (3, 4, 5, 6):
            self.gather(i, what).wait_recv()

    def part(self, kind, n):
        d, gu, qa = {"1": (self.d1, self.gu1, self.qa1), "2": (self.d2, self.gu2, self.qa2), "a": (self.da, self.gua, self.qaa),
                     "b": (self.db, self.gub, self.qab)}[kind]
        return self.pick(n, d, gu, qa)

    def chunk(self, n):
        k = CHUNKS.index(n)
        rows, cols = SHAPE[n]
        if n in SPREAD:
            ra, rb = self.axes[k % 2]
        else:
            ra, rb = (self.rx, self.ry) if k % 2 == 0 else (self.ry, self.rx)
        block = lambda row: ds(row * rows, rows)
        return k, rows, cols, ra, rb, block

    def copy0(self, n):
        k, rows, cols, *_ = self.chunk(n)
        at = (k % SLOTS, slice(0, 4 * rows), slice(0, cols))
        return self.remote(self.send0.at[at], self.recv0.at[at], self.s0.at[0, k], self.s0.at[1, k], col=self.oc)

    def copy1(self, n, which):
        k, rows, cols, ra, rb, block = self.chunk(n)
        if n in SPREAD:
            row, where = ((rb, {"dp": self.zn}), (self.diag, {"row": rb}))[which]
        else:
            row, where = (ra, self.diag)[which], {"row": ra}
        return self.remote(self.own(n).at[block(row), :], self.part("1", n).at[which], self.s1.at[0, k, which], self.s1.at[1, k, which], **where)

    def copy2(self, n):
        k, rows, cols, ra, rb, block = self.chunk(n)
        row = ra if n in SPREAD else rb
        return self.remote(self.own(n).at[block(row), :], self.part("2", n), self.s2.at[0, k], self.s2.at[1, k], row=row)

    def copy_z(self, n, leg):
        k, rows, cols, ra, rb, block = self.chunk(n)
        src = self.part("2", n) if leg == 2 else self.own(n).at[block(self.r), :]
        dst = self.part("b" if leg == 1 else "a", n)
        return self.remote(src, dst, self.sz.at[leg, 0, k], self.sz.at[leg, 1, k], dp=self.zm if leg == 1 else self.zn)

    def inner(self):
        return ((self.z + 1) // 2) % 2 == 1

    def outer(self):
        return ((self.z + 1) // 2) % 2 == 0

    def add(self, ref, other, to=None):
        unit = 48 if ref.shape[0] % 48 == 0 else 32
        to = ref if to is None else to

        def step(i):
            rows = ds(i * unit, unit)
            to[rows, :] = (ref[rows, :].astype(F32) + other[rows, :].astype(F32)).astype(BF16)
        loop(ref.shape[0] // unit, step)

    def make(self, n):
        k = CHUNKS.index(n)
        if k >= SLOTS:
            self.sent0[k - SLOTS].wait_send()
            self.sent = [cp for cp in self.sent if cp is not self.sent0[k - SLOTS]]
        self.grad(n)
        if k >= SLOTS:
            pl.semaphore_wait(self.credit.at[k % SLOTS], 1)
        self.begin(self.copy0(n), self.sent)
        self.sent0[k] = self.sent[-1]

    def sum0(self, n):
        k, rows, cols, ra, rb, block = self.chunk(n)
        self.copy0(n).wait_recv()
        own = self.own(n)
        got = self.recv0.at[k % SLOTS, 0:4 * rows, 0:cols]
        for row, which in ((self.diag, 1), (rb, 0), (ra, None), (self.r, None)) if n in SPREAD else ((self.diag, 1), (ra, 0), (rb, None), (self.r, None)):
            self.add(own.at[block(row), :], got.at[block(row), :])
            if which is not None:
                self.begin(self.copy1(n, which), self.sent)
        if k + SLOTS < len(CHUNKS):
            pl.semaphore_signal(self.credit.at[k % SLOTS], inc=1, device_id={"col": self.oc}, device_id_type=MESH)

    def sum1(self, n):
        k, rows, cols, ra, rb, block = self.chunk(n)
        self.copy1(n, 1).wait_recv()
        self.add(self.own(n).at[block(ra if n in SPREAD else rb), :], self.part("1", n).at[1])
        if n in SPREAD:
            self.copy1(n, 0).wait_recv()
            self.add(self.own(n).at[block(ra), :], self.part("1", n).at[0])
        self.begin(self.copy2(n), self.sent)

    def sum2(self, n):
        k, rows, cols, ra, rb, block = self.chunk(n)
        own = self.own(n).at[block(self.r), :]
        if n not in SPREAD:
            self.copy1(n, 0).wait_recv()
            self.add(own, self.part("1", n).at[0])
        self.copy2(n).wait_recv()
        self.add(own, self.part("2", n))

        @pl.when(self.outer())
        def _():
            self.copy_z(n, 0).start()

    def sum_z1(self, n):
        k, rows, cols, ra, rb, block = self.chunk(n)

        @pl.when(self.inner())
        def _():
            self.copy_z(n, 0).wait_recv()
            self.add(self.own(n).at[block(self.r), :], self.part("a", n))
            self.copy_z(n, 1).start()

    def sum_z2(self, n):
        k, rows, cols, ra, rb, block = self.chunk(n)

        @pl.when(self.inner())
        def _():
            self.copy_z(n, 1).wait_recv()
            total = self.part("2", n)
            own = self.own(n).at[block(self.r), :]
            self.add(own, self.part("b", n), total)
            self.copy_z(n, 2).start()
            for cp in self.results(n, total):
                cp.start()

    def sum_z3(self, n):
        self.ended.append(n)

        @pl.when(self.outer())
        def _():
            self.copy_z(n, 2).wait_recv()
            for cp in self.results(n, self.part("a", n)):
                cp.start()

    def results(self, n, src):
        k = CHUNKS.index(n)
        j = int(n[1:] or 0)
        if n[0] in "AB":
            rows, j = (slice(j * 96, j * 96 + 96), 2) if n[0] == "B" else (slice(0, 192), j)
            return [pltpu.make_async_copy(src.at[:, i * 128:(i + 1) * 128], getattr(self, "out_" + m).at[rows, j * 128:(j + 1) * 128], self.so.at[k, i])
                    for i, m in enumerate("qkv")]
        out = getattr(self, "out_" + n[0].lower())
        dst = {"D": lambda: out.at[j * 128:(j + 1) * 128, :], "G": lambda: out.at[:, j * 512:(j + 1) * 512],
               "U": lambda: out.at[:, j * 512:(j + 1) * 512], "O": lambda: out}[n[0]]()
        return [pltpu.make_async_copy(src, dst, self.so.at[k, 0])]

    def gains_copy(self, t):
        where = ({"col": self.oc}, {"row": self.rx}, {"row": self.ry}, {"dp": self.zn}, {"dp": self.zm})[t]
        return self.remote(self.gains, self.gains_in.at[t], self.sg.at[0, t], self.sg.at[1, t], **where)

    def gains_send(self, t):
        self.gains_copy(t).start()

    def gains_add(self, t):
        self.gains_copy(t).wait()
        self.gains[...] += self.gains_in[t]

    def settle(self):
        slots = [cp for cp in self.sent if any(cp is s for s in self.sent0.values())]
        for cp in self.sent:
            if not any(cp is s for s in slots):
                cp.wait_send()
        self.sent = slots

    def finish(self):
        for cp in self.sent:
            cp.wait_send()
        for inner, legs, kind in ((self.outer(), (0,), "a"), (self.inner(), (1, 2), "2")):
            @pl.when(inner)
            def _():
                for n in self.ended:
                    for leg in legs:
                        self.copy_z(n, leg).wait_send()
                    for cp in self.results(n, self.part(kind, n)):
                        cp.wait()
        for cp in self.copies:
            cp.wait()


D0, D1, D2, D3, G0, U0, G1, U1, O, A0, A1, B0, B1 = CHUNKS


def order(s):
    s.load(); s.push(0); s.push(1); s.share(2); s.share(10); s.push(2); s.share(5); s.push(3); s.push(4); s.relay(0); s.share(0); s.relay(1); s.push(5); s.relay(2)
    s.share(12); s.share(8); s.relay(3); s.relay_two(0); s.relay(4); s.share(13); s.share(1); s.tables(); s.push(6); s.relay_two(1); s.loaded(); s.transpose_x(); s.share(6); s.push(7)
    s.share(3); s.ready(0); s.relay_two(2); s.push(8); s.relay_two(3); s.relay(5); s.share(7); s.push(9); s.ready(1); s.ready(2); s.project('q'); s.ready(3); s.share(4); s.relay(6)
    s.project('k'); s.relay_two(4); s.ready(4); s.project('v'); s.relay(7); s.share(11); s.relay(8); s.push(10); s.attend(0); s.relay_two(5); s.relay(9); s.attend(2); s.attend(4); s.ready(5)
    s.push(11); s.relay_two(6); s.share(9); s.push(12); s.relay_two(7); s.relay(10); s.ready(6); s.norm_one(); s.ready(7); s.ffn(0); s.relay_two(8); s.relay_two(9); s.push(13); s.relay(11)
    s.ffn(1); s.ready(8); s.relay(12); s.ready(9); s.relay_two(10); s.ffn(2); s.relay(13); s.ready(10); s.ffn(3); s.relay_two(11); s.relay_two(12); s.down(0); s.ready(11); s.down(1)
    s.relay_two(13); s.ready(12); s.down(2); s.ready(13); s.down(3); s.make(D0); s.make(D1); s.sum0(D0); s.make(D2); s.sum0(D1); s.make(D3); s.dhidden(0); s.sum0(D2); s.dhidden(1)
    s.sum1(D0); s.make(G0); s.sum0(D3); s.sum1(D1); s.make(U0); s.sum0(G0); s.make(G1); s.sum1(D2); s.sum0(U0); s.make(U1); s.sum1(D3); s.back_one(); s.sum1(G0); s.sum0(G1)
    s.sum0(U1); s.sum2(D2); s.sum2(D0); s.gains_send(0); s.dattn(); s.attend_back(2); s.gains_add(0); s.sum_z1(D2); s.sum1(U0); s.sum2(G0); s.make(O); s.sum2(D1); s.sum_z1(D0); s.attend_back(0)
    s.make(A0); s.sum1(G1); s.sum_z1(G0); s.gains_send(1); s.sum1(U1); s.sum2(D3); s.sum_z2(D0); s.sum_z2(D2); s.sum0(O); s.sum0(A0); s.sum_z1(D1); s.sum2(U0); s.attend_back(1); s.sum_z2(G0)
    s.sum_z1(D3); s.sum2(G1); s.sum_z1(U0); s.gains_add(1); s.sum2(U1); s.sum_z2(D1); s.gains_send(2); s.make(A1); s.sum1(O); s.sum1(A0); s.make(B0); s.sum_z2(D3); s.sum_z1(G1); s.sum_z3(G0)
    s.sum0(A1); s.sum0(B0); s.sum_z2(U0); s.sum2(O); s.sum_z1(U1); s.sum_z3(D0); s.sum_z2(G1); s.sum1(A1); s.make(B1); s.gains_add(2); s.sum2(A0); s.settle(); s.sum0(B1); s.sum_z1(O)
    s.gains_send(3); s.sum_z2(U1); s.sum2(A1); s.sum_z1(A0); s.sum1(B1); s.sum1(B0); s.sum_z3(G1); s.gains_add(3); s.sum_z2(O); s.sum_z3(U0); s.sum_z1(A1); s.sum2(B1); s.gains_send(4); s.sum_z2(A0)
    s.sum2(B0); s.sum_z3(D2); s.sum_z3(U1); s.sum_z3(D1); s.sum_z1(B1); s.sum_z3(D3); s.sum_z2(A1); s.sum_z1(B0); s.sum_z2(B1); s.sum_z3(A0); s.sum_z2(B0); s.input_grad(); s.sum_z3(A1); s.sum_z3(O)
    s.gains_add(4); s.sum_z3(B1); s.sum_z3(B0)


OUTS = ("layer_out", "dx", "out_q", "out_k", "out_v", "out_o", "out_g", "out_u", "out_d", "gains_out")
INS = ("x_in", "c_in", "lens", "hq", "hk", "hv", "ho", "hg", "hu", "hd", "gain1_in", "gain2_in")


def step_kernel(*refs):
    names = INS + OUTS + tuple(SCRATCH) + tuple(REMOTE) + tuple(SEMS) + ("credit",)
    s = Step(dict(zip(names, refs, strict=True)), True)
    s.enter()
    order(s)
    s.gains_out[...] = s.gains[...]
    s.finish()


def widen_kernel(*refs):
    ins, outs, low, wide, sems = refs[:10], refs[10:21], refs[21:30], refs[30:37], refs[37]
    wide = [*low[:2], *wide]
    loads = [pltpu.make_async_copy(ins[i], low[i], sems.at[0, i]) for i in range(9)]
    stores = [pltpu.make_async_copy(wide[i], outs[i], sems.at[1, i]) for i in range(9)]
    for cp in loads:
        cp.start()
    outs[9][...] = ins[9][0, :]
    outs[10][...] = ins[9][1, :]
    for i in range(9):
        loads[i].wait()
        if i > 1:
            wide[i][...] = low[i][...].astype(F32)
        stores[i].start()
    for cp in stores:
        cp.wait()


def fused_body(x, c, lens, wq, wk, wv, wo, wg, wu, wd, gain1, gain2):
    hbm, vmem = pl.BlockSpec(memory_space=pl.ANY), pl.BlockSpec(memory_space=pltpu.VMEM)
    struct = jax.ShapeDtypeStruct
    shards = [SHARD[n] for n in NAMES]
    out = pl.pallas_call(
        step_kernel,
        out_shape=[struct((T, D), BF16), struct((T, D), F32), *[struct(s, BF16) for s in shards], struct((8, D), F32)],
        in_specs=[hbm, hbm, vmem, *[hbm] * 7, vmem, vmem],
        out_specs=[*[hbm] * 9, vmem],
        scratch_shapes=[*[pltpu.VMEM(*v) for v in (SCRATCH | REMOTE).values()], *[pltpu.SemaphoreType.DMA(v) for v in SEMS.values()],
                        pltpu.SemaphoreType.REGULAR((SLOTS,))],
        compiler_params=pltpu.CompilerParams(collective_id=0, has_side_effects=True, vmem_limit_bytes=63 << 20),
        name="step",
    )(x, c, lens.T, wq, wk, wv, wo, wg, wu, wd, gain1, gain2)
    return pl.pallas_call(
        widen_kernel,
        out_shape=[struct((T, D), BF16), struct((T, D), F32), *[struct(s, F32) for s in shards], struct((D,), F32), struct((D,), F32)],
        in_specs=[*[hbm] * 9, vmem],
        out_specs=[*[hbm] * 9, vmem, vmem],
        scratch_shapes=[pltpu.VMEM((T, D), BF16), pltpu.VMEM((T, D), F32), *[pltpu.VMEM(s, BF16) for s in shards],
                        *[pltpu.VMEM(s, F32) for s in shards], pltpu.SemaphoreType.DMA((2, 9))],
        compiler_params=pltpu.CompilerParams(vmem_limit_bytes=63 << 20),
        name="widen",
    )(*out)


def pack_info(lengths_row, places_count):
    places = jnp.arange(places_count, dtype=jnp.int32)
    segment = jnp.zeros((places_count,), jnp.int32)
    start = jnp.zeros((places_count,), jnp.int32)
    end = jnp.int32(0)
    for i in range(lengths_row.shape[0]):
        end = end + lengths_row[i]
        passed = (places >= end).astype(jnp.int32)
        segment = segment + passed
        start = start + passed * lengths_row[i]
    return segment, (places - start).astype(F32)


def angles(positions):
    frequency = 10000.0 ** (-jnp.arange(HALF, dtype=F32) * (2.0 / HEAD_DIM))
    turned = positions[..., None] * frequency
    return jnp.cos(turned), jnp.sin(turned)


def rotate(values, cosine, sine):
    a, b = values[..., :HALF], values[..., HALF:]
    return jnp.concatenate([a * cosine - b * sine, b * cosine + a * sine], axis=-1)


def norm_forward(resid):
    inverse = lax.rsqrt(jnp.mean(resid * resid, axis=-1, keepdims=True) + EPS)
    return resid * inverse, inverse


def norm_backward(grad, normed, inverse):
    return inverse * (grad - normed * jnp.mean(grad * normed, axis=-1, keepdims=True))


def heads_first(matrix):
    t, w = matrix.shape
    return matrix.reshape(t, w // HEAD_DIM, HEAD_DIM).transpose(1, 0, 2)


def heads_last(stacked):
    h, t, w = stacked.shape
    return stacked.transpose(1, 0, 2).reshape(t, h * w)


def block_local(x, c, lengths, wq, wk, wv, wo, wg, wu, wd, gain1, gain2):
    t = x.shape[0]
    segment, positions = pack_info(lengths, t)
    cosine, sine = angles(positions)
    places = jnp.arange(t, dtype=jnp.int32)
    mask = (segment[:, None] == segment[None, :]) & (places[:, None] >= places[None, :])
    scale = HEAD_DIM ** (-0.5)
    q = rotate(heads_first(dot(x, wq)), cosine, sine).astype(BF16)
    k = rotate(heads_first(dot(x, wk)), cosine, sine).astype(BF16)
    v = heads_first(dot(x, wv).astype(BF16))
    bmm = lambda e, a, b: jnp.einsum(e, a, b, preferred_element_type=F32)
    s = jnp.where(mask, bmm("htd,hsd->hts", q, k) * scale, MASKED)
    e = jnp.exp(s - jnp.max(s, axis=-1, keepdims=True))
    probs = e / jnp.sum(e, axis=-1, keepdims=True)
    low = probs.astype(BF16)
    attn = heads_last(bmm("hts,hsd->htd", low, v).astype(BF16))
    n1, r1 = norm_forward(x.astype(F32) + dot(attn, wo))
    y1 = n1 * gain1
    y1_low = y1.astype(BF16)
    gate, up = dot(y1_low, wg), dot(y1_low, wu)
    sig = jax.nn.sigmoid(gate)
    hidden = (gate * sig * up).astype(BF16)
    n2, r2 = norm_forward(y1 + dot(hidden, wd))
    layer_out = (n2 * gain2).astype(BF16)
    cf = c.astype(F32)
    gain2_grad = jnp.sum(cf * n2, axis=0)
    dh2 = norm_backward(cf * gain2, n2, r2)
    dffn = dh2.astype(BF16)
    d_down = dot_tn(hidden, dffn)
    dhidden = dot_nt(dffn, wd)
    dgate = (dhidden * up * sig * (1.0 + gate * (1.0 - sig))).astype(BF16)
    dup = (dhidden * gate * sig).astype(BF16)
    d_gate, d_up = dot_tn(y1_low, dgate), dot_tn(y1_low, dup)
    dy1 = dh2 + dot_nt(dgate, wg) + dot_nt(dup, wu)
    gain1_grad = jnp.sum(dy1 * n1, axis=0)
    dh1 = norm_backward(dy1 * gain1, n1, r1)
    dbranch = dh1.astype(BF16)
    d_out = dot_tn(attn, dbranch)
    dattn = heads_first(dot_nt(dbranch, wo).astype(BF16))
    dprobs = bmm("htd,hsd->hts", dattn, v)
    dscores = (probs * (dprobs - jnp.sum(probs * dprobs, axis=-1, keepdims=True)) * scale).astype(BF16)
    dq = heads_last(rotate(bmm("hts,hsd->htd", dscores, k), cosine, -sine)).astype(BF16)
    dk = heads_last(rotate(bmm("hts,htd->hsd", dscores, q), cosine, -sine)).astype(BF16)
    dv = heads_last(bmm("hts,htd->hsd", low, dattn)).astype(BF16)
    d_q, d_k, d_v = dot_tn(x, dq), dot_tn(x, dk), dot_tn(x, dv)
    dx = dh1 + dot_nt(dq, wq) + dot_nt(dk, wk) + dot_nt(dv, wv)
    return layer_out, dx, (d_q, d_k, d_v, d_out, d_gate, d_up, d_down), gain1_grad, gain2_grad


def body(x, c, seq_lengths, wq, wk, wv, wo, wg, wu, wd, gain1, gain2):
    block = (lax.axis_index("row") * lax.axis_size("col") + lax.axis_index("col")) * lax.axis_size("dp") + lax.axis_index("dp")
    lengths = lax.dynamic_index_in_dim(seq_lengths, block, keepdims=False)
    full = [
        lax.all_gather(lax.all_gather(w, "col", axis=1, tiled=True), "row", axis=0, tiled=True)
        for w in (wq, wk, wv, wo, wg, wu, wd)
    ]
    layer_out, dx, grads, g1, g2 = block_local(x, c, lengths, *full, gain1, gain2)
    summed = []
    for g in grads:
        g = lax.psum_scatter(g.astype(BF16), "col", scatter_dimension=1, tiled=True)
        g = lax.psum_scatter(g, "row", scatter_dimension=0, tiled=True)
        summed.append(lax.psum(g, "dp").astype(F32))
    g1, g2 = lax.psum((g1, g2), ("row", "col", "dp"))
    return (layer_out, dx, *summed, g1, g2)


def solution(mesh):
    tok = P(("row", "col", "dp"), None)
    mat = P("row", "col")
    fits = tuple(mesh.shape[a] for a in ("row", "col", "dp")) == (4, 2, 4)
    return jax.shard_map(
        fused_body if fits else body, mesh=mesh, in_specs=(tok, tok, P(), *[mat] * 7, P(), P()),
        out_specs=(tok, tok, *[mat] * 7, P(), P()), check_vma=False,
    )
```

```python
import math

import jax
import jax.numpy as jnp
from jax import lax
from jax.experimental import pallas as pl
from jax.experimental.pallas import tpu as pltpu
from jax.sharding import PartitionSpec as P

MESH = pl.DeviceIdType.MESH

HEAD_DIM = 64
HALF = HEAD_DIM // 2
EPS = 1e-06
MASKED = -1e30
BF16 = jnp.bfloat16
F32 = jnp.float32

T, D, FF, HEADS = 512, 768, 2048, 12
PAIRS = HEADS // 2
NAMES = ("q", "k", "v", "o", "g", "u", "d")
SHARD = {"q": (192, 384), "k": (192, 384), "v": (192, 384), "o": (192, 384), "g": (192, 1024), "u": (192, 1024), "d": (512, 384)}
PIECES = (
    ("q", 0, 64, 0, 384), ("q", 64, 64, 0, 384), ("q", 128, 64, 0, 384), ("k", 0, 192, 0, 384), ("v", 0, 192, 0, 384), ("o", 0, 192, 0, 384),
    ("g", 0, 192, 0, 512), ("u", 0, 192, 0, 512), ("g", 0, 192, 512, 512), ("u", 0, 192, 512, 512),
    ("d", 0, 128, 0, 384), ("d", 128, 128, 0, 384), ("d", 256, 128, 0, 384), ("d", 384, 128, 0, 384),
)
DIRECT = (13,)
CHUNKS = ("D0", "D1", "D2", "D3", "G0", "U0", "G1", "U1", "O", "A0", "A1", "B0", "B1")
SHAPE = {n: {"D": (128, 384), "G": (192, 512), "U": (192, 512), "O": (192, 384), "A": (192, 384), "B": (96, 384)}[n[0]] for n in CHUNKS}
SPREAD = ("D0", "D1", "D2", "D3", "G0", "U0")
SLOTS = 2


def dot(a, b):
    return jnp.dot(a, b, preferred_element_type=F32)


def dot_nt(a, b):
    return lax.dot_general(a, b, (((1,), (1,)), ((), ())), preferred_element_type=F32)


def dot_tn(a, b):
    return lax.dot_general(a, b, (((0,), (0,)), ((), ())), preferred_element_type=F32)


def ds(start, size, multiple=None):
    if isinstance(start, int):
        return pl.ds(start, size)
    return pl.ds(pl.multiple_of(start, multiple or size), size)


def loop(n, f, start=0):
    def step(i, carry):
        f(i)
        return carry
    lax.fori_loop(start, n, step, 0)


SCRATCH = dict(
    wq=((D, D), BF16), wk=((D, D), BF16), wv=((D, D), BF16), wo=((D, D), BF16),
    wg=((D, FF), BF16), wu=((D, FF), BF16), wd=((FF, D), BF16),
    x=((T, D), BF16), xt=((D, T), BF16), c=((T, D), BF16),
    q=((T, D), BF16), k=((T, D), BF16), v=((T, D), BF16),
    p0=((HEADS, 256, 256), BF16), p1=((HEADS, 256, 512), BF16),
    attn=((T, D), BF16), attnt=((D, T), BF16),
    n1=((T, D), F32), y1=((T, D), BF16), y1t=((D, T), BF16),
    a=((T, FF), BF16), b=((T, FF), BF16), hid=((T, FF), BF16), hidt=((FF, T), BF16),
    h2=((T, D), F32), dffn=((T, D), BF16), bias=((T, T), F32),
    cos=((T, 128), F32), sin=((T, 128), F32), r1=((T, 1), F32),
    lens=((4, 32), jnp.int32), gain1_low=((D,), F32), gain2_low=((D,), F32), gain1=((1, D), F32), gain2=((1, D), F32), gains=((8, D), F32), gains_in=((5, 8, D), F32),
    gd=((4, 512, 384), BF16), ggu=((4, 768, 512), BF16), ga=((4, 768, 384), BF16),
    send0=((SLOTS, 768, 512), BF16),
)
REMOTE = dict(
    recv0=((SLOTS, 768, 512), BF16),
    d1=((4, 2, 128, 384), BF16), gu1=((4, 2, 192, 512), BF16), qa1=((4, 2, 192, 384), BF16),
    d2=((4, 128, 384), BF16), gu2=((4, 192, 512), BF16), qa2=((4, 192, 384), BF16),
    da=((4, 128, 384), BF16), gua=((4, 192, 512), BF16), qaa=((4, 192, 384), BF16),
    db=((4, 128, 384), BF16), gub=((4, 192, 512), BF16), qab=((4, 192, 384), BF16),
)
SEMS = dict(
    lsem=(8,), gsend=(len(PIECES), 7), grecv=(len(PIECES), 7), glocal=(len(PIECES),),
    s0=(2, len(CHUNKS)), s1=(2, len(CHUNKS), 2), s2=(2, len(CHUNKS)), sz=(3, 2, len(CHUNKS)), so=(len(CHUNKS), 3), sg=(2, 5),
)


class Step:
    def __init__(self, refs, comm):
        self.__dict__.update(refs)
        self.comm = comm
        self.copies, self.sent, self.sent0, self.ended = [], [], {}, []
        if comm:
            self.r, self.cc, self.z = lax.axis_index("row"), lax.axis_index("col"), lax.axis_index("dp")
        else:
            self.r = self.cc = self.z = jnp.int32(0)
        self.oc = 1 - self.cc
        r, z = self.r, self.z
        rx = r + 1 - 2 * (r % 2)
        ry = r + 2 - 4 * (r // 2)
        odd = z % 2
        self.rx, self.ry = rx, ry
        first, second = rx + odd * (ry - rx), ry + odd * (rx - ry)
        self.axes = ((first, second), (second, first))
        self.diag = 3 - r
        self.zn = z + 1 - 2 * odd
        self.zm = 3 - z

    def load(self):
        self.copies = []
        pairs = ((self.x_in, self.x), (self.c_in, self.c), (self.lens_in, self.lens), (self.gain1_in, self.gain1_low), (self.gain2_in, self.gain2_low))
        for i, (src, dst) in enumerate(pairs):
            cp = pltpu.make_async_copy(src, dst, self.lsem.at[i])
            cp.start()
            self.copies.append(cp)

    def loaded(self):
        for cp in self.copies:
            cp.wait()
        self.copies = []

    def tables(self):
        for cp in self.copies[2:]:
            cp.wait()
        self.copies = self.copies[:2]
        block = (self.r * 2 + self.cc) * 4 + self.z
        mine = lax.broadcasted_iota(jnp.int32, (1, self.lens.shape[1]), 1) == block
        lens = [jnp.sum(jnp.where(mine, self.lens[i:i + 1, :], 0), axis=1, keepdims=True) for i in range(3)]
        ends = [lens[0], lens[0] + lens[1], lens[0] + lens[1] + lens[2]]

        def angle_rows(i):
            rows = ds(i * 128, 128)
            place = lax.broadcasted_iota(jnp.int32, (128, 128), 0) + i * 128
            lane = lax.broadcasted_iota(jnp.int32, (1, 128), 1)
            frequency = jnp.exp((lane % HALF).astype(F32) * (-2.0 / HEAD_DIM * math.log(10000.0)))
            start = jnp.zeros((128, 128), jnp.int32)
            for l, e in zip(lens, ends):
                start = start + jnp.where(place >= e, l, 0)
            angle = (place - start).astype(F32) * frequency
            self.cos[rows, :] = jnp.cos(angle)
            self.sin[rows, :] = jnp.sin(angle) * jnp.where(lane % HEAD_DIM < HALF, -1.0, 1.0)
        loop(4, angle_rows)
        self.gain1[...] = self.gain1_low[...].reshape(1, D)
        self.gain2[...] = self.gain2_low[...].reshape(1, D)

        def bias_rows(i):
            rows = ds(i * 128, 128)
            place = lax.broadcasted_iota(jnp.int32, (128, T), 0) + i * 128
            key = lax.broadcasted_iota(jnp.int32, (128, T), 1)
            seg_q = jnp.zeros((128, T), jnp.int32)
            seg_k = jnp.zeros((128, T), jnp.int32)
            for e in ends:
                seg_q = seg_q + jnp.where(place >= e, 1, 0)
                seg_k = seg_k + jnp.where(key >= e, 1, 0)
            ok = (seg_q == seg_k) & (place >= key)
            self.bias[rows, :] = jnp.where(ok, 0.0, MASKED)
        loop(4, bias_rows)

    def transpose_x(self):
        def step(i):
            cols = ds(i * 128, 128)
            self.xt[cols, :] = self.x[:, cols].T
        loop(6, step)

    def turn(self, t, sign):
        lane = lax.broadcasted_iota(jnp.int32, t.shape, 1)
        front = lane % HEAD_DIM < HALF
        partner = jnp.where(front, pltpu.roll(t, 128 - HALF, 1), pltpu.roll(t, HALF, 1))
        return t * self.cos[...] + partner * (self.sin[...] * sign)

    def project(self, name):
        out = getattr(self, name)
        t = dot(self.x[...], getattr(self, "w" + name)[...])
        for i in range(PAIRS):
            s = t[:, i * 128:(i + 1) * 128]
            if name != "v":
                s = self.turn(s, 1.0)
            if name == "q":
                s = s * HEAD_DIM ** -0.5
            out[:, i * 128:(i + 1) * 128] = s.astype(BF16)

    def halves(self, two):
        first = lax.broadcasted_iota(jnp.int32, two.shape, 1) < HEAD_DIM
        none = jnp.zeros_like(two)
        return jnp.where(first, two, none), jnp.where(first, none, two)

    def attend(self, first):
        loop(first + 2, self.attend_pair, first)

    def attend_pair(self, hp):
        lanes = ds(hp * 128, 128)
        q, k2, v = self.halves(self.q[:, lanes]), self.k[:, lanes], self.halves(self.v[:, lanes])
        for qb in range(2):
            keys = (qb + 1) * 256
            rows = slice(qb * 256, qb * 256 + 256)
            both = []
            for j in range(2):
                s = dot_nt(q[j][rows], k2[:keys]) + self.bias[rows, :keys]
                e = jnp.exp(s - jnp.max(s, axis=-1, keepdims=True))
                p = (e * (1.0 / jnp.sum(e, axis=-1, keepdims=True))).astype(BF16)
                (self.p1 if qb else self.p0)[2 * hp + j] = p
                both.append(p)
            o = dot(jnp.concatenate(both, axis=1), jnp.concatenate([v[0][:keys], v[1][:keys]], axis=0)).astype(BF16)
            self.attn[rows, lanes] = o
            self.attnt[lanes, rows] = o.T

    def norm_one(self):
        def step(i):
            rows = ds(i * 256, 256)
            h = self.x[rows, :].astype(F32) + dot(self.attn[rows, :], self.wo[...])
            r = lax.rsqrt(jnp.mean(h * h, axis=-1, keepdims=True) + EPS)
            n = h * r
            self.n1[rows, :] = n
            self.r1[rows, :] = r
            y = (n * self.gain1[...]).astype(BF16)
            self.y1[rows, :] = y
            self.y1t[:, rows] = y.T
        loop(2, step)

    def ffn(self, quarter):
        at = (quarter % 2) * 1024 + (quarter // 2) * 512
        cols = slice(at, at + 512)

        def step(i):
            rows = ds(i * 256, 256)
            g = dot(self.y1[rows, :], self.wg[:, cols])
            u = dot(self.y1[rows, :], self.wu[:, cols])
            s = jax.nn.sigmoid(g)
            gs = g * s
            h = (gs * u).astype(BF16)
            self.hid[rows, cols] = h
            self.hidt[cols, rows] = h.T
            self.b[rows, cols] = gs.astype(BF16)
            self.a[rows, cols] = (u * s * (1.0 + g * (1.0 - s))).astype(BF16)
        loop(2, step)

    def down(self, part):
        last = part == 3

        def step(i):
            rows = slice(i * 256, (i + 1) * 256)
            left = jnp.concatenate([self.hid[rows, s * 512 + part * 128:s * 512 + part * 128 + 128] for s in range(4)], axis=1)
            right = jnp.concatenate([self.wd[s * 512 + part * 128:s * 512 + part * 128 + 128, :] for s in range(4)], axis=0)
            t = dot(left, right)
            if part == 0:
                self.h2[rows, :] = self.n1[rows, :] * self.gain1[...] + t
                return
            h = self.h2[rows, :] + t
            if not last:
                self.h2[rows, :] = h
                return
            r = lax.rsqrt(jnp.mean(h * h, axis=-1, keepdims=True) + EPS)
            n = h * r
            c = self.c[rows, :].astype(F32)
            self.c[rows, :] = (n * self.gain2[...]).astype(BF16)
            self.gains[1:2, :] += jnp.sum(c * n, axis=0, keepdims=True)
            g = c * self.gain2[...]
            dh = r * (g - n * jnp.mean(g * n, axis=-1, keepdims=True))
            self.h2[rows, :] = dh
            self.dffn[rows, :] = dh.astype(BF16)
        if part == 0:
            self.gains[...] = jnp.zeros_like(self.gains)
        step(0)
        step(1)
        if last:
            cp = pltpu.make_async_copy(self.c, self.layer_out, self.lsem.at[5])
            cp.start()
            self.copies.append(cp)

    def dhidden(self, half):
        for i in (2 * half, 2 * half + 1):
            cols = slice(i * 512, (i + 1) * 512)
            t = dot_nt(self.dffn[...], self.wd[cols, :])
            self.a[:, cols] = (t * self.a[:, cols].astype(F32)).astype(BF16)
            self.b[:, cols] = (t * self.b[:, cols].astype(F32)).astype(BF16)

    def back_one(self):
        def step(i):
            rows = ds(i * 256, 256)
            dy = self.h2[rows, :] + dot_nt(self.a[rows, :], self.wg[...]) + dot_nt(self.b[rows, :], self.wu[...])
            n = self.n1[rows, :]
            self.gains[0:1, :] += jnp.sum(dy * n, axis=0, keepdims=True)
            g = dy * self.gain1[...]
            dh = self.r1[rows, :] * (g - n * jnp.mean(g * n, axis=-1, keepdims=True))
            self.h2[rows, :] = dh
            self.dffn[rows, :] = dh.astype(BF16)
        loop(2, step)

    def dattn(self):
        self.x[...] = dot_nt(self.dffn[...], self.wo[...]).astype(BF16)

    def attend_back(self, i):
        loop(2, lambda half: self.attend_back_pair(half * 3 + i))

    def attend_back_pair(self, hp):
        lanes = ds(hp * 128, 128)
        v2 = self.v[:, lanes]
        q, k, do = self.halves(self.q[:, lanes]), self.halves(self.k[:, lanes]), self.halves(self.x[:, lanes])
        dq, s, p = [], [], []
        for qb in range(2):
            keys = (qb + 1) * 256
            rows = slice(qb * 256, qb * 256 + 256)
            low = [(self.p1 if qb else self.p0)[2 * hp + j] for j in range(2)]
            ds_low = []
            for j in range(2):
                wide = low[j].astype(F32)
                dp = dot_nt(do[j][rows], v2[:keys])
                ds_low.append((wide * (dp - jnp.sum(wide * dp, axis=-1, keepdims=True))).astype(BF16))
            dq.append(dot(jnp.concatenate(ds_low, axis=1), jnp.concatenate([k[0][:keys], k[1][:keys]], axis=0)))
            s.append(ds_low)
            p.append(low)

        def over_queries(of, rows):
            first = dot_tn(jnp.concatenate([*of[0], of[1][0][:, :256], of[1][1][:, :256]], axis=0),
                           jnp.concatenate([rows[0][:256], rows[1][:256], rows[0][256:], rows[1][256:]], axis=0))
            second = dot_tn(jnp.concatenate([of[1][0][:, 256:], of[1][1][:, 256:]], axis=0),
                            jnp.concatenate([rows[0][256:], rows[1][256:]], axis=0))
            return jnp.concatenate([first, second], axis=0)
        dk, dv = over_queries(s, q), over_queries(p, do)
        self.q[:, lanes] = self.turn(jnp.concatenate(dq, axis=0) * HEAD_DIM ** -0.5, -1.0).astype(BF16)
        self.k[:, lanes] = self.turn(dk, -1.0).astype(BF16)
        self.v[:, lanes] = dv.astype(BF16)

    def input_grad(self):
        self.h2[...] += dot_nt(self.q[...], self.wq[...]) + dot_nt(self.k[...], self.wk[...]) + dot_nt(self.v[...], self.wv[...])
        cp = pltpu.make_async_copy(self.h2, self.dx, self.lsem.at[6])
        cp.start()
        self.copies.append(cp)

    def pick(self, n, d, gu, qa):
        j = int(n[1:] or 0)
        if n[0] == "D":
            return d.at[j]
        if n[0] in "GU":
            return gu.at[2 * j + (n[0] == "U")]
        if n[0] == "B":
            rows = qa.shape[-2] // 2
            return qa.at[(2, *[slice(None)] * (len(qa.shape) - 3), slice(j * rows, (j + 1) * rows))]
        return qa.at[3 if n[0] == "O" else j]

    def own(self, n):
        return self.pick(n, self.gd, self.ggu, self.ga)

    def out0(self, n):
        rows, cols = SHAPE[n]
        return self.send0.at[CHUNKS.index(n) % SLOTS, 0:4 * rows, 0:cols]

    def grad(self, n):
        own, other = self.own(n), self.out0(n)
        c0 = self.cc == 0

        def both(t):
            lo, hi = t[:, :384], t[:, 384:]
            own[...] = jnp.where(c0, lo, hi).astype(BF16)
            other[...] = jnp.where(c0, hi, lo).astype(BF16)
        j = int(n[1:] or 0)
        if n[0] == "D":
            both(dot(jnp.concatenate([self.hidt[s * 512 + j * 128:s * 512 + j * 128 + 128, :] for s in range(4)], axis=0), self.dffn[...]))
        elif n[0] == "O":
            both(dot(self.attnt[...], self.dffn[...]))
        elif n[0] in "GU":
            src = self.a if n[0] == "G" else self.b
            for half, dst in ((self.oc, other), (self.cc, own)):
                dst[...] = dot(self.y1t[...], src[:, ds(half * 1024 + j * 512, 512)]).astype(BF16)
        else:
            right = []
            for half in (self.oc, self.cc):
                lanes = ds((half * 3 + (2 if n[0] == "B" else j)) * 128, 128)
                right += [self.q[:, lanes], self.k[:, lanes], self.v[:, lanes]]
            left = self.xt[...]
            if n[0] == "B":
                left = jnp.concatenate([self.xt[s * 192 + j * 96:s * 192 + j * 96 + 96, :] for s in range(4)], axis=0)
            t = dot(left, jnp.concatenate(right, axis=1)).astype(BF16)
            other[...] = t[:, :384]
            own[...] = t[:, 384:]

    def remote(self, src, dst, send, recv, **where):
        cp = pltpu.make_async_remote_copy(src_ref=src, dst_ref=dst, send_sem=send, recv_sem=recv, device_id=where, device_id_type=MESH)
        return cp

    def begin(self, cp, sent):
        cp.start()
        sent.append(cp)

    def enter(self):
        barrier = pltpu.get_barrier_semaphore()
        for where in ({"col": self.oc}, {"row": self.rx}, {"row": self.ry}, {"dp": self.zn}, {"dp": self.zm}):
            pl.semaphore_signal(barrier, inc=1, device_id=where, device_id_type=MESH)
        pl.semaphore_wait(barrier, 5)

    def region(self, i, row, core):
        n, r0, nr, c0, nc = PIECES[i]
        rows, cols = SHARD[n]
        return getattr(self, "w" + n).at[ds(row * rows + r0, nr, 64), ds(core * cols + c0, nc, 128)]

    def shard(self, i):
        n, r0, nr, c0, nc = PIECES[i]
        return getattr(self, "h" + n).at[r0:r0 + nr, c0:c0 + nc]

    def gather(self, i, what):
        a, b = self.axes[i % 2]
        row = (self.r, a, a, self.r, a, self.diag, b)[what]
        where = ({"row": a}, {"row": b}, {"dp": self.zn}, *[{"col": self.oc}] * 4)[what]
        if what == 2 and i in DIRECT:
            row, where = self.r, {"row": b}
        src = self.shard(i) if what in (0, 3) or (what == 2 and i in DIRECT) else self.region(i, row, self.cc)
        return self.remote(src, self.region(i, row, self.cc), self.gsend.at[i, what], self.grecv.at[i, what], **where)

    def go(self, i, *whats):
        for what in whats:
            self.begin(self.gather(i, what), self.sent)

    def push(self, i):
        self.go(i, *((0, 2) if i in DIRECT else (0,)))

    def share(self, i):
        self.go(i, 3)
        pltpu.make_async_copy(self.shard(i), self.region(i, self.r, self.cc), self.glocal.at[i]).start()

    def relay(self, i):
        self.gather(i, 0).wait_recv()
        self.go(i, *((1, 4) if i in DIRECT else (1, 2, 4)))

    def relay_two(self, i):
        self.gather(i, 1).wait_recv()
        self.go(i, 5)
        self.gather(i, 2).wait_recv()
        self.go(i, 6)

    def ready(self, i):
        pltpu.make_async_copy(self.shard(i), self.region(i, self.r, self.cc), self.glocal.at[i]).wait()
        for what in (3, 4, 5, 6):
            self.gather(i, what).wait_recv()

    def part(self, kind, n):
        d, gu, qa = {"1": (self.d1, self.gu1, self.qa1), "2": (self.d2, self.gu2, self.qa2), "a": (self.da, self.gua, self.qaa),
                     "b": (self.db, self.gub, self.qab)}[kind]
        return self.pick(n, d, gu, qa)

    def chunk(self, n):
        k = CHUNKS.index(n)
        rows, cols = SHAPE[n]
        if n in SPREAD:
            ra, rb = self.axes[k % 2]
        else:
            ra, rb = (self.rx, self.ry) if k % 2 == 0 else (self.ry, self.rx)
        block = lambda row: ds(row * rows, rows)
        return k, rows, cols, ra, rb, block

    def copy0(self, n):
        k, rows, cols, *_ = self.chunk(n)
        at = (k % SLOTS, slice(0, 4 * rows), slice(0, cols))
        return self.remote(self.send0.at[at], self.recv0.at[at], self.s0.at[0, k], self.s0.at[1, k], col=self.oc)

    def copy1(self, n, which):
        k, rows, cols, ra, rb, block = self.chunk(n)
        if n in SPREAD:
            row, where = ((rb, {"dp": self.zn}), (self.diag, {"row": rb}))[which]
        else:
            row, where = (ra, self.diag)[which], {"row": ra}
        return self.remote(self.own(n).at[block(row), :], self.part("1", n).at[which], self.s1.at[0, k, which], self.s1.at[1, k, which], **where)

    def copy2(self, n):
        k, rows, cols, ra, rb, block = self.chunk(n)
        row = ra if n in SPREAD else rb
        return self.remote(self.own(n).at[block(row), :], self.part("2", n), self.s2.at[0, k], self.s2.at[1, k], row=row)

    def copy_z(self, n, leg):
        k, rows, cols, ra, rb, block = self.chunk(n)
        src = self.part("2", n) if leg == 2 else self.own(n).at[block(self.r), :]
        dst = self.part("b" if leg == 1 else "a", n)
        return self.remote(src, dst, self.sz.at[leg, 0, k], self.sz.at[leg, 1, k], dp=self.zm if leg == 1 else self.zn)

    def inner(self):
        return ((self.z + 1) // 2) % 2 == 1

    def outer(self):
        return ((self.z + 1) // 2) % 2 == 0

    def add(self, ref, other, to=None):
        unit = 48 if ref.shape[0] % 48 == 0 else 32
        to = ref if to is None else to

        def step(i):
            rows = ds(i * unit, unit)
            to[rows, :] = (ref[rows, :].astype(F32) + other[rows, :].astype(F32)).astype(BF16)
        loop(ref.shape[0] // unit, step)

    def make(self, n):
        k = CHUNKS.index(n)
        if k >= SLOTS:
            self.sent0[k - SLOTS].wait_send()
            self.sent = [cp for cp in self.sent if cp is not self.sent0[k - SLOTS]]
        self.grad(n)
        if k >= SLOTS:
            pl.semaphore_wait(self.credit.at[k % SLOTS], 1)
        self.begin(self.copy0(n), self.sent)
        self.sent0[k] = self.sent[-1]

    def sum0(self, n):
        k, rows, cols, ra, rb, block = self.chunk(n)
        self.copy0(n).wait_recv()
        own = self.own(n)
        got = self.recv0.at[k % SLOTS, 0:4 * rows, 0:cols]
        for row, which in ((self.diag, 1), (rb, 0), (ra, None), (self.r, None)) if n in SPREAD else ((self.diag, 1), (ra, 0), (rb, None), (self.r, None)):
            self.add(own.at[block(row), :], got.at[block(row), :])
            if which is not None:
                self.begin(self.copy1(n, which), self.sent)
        if k + SLOTS < len(CHUNKS):
            pl.semaphore_signal(self.credit.at[k % SLOTS], inc=1, device_id={"col": self.oc}, device_id_type=MESH)

    def sum1(self, n):
        k, rows, cols, ra, rb, block = self.chunk(n)
        self.copy1(n, 1).wait_recv()
        self.add(self.own(n).at[block(ra if n in SPREAD else rb), :], self.part("1", n).at[1])
        if n in SPREAD:
            self.copy1(n, 0).wait_recv()
            self.add(self.own(n).at[block(ra), :], self.part("1", n).at[0])
        self.begin(self.copy2(n), self.sent)

    def sum2(self, n):
        k, rows, cols, ra, rb, block = self.chunk(n)
        own = self.own(n).at[block(self.r), :]
        if n not in SPREAD:
            self.copy1(n, 0).wait_recv()
            self.add(own, self.part("1", n).at[0])
        self.copy2(n).wait_recv()
        self.add(own, self.part("2", n))

        @pl.when(self.outer())
        def _():
            self.copy_z(n, 0).start()

    def sum_z1(self, n):
        k, rows, cols, ra, rb, block = self.chunk(n)

        @pl.when(self.inner())
        def _():
            self.copy_z(n, 0).wait_recv()
            self.add(self.own(n).at[block(self.r), :], self.part("a", n))
            self.copy_z(n, 1).start()

    def sum_z2(self, n):
        k, rows, cols, ra, rb, block = self.chunk(n)

        @pl.when(self.inner())
        def _():
            self.copy_z(n, 1).wait_recv()
            total = self.part("2", n)
            own = self.own(n).at[block(self.r), :]
            self.add(own, self.part("b", n), total)
            self.copy_z(n, 2).start()
            for cp in self.results(n, total):
                cp.start()

    def sum_z3(self, n):
        self.ended.append(n)

        @pl.when(self.outer())
        def _():
            self.copy_z(n, 2).wait_recv()
            for cp in self.results(n, self.part("a", n)):
                cp.start()

    def results(self, n, src):
        k = CHUNKS.index(n)
        j = int(n[1:] or 0)
        if n[0] in "AB":
            rows, j = (slice(j * 96, j * 96 + 96), 2) if n[0] == "B" else (slice(0, 192), j)
            return [pltpu.make_async_copy(src.at[:, i * 128:(i + 1) * 128], getattr(self, "out_" + m).at[rows, j * 128:(j + 1) * 128], self.so.at[k, i])
                    for i, m in enumerate("qkv")]
        out = getattr(self, "out_" + n[0].lower())
        dst = {"D": lambda: out.at[j * 128:(j + 1) * 128, :], "G": lambda: out.at[:, j * 512:(j + 1) * 512],
               "U": lambda: out.at[:, j * 512:(j + 1) * 512], "O": lambda: out}[n[0]]()
        return [pltpu.make_async_copy(src, dst, self.so.at[k, 0])]

    def gains_copy(self, t):
        where = ({"col": self.oc}, {"row": self.rx}, {"row": self.ry}, {"dp": self.zn}, {"dp": self.zm})[t]
        return self.remote(self.gains, self.gains_in.at[t], self.sg.at[0, t], self.sg.at[1, t], **where)

    def gains_send(self, t):
        self.gains_copy(t).start()

    def gains_add(self, t):
        self.gains_copy(t).wait()
        self.gains[...] += self.gains_in[t]
        if t == 4:
            cp = pltpu.make_async_copy(self.gains, self.gains_out, self.lsem.at[7])
            cp.start()
            self.copies.append(cp)

    def settle(self):
        slots = [cp for cp in self.sent if any(cp is s for s in self.sent0.values())]
        for cp in self.sent:
            if not any(cp is s for s in slots):
                cp.wait_send()
        self.sent = slots

    def finish(self):
        for cp in self.sent:
            cp.wait_send()
        for inner, legs, kind in ((self.outer(), (0,), "a"), (self.inner(), (1, 2), "2")):
            @pl.when(inner)
            def _():
                for n in self.ended:
                    for leg in legs:
                        self.copy_z(n, leg).wait_send()
                    for cp in self.results(n, self.part(kind, n)):
                        cp.wait()
        for cp in self.copies:
            cp.wait()


D0, D1, D2, D3, G0, U0, G1, U1, O, A0, A1, B0, B1 = CHUNKS


def order(s):
    s.load(); s.push(0); s.push(1); s.push(2); s.share(5); s.push(3); s.push(4); s.relay(0); s.relay(1); s.share(7); s.relay(2); s.push(5); s.share(10); s.share(3)
    s.tables(); s.relay(3); s.push(6); s.share(4); s.share(11); s.relay_two(0); s.share(0); s.relay_two(1); s.share(8); s.share(1); s.relay(4); s.relay_two(2); s.share(2); s.relay_two(3)
    s.relay(5); s.ready(1); s.push(7); s.loaded(); s.transpose_x(); s.ready(2); s.push(8); s.share(12); s.push(9); s.ready(3); s.project('k'); s.relay(6); s.share(6); s.push(10)
    s.relay_two(4); s.ready(0); s.share(13); s.share(9); s.ready(4); s.project('v'); s.relay(7); s.relay_two(5); s.project('q'); s.attend(0); s.push(11); s.ready(5); s.relay(8); s.relay(9)
    s.attend(2); s.attend(4); s.push(12); s.relay(10); s.relay_two(6); s.relay_two(7); s.norm_one(); s.relay(11); s.ready(6); s.ready(7); s.ffn(0); s.relay_two(8); s.push(13); s.relay_two(9)
    s.ffn(1); s.relay(12); s.ready(8); s.ready(9); s.relay_two(10); s.ffn(2); s.relay(13); s.ready(10); s.ffn(3); s.relay_two(11); s.down(0); s.relay_two(12); s.ready(11); s.down(1)
    s.relay_two(13); s.ready(12); s.down(2); s.ready(13); s.down(3); s.make(D0); s.make(D1); s.sum0(D0); s.make(D2); s.sum0(D1); s.make(D3); s.dhidden(0); s.sum0(D2); s.dhidden(1)
    s.sum1(D0); s.make(G0); s.sum0(D3); s.sum1(D1); s.make(U0); s.sum0(G0); s.make(G1); s.sum1(D2); s.sum0(U0); s.make(U1); s.sum1(D3); s.back_one(); s.sum1(G0); s.sum0(G1)
    s.sum0(U1); s.sum2(D2); s.sum2(D0); s.gains_send(0); s.dattn(); s.attend_back(2); s.gains_add(0); s.sum_z1(D2); s.sum1(U0); s.sum2(G0); s.make(O); s.sum2(D1); s.sum_z1(D0); s.attend_back(0)
    s.make(A0); s.sum1(G1); s.sum_z1(G0); s.gains_send(1); s.sum1(U1); s.sum2(D3); s.sum_z2(D0); s.sum_z2(D2); s.sum0(O); s.sum0(A0); s.sum_z1(D1); s.sum2(U0); s.attend_back(1); s.sum_z2(G0)
    s.sum_z1(D3); s.sum2(G1); s.sum_z1(U0); s.gains_add(1); s.sum2(U1); s.sum_z2(D1); s.gains_send(2); s.make(A1); s.sum1(O); s.sum1(A0); s.make(B0); s.sum_z2(D3); s.sum_z1(G1); s.sum_z3(G0)
    s.sum0(A1); s.sum0(B0); s.sum_z2(U0); s.sum2(O); s.sum_z1(U1); s.sum_z3(D0); s.sum_z2(G1); s.sum1(A1); s.make(B1); s.gains_add(2); s.sum2(A0); s.settle(); s.sum0(B1); s.sum_z1(O)
    s.gains_send(3); s.sum_z2(U1); s.sum2(A1); s.sum_z1(A0); s.sum1(B1); s.sum1(B0); s.sum_z3(G1); s.gains_add(3); s.sum_z2(O); s.sum_z3(U0); s.sum_z1(A1); s.sum2(B1); s.gains_send(4); s.sum_z2(A0)
    s.sum2(B0); s.sum_z3(D2); s.sum_z3(U1); s.sum_z3(D1); s.sum_z1(B1); s.sum_z3(D3); s.sum_z2(A1); s.sum_z1(B0); s.sum_z2(B1); s.sum_z3(A0); s.sum_z2(B0); s.input_grad(); s.sum_z3(A1); s.sum_z3(O)
    s.gains_add(4); s.sum_z3(B1); s.sum_z3(B0)


OUTS = ("layer_out", "dx", "out_q", "out_k", "out_v", "out_o", "out_g", "out_u", "out_d", "gains_out")
INS = ("x_in", "c_in", "lens_in", "hq", "hk", "hv", "ho", "hg", "hu", "hd", "gain1_in", "gain2_in")


def step_kernel(*refs):
    names = INS + OUTS + tuple(SCRATCH) + tuple(REMOTE) + tuple(SEMS) + ("credit",)
    s = Step(dict(zip(names, refs, strict=True)), True)
    s.enter()
    order(s)
    s.finish()


def widen_kernel(*refs):
    ins, outs, low, wide, gains, sems = refs[:10], refs[10:21], refs[21:31], refs[31:38], refs[38:40], refs[40]
    wide = [*low[:2], *wide, *gains]
    loads = [pltpu.make_async_copy(ins[i], low[i], sems.at[0, i]) for i in range(10)]
    stores = [pltpu.make_async_copy(wide[i], outs[i], sems.at[1, i]) for i in range(11)]
    for i in (9, *range(9)):
        loads[i].start()
    loads[9].wait()
    for i in range(2):
        gains[i][...] = low[9][i, :]
        stores[9 + i].start()
    for i in range(9):
        loads[i].wait()
        if i > 1:
            wide[i][...] = low[i][...].astype(F32)
        stores[i].start()
    for cp in stores:
        cp.wait()


def fused_body(x, c, lens, wq, wk, wv, wo, wg, wu, wd, gain1, gain2):
    hbm = pl.BlockSpec(memory_space=pl.ANY)
    struct = jax.ShapeDtypeStruct
    shards = [SHARD[n] for n in NAMES]
    out = pl.pallas_call(
        step_kernel,
        out_shape=[struct((T, D), BF16), struct((T, D), F32), *[struct(s, BF16) for s in shards], struct((8, D), F32)],
        in_specs=[hbm] * 12,
        out_specs=[hbm] * 10,
        scratch_shapes=[*[pltpu.VMEM(*v) for v in (SCRATCH | REMOTE).values()], *[pltpu.SemaphoreType.DMA(v) for v in SEMS.values()],
                        pltpu.SemaphoreType.REGULAR((SLOTS,))],
        compiler_params=pltpu.CompilerParams(collective_id=0, has_side_effects=True, vmem_limit_bytes=63 << 20),
        name="step",
    )(x, c, lens.T, wq, wk, wv, wo, wg, wu, wd, gain1, gain2)
    return pl.pallas_call(
        widen_kernel,
        out_shape=[struct((T, D), BF16), struct((T, D), F32), *[struct(s, F32) for s in shards], struct((D,), F32), struct((D,), F32)],
        in_specs=[hbm] * 10,
        out_specs=[hbm] * 11,
        scratch_shapes=[pltpu.VMEM((T, D), BF16), pltpu.VMEM((T, D), F32), *[pltpu.VMEM(s, BF16) for s in shards], pltpu.VMEM((8, D), F32),
                        *[pltpu.VMEM(s, F32) for s in shards], pltpu.VMEM((D,), F32), pltpu.VMEM((D,), F32), pltpu.SemaphoreType.DMA((2, 11))],
        compiler_params=pltpu.CompilerParams(vmem_limit_bytes=63 << 20),
        name="widen",
    )(*out)


def pack_info(lengths_row, places_count):
    places = jnp.arange(places_count, dtype=jnp.int32)
    segment = jnp.zeros((places_count,), jnp.int32)
    start = jnp.zeros((places_count,), jnp.int32)
    end = jnp.int32(0)
    for i in range(lengths_row.shape[0]):
        end = end + lengths_row[i]
        passed = (places >= end).astype(jnp.int32)
        segment = segment + passed
        start = start + passed * lengths_row[i]
    return segment, (places - start).astype(F32)


def angles(positions):
    frequency = 10000.0 ** (-jnp.arange(HALF, dtype=F32) * (2.0 / HEAD_DIM))
    turned = positions[..., None] * frequency
    return jnp.cos(turned), jnp.sin(turned)


def rotate(values, cosine, sine):
    a, b = values[..., :HALF], values[..., HALF:]
    return jnp.concatenate([a * cosine - b * sine, b * cosine + a * sine], axis=-1)


def norm_forward(resid):
    inverse = lax.rsqrt(jnp.mean(resid * resid, axis=-1, keepdims=True) + EPS)
    return resid * inverse, inverse


def norm_backward(grad, normed, inverse):
    return inverse * (grad - normed * jnp.mean(grad * normed, axis=-1, keepdims=True))


def heads_first(matrix):
    t, w = matrix.shape
    return matrix.reshape(t, w // HEAD_DIM, HEAD_DIM).transpose(1, 0, 2)


def heads_last(stacked):
    h, t, w = stacked.shape
    return stacked.transpose(1, 0, 2).reshape(t, h * w)


def block_local(x, c, lengths, wq, wk, wv, wo, wg, wu, wd, gain1, gain2):
    t = x.shape[0]
    segment, positions = pack_info(lengths, t)
    cosine, sine = angles(positions)
    places = jnp.arange(t, dtype=jnp.int32)
    mask = (segment[:, None] == segment[None, :]) & (places[:, None] >= places[None, :])
    scale = HEAD_DIM ** (-0.5)
    q = rotate(heads_first(dot(x, wq)), cosine, sine).astype(BF16)
    k = rotate(heads_first(dot(x, wk)), cosine, sine).astype(BF16)
    v = heads_first(dot(x, wv).astype(BF16))
    bmm = lambda e, a, b: jnp.einsum(e, a, b, preferred_element_type=F32)
    s = jnp.where(mask, bmm("htd,hsd->hts", q, k) * scale, MASKED)
    e = jnp.exp(s - jnp.max(s, axis=-1, keepdims=True))
    probs = e / jnp.sum(e, axis=-1, keepdims=True)
    low = probs.astype(BF16)
    attn = heads_last(bmm("hts,hsd->htd", low, v).astype(BF16))
    n1, r1 = norm_forward(x.astype(F32) + dot(attn, wo))
    y1 = n1 * gain1
    y1_low = y1.astype(BF16)
    gate, up = dot(y1_low, wg), dot(y1_low, wu)
    sig = jax.nn.sigmoid(gate)
    hidden = (gate * sig * up).astype(BF16)
    n2, r2 = norm_forward(y1 + dot(hidden, wd))
    layer_out = (n2 * gain2).astype(BF16)
    cf = c.astype(F32)
    gain2_grad = jnp.sum(cf * n2, axis=0)
    dh2 = norm_backward(cf * gain2, n2, r2)
    dffn = dh2.astype(BF16)
    d_down = dot_tn(hidden, dffn)
    dhidden = dot_nt(dffn, wd)
    dgate = (dhidden * up * sig * (1.0 + gate * (1.0 - sig))).astype(BF16)
    dup = (dhidden * gate * sig).astype(BF16)
    d_gate, d_up = dot_tn(y1_low, dgate), dot_tn(y1_low, dup)
    dy1 = dh2 + dot_nt(dgate, wg) + dot_nt(dup, wu)
    gain1_grad = jnp.sum(dy1 * n1, axis=0)
    dh1 = norm_backward(dy1 * gain1, n1, r1)
    dbranch = dh1.astype(BF16)
    d_out = dot_tn(attn, dbranch)
    dattn = heads_first(dot_nt(dbranch, wo).astype(BF16))
    dprobs = bmm("htd,hsd->hts", dattn, v)
    dscores = (probs * (dprobs - jnp.sum(probs * dprobs, axis=-1, keepdims=True)) * scale).astype(BF16)
    dq = heads_last(rotate(bmm("hts,hsd->htd", dscores, k), cosine, -sine)).astype(BF16)
    dk = heads_last(rotate(bmm("hts,htd->hsd", dscores, q), cosine, -sine)).astype(BF16)
    dv = heads_last(bmm("hts,htd->hsd", low, dattn)).astype(BF16)
    d_q, d_k, d_v = dot_tn(x, dq), dot_tn(x, dk), dot_tn(x, dv)
    dx = dh1 + dot_nt(dq, wq) + dot_nt(dk, wk) + dot_nt(dv, wv)
    return layer_out, dx, (d_q, d_k, d_v, d_out, d_gate, d_up, d_down), gain1_grad, gain2_grad


def body(x, c, seq_lengths, wq, wk, wv, wo, wg, wu, wd, gain1, gain2):
    block = (lax.axis_index("row") * lax.axis_size("col") + lax.axis_index("col")) * lax.axis_size("dp") + lax.axis_index("dp")
    lengths = lax.dynamic_index_in_dim(seq_lengths, block, keepdims=False)
    full = [
        lax.all_gather(lax.all_gather(w, "col", axis=1, tiled=True), "row", axis=0, tiled=True)
        for w in (wq, wk, wv, wo, wg, wu, wd)
    ]
    layer_out, dx, grads, g1, g2 = block_local(x, c, lengths, *full, gain1, gain2)
    summed = []
    for g in grads:
        g = lax.psum_scatter(g.astype(BF16), "col", scatter_dimension=1, tiled=True)
        g = lax.psum_scatter(g, "row", scatter_dimension=0, tiled=True)
        summed.append(lax.psum(g, "dp").astype(F32))
    g1, g2 = lax.psum((g1, g2), ("row", "col", "dp"))
    return (layer_out, dx, *summed, g1, g2)


def solution(mesh):
    tok = P(("row", "col", "dp"), None)
    mat = P("row", "col")
    fits = tuple(mesh.shape[a] for a in ("row", "col", "dp")) == (4, 2, 4)
    return jax.shard_map(
        fused_body if fits else body, mesh=mesh, in_specs=(tok, tok, P(), *[mat] * 7, P(), P()),
        out_specs=(tok, tok, *[mat] * 7, P(), P()), check_vma=False,
    )
```

```python
import math

import jax
import jax.numpy as jnp
from jax import lax
from jax.experimental import pallas as pl
from jax.experimental.pallas import tpu as pltpu
from jax.sharding import PartitionSpec as P

MESH = pl.DeviceIdType.MESH

HEAD_DIM = 64
HALF = HEAD_DIM // 2
EPS = 1e-06
MASKED = -1e30
BF16 = jnp.bfloat16
F32 = jnp.float32

T, D, FF, HEADS = 512, 768, 2048, 12
PAIRS = HEADS // 2
NAMES = ("q", "k", "v", "o", "g", "u", "d")
SHARD = {"q": (192, 384), "k": (192, 384), "v": (192, 384), "o": (192, 384), "g": (192, 1024), "u": (192, 1024), "d": (512, 384)}
PIECES = (
    ("q", 0, 64, 0, 384), ("q", 64, 64, 0, 384), ("q", 128, 64, 0, 384), ("k", 0, 192, 0, 384), ("v", 0, 192, 0, 384), ("o", 0, 192, 0, 384),
    ("g", 0, 192, 0, 512), ("u", 0, 192, 0, 512), ("g", 0, 192, 512, 512), ("u", 0, 192, 512, 512),
    ("d", 0, 128, 0, 384), ("d", 128, 128, 0, 384), ("d", 256, 128, 0, 384), ("d", 384, 128, 0, 384),
)
DIRECT = (13,)
CHUNKS = ("D0", "D1", "D2", "D3", "G0", "U0", "G1", "U1", "O", "A0", "A1", "B0", "B1")
SHAPE = {n: {"D": (128, 384), "G": (192, 512), "U": (192, 512), "O": (192, 384), "A": (192, 384), "B": (96, 384)}[n[0]] for n in CHUNKS}
SPREAD = ("D0", "D1", "D2", "D3", "G0", "U0")
SLOTS = 2


def dot(a, b):
    return jnp.dot(a, b, preferred_element_type=F32)


def dot_nt(a, b):
    return lax.dot_general(a, b, (((1,), (1,)), ((), ())), preferred_element_type=F32)


def dot_tn(a, b):
    return lax.dot_general(a, b, (((0,), (0,)), ((), ())), preferred_element_type=F32)


def ds(start, size, multiple=None):
    if isinstance(start, int):
        return pl.ds(start, size)
    return pl.ds(pl.multiple_of(start, multiple or size), size)


def loop(n, f, start=0):
    def step(i, carry):
        f(i)
        return carry
    lax.fori_loop(start, n, step, 0)


SCRATCH = dict(
    wq=((D, D), BF16), wk=((D, D), BF16), wv=((D, D), BF16), wo=((D, D), BF16),
    wg=((D, FF), BF16), wu=((D, FF), BF16), wd=((FF, D), BF16),
    x=((T, D), BF16), xt=((D, T), BF16), c=((T, D), BF16),
    q=((T, D), BF16), k=((T, D), BF16), v=((T, D), BF16),
    p0=((HEADS, 256, 256), BF16), p1=((HEADS, 256, 512), BF16),
    attn=((T, D), BF16), attnt=((D, T), BF16),
    n1=((T, D), F32), y1=((T, D), BF16), y1t=((D, T), BF16),
    a=((T, FF), BF16), b=((T, FF), BF16), hid=((T, FF), BF16), hidt=((FF, T), BF16),
    h2=((T, D), F32), dffn=((T, D), BF16), bias=((T, T), F32),
    cos=((T, 128), F32), sin=((T, 128), F32), r1=((T, 1), F32),
    lens=((4, 32), jnp.int32), gain1_low=((D,), F32), gain2_low=((D,), F32), gain1=((1, D), F32), gain2=((1, D), F32), gains=((8, D), F32), gains_in=((5, 8, D), F32),
    gd=((4, 512, 384), BF16), ggu=((4, 768, 512), BF16), ga=((4, 768, 384), BF16),
    send0=((SLOTS, 768, 512), BF16),
)
REMOTE = dict(
    recv0=((SLOTS, 768, 512), BF16),
    d1=((4, 2, 128, 384), BF16), gu1=((4, 2, 192, 512), BF16), qa1=((4, 2, 192, 384), BF16),
    d2=((4, 128, 384), BF16), gu2=((4, 192, 512), BF16), qa2=((4, 192, 384), BF16),
    da=((4, 128, 384), BF16), gua=((4, 192, 512), BF16), qaa=((4, 192, 384), BF16),
    db=((4, 128, 384), BF16), gub=((4, 192, 512), BF16), qab=((4, 192, 384), BF16),
)
SEMS = dict(
    lsem=(8,), gsend=(len(PIECES), 7), grecv=(len(PIECES), 7), glocal=(len(PIECES),),
    s0=(2, len(CHUNKS)), s1=(2, len(CHUNKS), 2), s2=(2, len(CHUNKS)), sz=(3, 2, len(CHUNKS)), so=(len(CHUNKS), 3), sg=(2, 5),
)


class Step:
    def __init__(self, refs, comm):
        self.__dict__.update(refs)
        self.comm = comm
        self.copies, self.sent, self.sent0, self.ended = [], [], {}, []
        if comm:
            self.r, self.cc, self.z = lax.axis_index("row"), lax.axis_index("col"), lax.axis_index("dp")
        else:
            self.r = self.cc = self.z = jnp.int32(0)
        self.oc = 1 - self.cc
        r, z = self.r, self.z
        rx = r + 1 - 2 * (r % 2)
        ry = r + 2 - 4 * (r // 2)
        odd = z % 2
        self.rx, self.ry = rx, ry
        first, second = rx + odd * (ry - rx), ry + odd * (rx - ry)
        self.axes = ((first, second), (second, first))
        self.diag = 3 - r
        self.zn = z + 1 - 2 * odd
        self.zm = 3 - z

    def load(self):
        self.copies = []
        pairs = ((self.x_in, self.x), (self.c_in, self.c), (self.lens_in, self.lens), (self.gain1_in, self.gain1_low), (self.gain2_in, self.gain2_low))
        for i, (src, dst) in enumerate(pairs):
            cp = pltpu.make_async_copy(src, dst, self.lsem.at[i])
            cp.start()
            self.copies.append(cp)

    def loaded(self):
        for cp in self.copies:
            cp.wait()
        self.copies = []

    def tables(self):
        for cp in self.copies[2:]:
            cp.wait()
        self.copies = self.copies[:2]
        block = (self.r * 2 + self.cc) * 4 + self.z
        mine = lax.broadcasted_iota(jnp.int32, (1, self.lens.shape[1]), 1) == block
        lens = [jnp.sum(jnp.where(mine, self.lens[i:i + 1, :], 0), axis=1, keepdims=True) for i in range(3)]
        ends = [lens[0], lens[0] + lens[1], lens[0] + lens[1] + lens[2]]

        def angle_rows(i):
            rows = ds(i * 128, 128)
            place = lax.broadcasted_iota(jnp.int32, (128, 128), 0) + i * 128
            lane = lax.broadcasted_iota(jnp.int32, (1, 128), 1)
            frequency = jnp.exp((lane % HALF).astype(F32) * (-2.0 / HEAD_DIM * math.log(10000.0)))
            start = jnp.zeros((128, 128), jnp.int32)
            for l, e in zip(lens, ends):
                start = start + jnp.where(place >= e, l, 0)
            angle = (place - start).astype(F32) * frequency
            self.cos[rows, :] = jnp.cos(angle)
            self.sin[rows, :] = jnp.sin(angle) * jnp.where(lane % HEAD_DIM < HALF, -1.0, 1.0)
        loop(4, angle_rows)
        self.gain1[...] = self.gain1_low[...].reshape(1, D)
        self.gain2[...] = self.gain2_low[...].reshape(1, D)

        def bias_rows(i):
            rows = ds(i * 128, 128)
            place = lax.broadcasted_iota(jnp.int32, (128, T), 0) + i * 128
            key = lax.broadcasted_iota(jnp.int32, (128, T), 1)
            seg_q = jnp.zeros((128, T), jnp.int32)
            seg_k = jnp.zeros((128, T), jnp.int32)
            for e in ends:
                seg_q = seg_q + jnp.where(place >= e, 1, 0)
                seg_k = seg_k + jnp.where(key >= e, 1, 0)
            ok = (seg_q == seg_k) & (place >= key)
            self.bias[rows, :] = jnp.where(ok, 0.0, MASKED)
        loop(4, bias_rows)

    def transpose_x(self):
        def step(i):
            cols = ds(i * 128, 128)
            self.xt[cols, :] = self.x[:, cols].T
        loop(6, step)

    def turn(self, t, sign):
        lane = lax.broadcasted_iota(jnp.int32, t.shape, 1)
        front = lane % HEAD_DIM < HALF
        partner = jnp.where(front, pltpu.roll(t, 128 - HALF, 1), pltpu.roll(t, HALF, 1))
        return t * self.cos[...] + partner * (self.sin[...] * sign)

    def project(self, name):
        out = getattr(self, name)
        t = dot(self.x[...], getattr(self, "w" + name)[...])
        for i in range(PAIRS):
            s = t[:, i * 128:(i + 1) * 128]
            if name != "v":
                s = self.turn(s, 1.0)
            if name == "q":
                s = s * HEAD_DIM ** -0.5
            out[:, i * 128:(i + 1) * 128] = s.astype(BF16)

    def halves(self, two):
        first = lax.broadcasted_iota(jnp.int32, two.shape, 1) < HEAD_DIM
        none = jnp.zeros_like(two)
        return jnp.where(first, two, none), jnp.where(first, none, two)

    def attend(self, first):
        loop(first + 2, self.attend_pair, first)

    def attend_pair(self, hp):
        lanes = ds(hp * 128, 128)
        q, k2, v = self.halves(self.q[:, lanes]), self.k[:, lanes], self.halves(self.v[:, lanes])
        for qb in range(2):
            keys = (qb + 1) * 256
            rows = slice(qb * 256, qb * 256 + 256)
            both = []
            for j in range(2):
                s = dot_nt(q[j][rows], k2[:keys]) + self.bias[rows, :keys]
                e = jnp.exp(s - jnp.max(s, axis=-1, keepdims=True))
                p = (e * (1.0 / jnp.sum(e, axis=-1, keepdims=True))).astype(BF16)
                (self.p1 if qb else self.p0)[2 * hp + j] = p
                both.append(p)
            o = dot(jnp.concatenate(both, axis=1), jnp.concatenate([v[0][:keys], v[1][:keys]], axis=0)).astype(BF16)
            self.attn[rows, lanes] = o
            self.attnt[lanes, rows] = o.T

    def norm_one(self):
        def step(i):
            rows = ds(i * 256, 256)
            h = self.x[rows, :].astype(F32) + dot(self.attn[rows, :], self.wo[...])
            r = lax.rsqrt(jnp.mean(h * h, axis=-1, keepdims=True) + EPS)
            n = h * r
            self.n1[rows, :] = n
            self.r1[rows, :] = r
            y = (n * self.gain1[...]).astype(BF16)
            self.y1[rows, :] = y
            self.y1t[:, rows] = y.T
        loop(2, step)

    def ffn(self, quarter):
        at = (quarter % 2) * 1024 + (quarter // 2) * 512
        cols = slice(at, at + 512)

        def step(i):
            rows = ds(i * 256, 256)
            g = dot(self.y1[rows, :], self.wg[:, cols])
            u = dot(self.y1[rows, :], self.wu[:, cols])
            s = jax.nn.sigmoid(g)
            gs = g * s
            h = (gs * u).astype(BF16)
            self.hid[rows, cols] = h
            self.hidt[cols, rows] = h.T
            self.b[rows, cols] = gs.astype(BF16)
            self.a[rows, cols] = (u * s * (1.0 + g * (1.0 - s))).astype(BF16)
        loop(2, step)

    def down(self, part):
        last = part == 3

        def step(i):
            rows = slice(i * 256, (i + 1) * 256)
            left = jnp.concatenate([self.hid[rows, s * 512 + part * 128:s * 512 + part * 128 + 128] for s in range(4)], axis=1)
            right = jnp.concatenate([self.wd[s * 512 + part * 128:s * 512 + part * 128 + 128, :] for s in range(4)], axis=0)
            t = dot(left, right)
            if part == 0:
                self.h2[rows, :] = self.n1[rows, :] * self.gain1[...] + t
                return
            h = self.h2[rows, :] + t
            if not last:
                self.h2[rows, :] = h
                return
            r = lax.rsqrt(jnp.mean(h * h, axis=-1, keepdims=True) + EPS)
            n = h * r
            c = self.c[rows, :].astype(F32)
            self.c[rows, :] = (n * self.gain2[...]).astype(BF16)
            self.gains[1:2, :] += jnp.sum(c * n, axis=0, keepdims=True)
            g = c * self.gain2[...]
            dh = r * (g - n * jnp.mean(g * n, axis=-1, keepdims=True))
            self.h2[rows, :] = dh
            self.dffn[rows, :] = dh.astype(BF16)
        if part == 0:
            self.gains[...] = jnp.zeros_like(self.gains)
        step(0)
        step(1)
        if last:
            cp = pltpu.make_async_copy(self.c, self.layer_out, self.lsem.at[5])
            cp.start()
            self.copies.append(cp)

    def dhidden(self, half):
        for i in (2 * half, 2 * half + 1):
            cols = slice(i * 512, (i + 1) * 512)
            t = dot_nt(self.dffn[...], self.wd[cols, :])
            self.a[:, cols] = (t * self.a[:, cols].astype(F32)).astype(BF16)
            self.b[:, cols] = (t * self.b[:, cols].astype(F32)).astype(BF16)

    def back_one(self):
        def step(i):
            rows = ds(i * 256, 256)
            dy = self.h2[rows, :] + dot_nt(self.a[rows, :], self.wg[...]) + dot_nt(self.b[rows, :], self.wu[...])
            n = self.n1[rows, :]
            self.gains[0:1, :] += jnp.sum(dy * n, axis=0, keepdims=True)
            g = dy * self.gain1[...]
            dh = self.r1[rows, :] * (g - n * jnp.mean(g * n, axis=-1, keepdims=True))
            self.h2[rows, :] = dh
            self.dffn[rows, :] = dh.astype(BF16)
        loop(2, step)

    def dattn(self):
        self.x[...] = dot_nt(self.dffn[...], self.wo[...]).astype(BF16)

    def attend_back(self, i):
        loop(2, lambda half: self.attend_back_pair(half * 3 + i))

    def attend_back_pair(self, hp):
        lanes = ds(hp * 128, 128)
        v2 = self.v[:, lanes]
        q, k, do = self.halves(self.q[:, lanes]), self.halves(self.k[:, lanes]), self.halves(self.x[:, lanes])
        dq, s, p = [], [], []
        for qb in range(2):
            keys = (qb + 1) * 256
            rows = slice(qb * 256, qb * 256 + 256)
            low = [(self.p1 if qb else self.p0)[2 * hp + j] for j in range(2)]
            ds_low = []
            for j in range(2):
                wide = low[j].astype(F32)
                dp = dot_nt(do[j][rows], v2[:keys])
                ds_low.append((wide * (dp - jnp.sum(wide * dp, axis=-1, keepdims=True))).astype(BF16))
            dq.append(dot(jnp.concatenate(ds_low, axis=1), jnp.concatenate([k[0][:keys], k[1][:keys]], axis=0)))
            s.append(ds_low)
            p.append(low)

        def over_queries(of, rows):
            first = dot_tn(jnp.concatenate([*of[0], of[1][0][:, :256], of[1][1][:, :256]], axis=0),
                           jnp.concatenate([rows[0][:256], rows[1][:256], rows[0][256:], rows[1][256:]], axis=0))
            second = dot_tn(jnp.concatenate([of[1][0][:, 256:], of[1][1][:, 256:]], axis=0),
                            jnp.concatenate([rows[0][256:], rows[1][256:]], axis=0))
            return jnp.concatenate([first, second], axis=0)
        dk, dv = over_queries(s, q), over_queries(p, do)
        self.q[:, lanes] = self.turn(jnp.concatenate(dq, axis=0) * HEAD_DIM ** -0.5, -1.0).astype(BF16)
        self.k[:, lanes] = self.turn(dk, -1.0).astype(BF16)
        self.v[:, lanes] = dv.astype(BF16)

    def input_grad(self):
        self.h2[...] += dot_nt(self.q[...], self.wq[...]) + dot_nt(self.k[...], self.wk[...]) + dot_nt(self.v[...], self.wv[...])
        cp = pltpu.make_async_copy(self.h2, self.dx, self.lsem.at[6])
        cp.start()
        self.copies.append(cp)

    def pick(self, n, d, gu, qa):
        j = int(n[1:] or 0)
        if n[0] == "D":
            return d.at[j]
        if n[0] in "GU":
            return gu.at[2 * j + (n[0] == "U")]
        if n[0] == "B":
            rows = qa.shape[-2] // 2
            return qa.at[(2, *[slice(None)] * (len(qa.shape) - 3), slice(j * rows, (j + 1) * rows))]
        return qa.at[3 if n[0] == "O" else j]

    def own(self, n):
        return self.pick(n, self.gd, self.ggu, self.ga)

    def out0(self, n):
        rows, cols = SHAPE[n]
        return self.send0.at[CHUNKS.index(n) % SLOTS, 0:4 * rows, 0:cols]

    def grad(self, n):
        own, other = self.own(n), self.out0(n)
        c0 = self.cc == 0

        def both(t):
            lo, hi = t[:, :384], t[:, 384:]
            own[...] = jnp.where(c0, lo, hi).astype(BF16)
            other[...] = jnp.where(c0, hi, lo).astype(BF16)
        j = int(n[1:] or 0)
        if n[0] == "D":
            both(dot(jnp.concatenate([self.hidt[s * 512 + j * 128:s * 512 + j * 128 + 128, :] for s in range(4)], axis=0), self.dffn[...]))
        elif n[0] == "O":
            both(dot(self.attnt[...], self.dffn[...]))
        elif n[0] in "GU":
            src = self.a if n[0] == "G" else self.b
            for half, dst in ((self.oc, other), (self.cc, own)):
                dst[...] = dot(self.y1t[...], src[:, ds(half * 1024 + j * 512, 512)]).astype(BF16)
        else:
            right = []
            for half in (self.oc, self.cc):
                lanes = ds((half * 3 + (2 if n[0] == "B" else j)) * 128, 128)
                right += [self.q[:, lanes], self.k[:, lanes], self.v[:, lanes]]
            left = self.xt[...]
            if n[0] == "B":
                left = jnp.concatenate([self.xt[s * 192 + j * 96:s * 192 + j * 96 + 96, :] for s in range(4)], axis=0)
            t = dot(left, jnp.concatenate(right, axis=1)).astype(BF16)
            other[...] = t[:, :384]
            own[...] = t[:, 384:]

    def remote(self, src, dst, send, recv, **where):
        cp = pltpu.make_async_remote_copy(src_ref=src, dst_ref=dst, send_sem=send, recv_sem=recv, device_id=where, device_id_type=MESH)
        return cp

    def begin(self, cp, sent):
        cp.start()
        sent.append(cp)

    def enter(self):
        barrier = pltpu.get_barrier_semaphore()
        for where in ({"col": self.oc}, {"row": self.rx}, {"row": self.ry}, {"dp": self.zn}, {"dp": self.zm}):
            pl.semaphore_signal(barrier, inc=1, device_id=where, device_id_type=MESH)
        pl.semaphore_wait(barrier, 5)

    def region(self, i, row, core):
        n, r0, nr, c0, nc = PIECES[i]
        rows, cols = SHARD[n]
        return getattr(self, "w" + n).at[ds(row * rows + r0, nr, 64), ds(core * cols + c0, nc, 128)]

    def shard(self, i):
        n, r0, nr, c0, nc = PIECES[i]
        return getattr(self, "h" + n).at[r0:r0 + nr, c0:c0 + nc]

    def gather(self, i, what):
        a, b = self.axes[i % 2]
        row = (self.r, a, a, self.r, a, self.diag, b)[what]
        where = ({"row": a}, {"row": b}, {"dp": self.zn}, *[{"col": self.oc}] * 4)[what]
        if what == 2 and i in DIRECT:
            row, where = self.r, {"row": b}
        src = self.shard(i) if what in (0, 3) or (what == 2 and i in DIRECT) else self.region(i, row, self.cc)
        return self.remote(src, self.region(i, row, self.cc), self.gsend.at[i, what], self.grecv.at[i, what], **where)

    def go(self, i, *whats):
        for what in whats:
            self.begin(self.gather(i, what), self.sent)

    def push(self, i):
        self.go(i, *((0, 2) if i in DIRECT else (0,)))

    def share(self, i):
        self.go(i, 3)
        pltpu.make_async_copy(self.shard(i), self.region(i, self.r, self.cc), self.glocal.at[i]).start()

    def relay(self, i):
        self.gather(i, 0).wait_recv()
        self.go(i, *((1, 4) if i in DIRECT else (1, 2, 4)))

    def relay_two(self, i):
        self.gather(i, 1).wait_recv()
        self.go(i, 5)
        self.gather(i, 2).wait_recv()
        self.go(i, 6)

    def ready(self, i):
        pltpu.make_async_copy(self.shard(i), self.region(i, self.r, self.cc), self.glocal.at[i]).wait()
        for what in (3, 4, 5, 6):
            self.gather(i, what).wait_recv()

    def part(self, kind, n):
        d, gu, qa = {"1": (self.d1, self.gu1, self.qa1), "2": (self.d2, self.gu2, self.qa2), "a": (self.da, self.gua, self.qaa),
                     "b": (self.db, self.gub, self.qab)}[kind]
        return self.pick(n, d, gu, qa)

    def chunk(self, n):
        k = CHUNKS.index(n)
        rows, cols = SHAPE[n]
        if n in SPREAD:
            ra, rb = self.axes[k % 2]
        else:
            ra, rb = (self.rx, self.ry) if k % 2 == 0 else (self.ry, self.rx)
        block = lambda row: ds(row * rows, rows)
        return k, rows, cols, ra, rb, block

    def copy0(self, n):
        k, rows, cols, *_ = self.chunk(n)
        at = (k % SLOTS, slice(0, 4 * rows), slice(0, cols))
        return self.remote(self.send0.at[at], self.recv0.at[at], self.s0.at[0, k], self.s0.at[1, k], col=self.oc)

    def copy1(self, n, which):
        k, rows, cols, ra, rb, block = self.chunk(n)
        if n in SPREAD:
            row, where = ((rb, {"dp": self.zn}), (self.diag, {"row": rb}))[which]
        else:
            row, where = (ra, self.diag)[which], {"row": ra}
        return self.remote(self.own(n).at[block(row), :], self.part("1", n).at[which], self.s1.at[0, k, which], self.s1.at[1, k, which], **where)

    def copy2(self, n):
        k, rows, cols, ra, rb, block = self.chunk(n)
        row = ra if n in SPREAD else rb
        return self.remote(self.own(n).at[block(row), :], self.part("2", n), self.s2.at[0, k], self.s2.at[1, k], row=row)

    def copy_z(self, n, leg):
        k, rows, cols, ra, rb, block = self.chunk(n)
        src = self.part("2", n) if leg == 2 else self.own(n).at[block(self.r), :]
        dst = self.part("b" if leg == 1 else "a", n)
        return self.remote(src, dst, self.sz.at[leg, 0, k], self.sz.at[leg, 1, k], dp=self.zm if leg == 1 else self.zn)

    def inner(self):
        return ((self.z + 1) // 2) % 2 == 1

    def outer(self):
        return ((self.z + 1) // 2) % 2 == 0

    def add(self, ref, other, to=None):
        unit = 48 if ref.shape[0] % 48 == 0 else 32
        to = ref if to is None else to

        def step(i):
            rows = ds(i * unit, unit)
            to[rows, :] = (ref[rows, :].astype(F32) + other[rows, :].astype(F32)).astype(BF16)
        loop(ref.shape[0] // unit, step)

    def make(self, n):
        k = CHUNKS.index(n)
        if k >= SLOTS:
            self.sent0[k - SLOTS].wait_send()
            self.sent = [cp for cp in self.sent if cp is not self.sent0[k - SLOTS]]
        self.grad(n)
        if k >= SLOTS:
            pl.semaphore_wait(self.credit.at[k % SLOTS], 1)
        self.begin(self.copy0(n), self.sent)
        self.sent0[k] = self.sent[-1]

    def sum0(self, n):
        k, rows, cols, ra, rb, block = self.chunk(n)
        self.copy0(n).wait_recv()
        own = self.own(n)
        got = self.recv0.at[k % SLOTS, 0:4 * rows, 0:cols]
        for row, which in ((self.diag, 1), (rb, 0), (ra, None), (self.r, None)) if n in SPREAD else ((self.diag, 1), (ra, 0), (rb, None), (self.r, None)):
            self.add(own.at[block(row), :], got.at[block(row), :])
            if which is not None:
                self.begin(self.copy1(n, which), self.sent)
        if k + SLOTS < len(CHUNKS):
            pl.semaphore_signal(self.credit.at[k % SLOTS], inc=1, device_id={"col": self.oc}, device_id_type=MESH)

    def sum1(self, n):
        k, rows, cols, ra, rb, block = self.chunk(n)
        self.copy1(n, 1).wait_recv()
        self.add(self.own(n).at[block(ra if n in SPREAD else rb), :], self.part("1", n).at[1])
        if n in SPREAD:
            self.copy1(n, 0).wait_recv()
            self.add(self.own(n).at[block(ra), :], self.part("1", n).at[0])
        self.begin(self.copy2(n), self.sent)

    def sum2(self, n):
        k, rows, cols, ra, rb, block = self.chunk(n)
        own = self.own(n).at[block(self.r), :]
        if n not in SPREAD:
            self.copy1(n, 0).wait_recv()
            self.add(own, self.part("1", n).at[0])
        self.copy2(n).wait_recv()
        self.add(own, self.part("2", n))

        @pl.when(self.outer())
        def _():
            self.copy_z(n, 0).start()

    def sum_z1(self, n):
        k, rows, cols, ra, rb, block = self.chunk(n)

        @pl.when(self.inner())
        def _():
            self.copy_z(n, 0).wait_recv()
            self.add(self.own(n).at[block(self.r), :], self.part("a", n))
            self.copy_z(n, 1).start()

    def sum_z2(self, n):
        k, rows, cols, ra, rb, block = self.chunk(n)

        @pl.when(self.inner())
        def _():
            self.copy_z(n, 1).wait_recv()
            total = self.part("2", n)
            own = self.own(n).at[block(self.r), :]
            self.add(own, self.part("b", n), total)
            self.copy_z(n, 2).start()
            for cp in self.results(n, total):
                cp.start()

    def sum_z3(self, n):
        self.ended.append(n)

        @pl.when(self.outer())
        def _():
            self.copy_z(n, 2).wait_recv()
            for cp in self.results(n, self.part("a", n)):
                cp.start()

    def results(self, n, src):
        k = CHUNKS.index(n)
        j = int(n[1:] or 0)
        if n[0] in "AB":
            rows, j = (slice(j * 96, j * 96 + 96), 2) if n[0] == "B" else (slice(0, 192), j)
            return [pltpu.make_async_copy(src.at[:, i * 128:(i + 1) * 128], getattr(self, "out_" + m).at[rows, j * 128:(j + 1) * 128], self.so.at[k, i])
                    for i, m in enumerate("qkv")]
        out = getattr(self, "out_" + n[0].lower())
        dst = {"D": lambda: out.at[j * 128:(j + 1) * 128, :], "G": lambda: out.at[:, j * 512:(j + 1) * 512],
               "U": lambda: out.at[:, j * 512:(j + 1) * 512], "O": lambda: out}[n[0]]()
        return [pltpu.make_async_copy(src, dst, self.so.at[k, 0])]

    def gains_copy(self, t):
        where = ({"col": self.oc}, {"row": self.rx}, {"row": self.ry}, {"dp": self.zn}, {"dp": self.zm})[t]
        return self.remote(self.gains, self.gains_in.at[t], self.sg.at[0, t], self.sg.at[1, t], **where)

    def gains_send(self, t):
        self.gains_copy(t).start()

    def gains_add(self, t):
        self.gains_copy(t).wait()
        self.gains[...] += self.gains_in[t]
        if t == 4:
            cp = pltpu.make_async_copy(self.gains, self.gains_out, self.lsem.at[7])
            cp.start()
            self.copies.append(cp)

    def settle(self):
        slots = [cp for cp in self.sent if any(cp is s for s in self.sent0.values())]
        for cp in self.sent:
            if not any(cp is s for s in slots):
                cp.wait_send()
        self.sent = slots

    def finish(self):
        for cp in self.sent:
            cp.wait_send()
        for inner, legs, kind in ((self.outer(), (0,), "a"), (self.inner(), (1, 2), "2")):
            @pl.when(inner)
            def _():
                for n in self.ended:
                    for leg in legs:
                        self.copy_z(n, leg).wait_send()
                    for cp in self.results(n, self.part(kind, n)):
                        cp.wait()
        for cp in self.copies:
            cp.wait()


D0, D1, D2, D3, G0, U0, G1, U1, O, A0, A1, B0, B1 = CHUNKS


def order(s):
    s.push(0); s.push(1); s.push(2); s.share(5); s.push(3); s.push(4); s.relay(0); s.relay(1); s.share(7); s.relay(2); s.push(5); s.share(10); s.share(3)
    s.tables(); s.relay(3); s.push(6); s.share(4); s.share(11); s.relay_two(0); s.share(0); s.relay_two(1); s.share(8); s.share(1); s.relay(4); s.relay_two(2); s.share(2); s.relay_two(3)
    s.relay(5); s.ready(1); s.push(7); s.loaded(); s.transpose_x(); s.ready(2); s.push(8); s.share(12); s.push(9); s.ready(3); s.project('k'); s.relay(6); s.share(6); s.push(10)
    s.relay_two(4); s.ready(0); s.share(13); s.share(9); s.ready(4); s.project('v'); s.relay(7); s.relay_two(5); s.project('q'); s.attend(0); s.push(11); s.ready(5); s.relay(8); s.relay(9)
    s.attend(2); s.attend(4); s.push(12); s.relay(10); s.relay_two(6); s.relay_two(7); s.norm_one(); s.relay(11); s.ready(6); s.ready(7); s.ffn(0); s.relay_two(8); s.push(13); s.relay_two(9)
    s.ffn(1); s.relay(12); s.ready(8); s.ready(9); s.relay_two(10); s.ffn(2); s.relay(13); s.ready(10); s.ffn(3); s.relay_two(11); s.down(0); s.relay_two(12); s.ready(11); s.down(1)
    s.relay_two(13); s.ready(12); s.down(2); s.ready(13); s.down(3); s.make(D0); s.make(D1); s.sum0(D0); s.make(D2); s.sum0(D1); s.make(D3); s.dhidden(0); s.sum0(D2); s.dhidden(1)
    s.sum1(D0); s.make(G0); s.sum0(D3); s.sum1(D1); s.make(U0); s.sum0(G0); s.make(G1); s.sum1(D2); s.sum0(U0); s.make(U1); s.sum1(D3); s.back_one(); s.sum1(G0); s.sum0(G1)
    s.sum0(U1); s.sum2(D2); s.sum2(D0); s.gains_send(0); s.dattn(); s.attend_back(2); s.gains_add(0); s.sum_z1(D2); s.sum1(U0); s.sum2(G0); s.make(O); s.sum2(D1); s.sum_z1(D0); s.attend_back(0)
    s.make(A0); s.sum1(G1); s.sum_z1(G0); s.gains_send(1); s.sum1(U1); s.sum2(D3); s.sum_z2(D0); s.sum_z2(D2); s.sum0(O); s.sum0(A0); s.sum_z1(D1); s.sum2(U0); s.attend_back(1); s.sum_z2(G0)
    s.sum_z1(D3); s.sum2(G1); s.sum_z1(U0); s.gains_add(1); s.sum2(U1); s.sum_z2(D1); s.gains_send(2); s.make(A1); s.sum1(O); s.sum1(A0); s.make(B0); s.sum_z2(D3); s.sum_z1(G1); s.sum_z3(G0)
    s.sum0(A1); s.sum0(B0); s.sum_z2(U0); s.sum2(O); s.sum_z1(U1); s.sum_z3(D0); s.sum_z2(G1); s.sum1(A1); s.make(B1); s.gains_add(2); s.sum2(A0); s.settle(); s.sum0(B1); s.sum_z1(O)
    s.gains_send(3); s.sum_z2(U1); s.sum2(A1); s.sum_z1(A0); s.sum1(B1); s.sum1(B0); s.sum_z3(G1); s.gains_add(3); s.sum_z2(O); s.sum_z3(U0); s.sum_z1(A1); s.sum2(B1); s.gains_send(4); s.sum_z2(A0)
    s.sum2(B0); s.sum_z3(D2); s.sum_z3(U1); s.sum_z3(D1); s.sum_z1(B1); s.sum_z3(D3); s.sum_z2(A1); s.sum_z1(B0); s.sum_z2(B1); s.sum_z3(A0); s.sum_z2(B0); s.input_grad(); s.sum_z3(A1); s.sum_z3(O)
    s.gains_add(4); s.sum_z3(B1); s.sum_z3(B0)


OUTS = ("layer_out", "dx", "out_q", "out_k", "out_v", "out_o", "out_g", "out_u", "out_d", "gains_out")
INS = ("x_in", "c_in", "lens_in", "hq", "hk", "hv", "ho", "hg", "hu", "hd", "gain1_in", "gain2_in")


def step_kernel(*refs):
    names = INS + OUTS + tuple(SCRATCH) + tuple(REMOTE) + tuple(SEMS) + ("credit",)
    s = Step(dict(zip(names, refs, strict=True)), True)
    s.load()
    s.enter()
    order(s)
    s.finish()


def widen_kernel(*refs):
    ins, outs, low, wide, gains, sems = refs[:10], refs[10:21], refs[21:31], refs[31:38], refs[38:40], refs[40]
    wide = [*low[:2], *wide]
    halves = [(i, slice(h * (low[i].shape[0] // 2), (h + 1) * (low[i].shape[0] // 2))) for i in range(9) for h in range(2)]
    loads = [pltpu.make_async_copy(ins[i].at[rows], low[i].at[rows], sems.at[0, k]) for k, (i, rows) in enumerate(halves)]
    stores = [pltpu.make_async_copy(wide[i].at[rows], outs[i].at[rows], sems.at[1, k]) for k, (i, rows) in enumerate(halves)]
    first = pltpu.make_async_copy(ins[9], low[9], sems.at[0, 18])
    ends = [pltpu.make_async_copy(gains[i], outs[9 + i], sems.at[1, 18 + i]) for i in range(2)]
    first.start()
    for cp in loads:
        cp.start()
    first.wait()
    for i in range(2):
        gains[i][...] = low[9][i, :]
        ends[i].start()
    for k, (i, rows) in enumerate(halves):
        loads[k].wait()
        if i > 1:
            wide[i][rows, :] = low[i][rows, :].astype(F32)
        stores[k].start()
    for cp in stores + ends:
        cp.wait()


def fused_body(x, c, lens, wq, wk, wv, wo, wg, wu, wd, gain1, gain2):
    hbm = pl.BlockSpec(memory_space=pl.ANY)
    struct = jax.ShapeDtypeStruct
    shards = [SHARD[n] for n in NAMES]
    out = pl.pallas_call(
        step_kernel,
        out_shape=[struct((T, D), BF16), struct((T, D), F32), *[struct(s, BF16) for s in shards], struct((8, D), F32)],
        in_specs=[hbm] * 12,
        out_specs=[hbm] * 10,
        scratch_shapes=[*[pltpu.VMEM(*v) for v in (SCRATCH | REMOTE).values()], *[pltpu.SemaphoreType.DMA(v) for v in SEMS.values()],
                        pltpu.SemaphoreType.REGULAR((SLOTS,))],
        compiler_params=pltpu.CompilerParams(collective_id=0, has_side_effects=True, vmem_limit_bytes=63 << 20),
        name="step",
    )(x, c, lens.T, wq, wk, wv, wo, wg, wu, wd, gain1, gain2)
    return pl.pallas_call(
        widen_kernel,
        out_shape=[struct((T, D), BF16), struct((T, D), F32), *[struct(s, F32) for s in shards], struct((D,), F32), struct((D,), F32)],
        in_specs=[hbm] * 10,
        out_specs=[hbm] * 11,
        scratch_shapes=[pltpu.VMEM((T, D), BF16), pltpu.VMEM((T, D), F32), *[pltpu.VMEM(s, BF16) for s in shards], pltpu.VMEM((8, D), F32),
                        *[pltpu.VMEM(s, F32) for s in shards], pltpu.VMEM((D,), F32), pltpu.VMEM((D,), F32), pltpu.SemaphoreType.DMA((2, 20))],
        compiler_params=pltpu.CompilerParams(vmem_limit_bytes=63 << 20),
        name="widen",
    )(*out)


def pack_info(lengths_row, places_count):
    places = jnp.arange(places_count, dtype=jnp.int32)
    segment = jnp.zeros((places_count,), jnp.int32)
    start = jnp.zeros((places_count,), jnp.int32)
    end = jnp.int32(0)
    for i in range(lengths_row.shape[0]):
        end = end + lengths_row[i]
        passed = (places >= end).astype(jnp.int32)
        segment = segment + passed
        start = start + passed * lengths_row[i]
    return segment, (places - start).astype(F32)


def angles(positions):
    frequency = 10000.0 ** (-jnp.arange(HALF, dtype=F32) * (2.0 / HEAD_DIM))
    turned = positions[..., None] * frequency
    return jnp.cos(turned), jnp.sin(turned)


def rotate(values, cosine, sine):
    a, b = values[..., :HALF], values[..., HALF:]
    return jnp.concatenate([a * cosine - b * sine, b * cosine + a * sine], axis=-1)


def norm_forward(resid):
    inverse = lax.rsqrt(jnp.mean(resid * resid, axis=-1, keepdims=True) + EPS)
    return resid * inverse, inverse


def norm_backward(grad, normed, inverse):
    return inverse * (grad - normed * jnp.mean(grad * normed, axis=-1, keepdims=True))


def heads_first(matrix):
    t, w = matrix.shape
    return matrix.reshape(t, w // HEAD_DIM, HEAD_DIM).transpose(1, 0, 2)


def heads_last(stacked):
    h, t, w = stacked.shape
    return stacked.transpose(1, 0, 2).reshape(t, h * w)


def block_local(x, c, lengths, wq, wk, wv, wo, wg, wu, wd, gain1, gain2):
    t = x.shape[0]
    segment, positions = pack_info(lengths, t)
    cosine, sine = angles(positions)
    places = jnp.arange(t, dtype=jnp.int32)
    mask = (segment[:, None] == segment[None, :]) & (places[:, None] >= places[None, :])
    scale = HEAD_DIM ** (-0.5)
    q = rotate(heads_first(dot(x, wq)), cosine, sine).astype(BF16)
    k = rotate(heads_first(dot(x, wk)), cosine, sine).astype(BF16)
    v = heads_first(dot(x, wv).astype(BF16))
    bmm = lambda e, a, b: jnp.einsum(e, a, b, preferred_element_type=F32)
    s = jnp.where(mask, bmm("htd,hsd->hts", q, k) * scale, MASKED)
    e = jnp.exp(s - jnp.max(s, axis=-1, keepdims=True))
    probs = e / jnp.sum(e, axis=-1, keepdims=True)
    low = probs.astype(BF16)
    attn = heads_last(bmm("hts,hsd->htd", low, v).astype(BF16))
    n1, r1 = norm_forward(x.astype(F32) + dot(attn, wo))
    y1 = n1 * gain1
    y1_low = y1.astype(BF16)
    gate, up = dot(y1_low, wg), dot(y1_low, wu)
    sig = jax.nn.sigmoid(gate)
    hidden = (gate * sig * up).astype(BF16)
    n2, r2 = norm_forward(y1 + dot(hidden, wd))
    layer_out = (n2 * gain2).astype(BF16)
    cf = c.astype(F32)
    gain2_grad = jnp.sum(cf * n2, axis=0)
    dh2 = norm_backward(cf * gain2, n2, r2)
    dffn = dh2.astype(BF16)
    d_down = dot_tn(hidden, dffn)
    dhidden = dot_nt(dffn, wd)
    dgate = (dhidden * up * sig * (1.0 + gate * (1.0 - sig))).astype(BF16)
    dup = (dhidden * gate * sig).astype(BF16)
    d_gate, d_up = dot_tn(y1_low, dgate), dot_tn(y1_low, dup)
    dy1 = dh2 + dot_nt(dgate, wg) + dot_nt(dup, wu)
    gain1_grad = jnp.sum(dy1 * n1, axis=0)
    dh1 = norm_backward(dy1 * gain1, n1, r1)
    dbranch = dh1.astype(BF16)
    d_out = dot_tn(attn, dbranch)
    dattn = heads_first(dot_nt(dbranch, wo).astype(BF16))
    dprobs = bmm("htd,hsd->hts", dattn, v)
    dscores = (probs * (dprobs - jnp.sum(probs * dprobs, axis=-1, keepdims=True)) * scale).astype(BF16)
    dq = heads_last(rotate(bmm("hts,hsd->htd", dscores, k), cosine, -sine)).astype(BF16)
    dk = heads_last(rotate(bmm("hts,htd->hsd", dscores, q), cosine, -sine)).astype(BF16)
    dv = heads_last(bmm("hts,htd->hsd", low, dattn)).astype(BF16)
    d_q, d_k, d_v = dot_tn(x, dq), dot_tn(x, dk), dot_tn(x, dv)
    dx = dh1 + dot_nt(dq, wq) + dot_nt(dk, wk) + dot_nt(dv, wv)
    return layer_out, dx, (d_q, d_k, d_v, d_out, d_gate, d_up, d_down), gain1_grad, gain2_grad


def body(x, c, seq_lengths, wq, wk, wv, wo, wg, wu, wd, gain1, gain2):
    block = (lax.axis_index("row") * lax.axis_size("col") + lax.axis_index("col")) * lax.axis_size("dp") + lax.axis_index("dp")
    lengths = lax.dynamic_index_in_dim(seq_lengths, block, keepdims=False)
    full = [
        lax.all_gather(lax.all_gather(w, "col", axis=1, tiled=True), "row", axis=0, tiled=True)
        for w in (wq, wk, wv, wo, wg, wu, wd)
    ]
    layer_out, dx, grads, g1, g2 = block_local(x, c, lengths, *full, gain1, gain2)
    summed = []
    for g in grads:
        g = lax.psum_scatter(g.astype(BF16), "col", scatter_dimension=1, tiled=True)
        g = lax.psum_scatter(g, "row", scatter_dimension=0, tiled=True)
        summed.append(lax.psum(g, "dp").astype(F32))
    g1, g2 = lax.psum((g1, g2), ("row", "col", "dp"))
    return (layer_out, dx, *summed, g1, g2)


def solution(mesh):
    tok = P(("row", "col", "dp"), None)
    mat = P("row", "col")
    fits = tuple(mesh.shape[a] for a in ("row", "col", "dp")) == (4, 2, 4)
    return jax.shard_map(
        fused_body if fits else body, mesh=mesh, in_specs=(tok, tok, P(), *[mat] * 7, P(), P()),
        out_specs=(tok, tok, *[mat] * 7, P(), P()), check_vma=False,
    )
```
